32 devices in a mesh: gx: 16 (over z, x, core), gy: 2 (over y).
Axes of the slice: x: 2, y: 2, z: 4, core: 2. Of those that a mesh axis runs over, the one named last changes fastest.
Arguments:
- right_side: float32 [2, 512, 64, 256], P(None, 'gx', 'gy'), may hold values from -8 to 8
- diagonal: float32 [512, 64, 256], P('gx', 'gy'), may hold values from 0.005 to 0.3
- aggregates: int32 [16], replicated, may hold values from 0 to 3, never falling along the last dimension, each value on 1 to 8 neighbouring positions
Outputs:
- solution: float32 [2, 512, 64, 256], P(None, 'gx', 'gy')
The draws below stay inside these ranges and needn't reach their ends.
Inputs may be any that keep to these rules, and one draw needn't show every extreme that they name: aggregates never falls from one index of gx to the next; each aggregate holds between 1 and 8 consecutive indices, and one holds exactly 8.
All inputs are finite; a program needn't handle non-finite values.
Results may differ from the reference program's by a relative error of at most 0.000071.
Values sent between devices are 32-bit elements; how exact they have to be, the bound alone decides.
No kernel may reach another device: no remote copies, remote signals or barrier semaphores. Data moves between devices by JAX's collectives and lax.ppermute only.
A program may use at most 128 MiB of HBM per device.

```python
import math
import jax
import jax.numpy as jnp
import numpy as np

CX = 32
DEGREE = 3
COARSE_DEG = 6
NX = 512
NY = 64
NZ = 256
N_GX = 16


def levels(rng, shape, pieces, smallest, largest):
    def one(axis_at, blocks):
        draws = jax.random.uniform(jax.random.fold_in(jax.random.fold_in(rng, 6), axis_at), (blocks,), jnp.float32, smallest / len(pieces), largest / len(pieces))
        return jnp.repeat(jnp.exp(draws), shape[axis_at] // blocks).reshape((-1,) + (1,) * (len(shape) - axis_at - 1))

    loudness = one(*pieces[0])
    for cut in pieces[1:]:
        loudness = loudness * one(*cut)
    return loudness


def length_profile(amount, total, most, lean):
    portions = [(1 << 20) // math.isqrt(standing ** lean) + 1 for standing in range(2, amount + 1)]
    spare, given = total - most - (amount - 1), [1] * (amount - 1)
    while spare > 0:
        candidates = [i for i in range(amount - 1) if given[i] < most]
        whole, budget = sum([portions[i] for i in candidates]), spare
        for i in candidates:
            addition = min(most - given[i], max(1, budget * portions[i] // whole), spare)
            given[i] = given[i] + addition
            spare = spare - addition
    return np.array([most] + given)


def ragged(stream_key, number_of, total, most, lean):
    if number_of == 2:
        one = jax.random.randint(stream_key, (), max(1, total - most), min(most, total - 1) + 1)
        return jnp.stack([one, total - one])
    tallies = jnp.asarray(length_profile(number_of, total, most, lean), jnp.int32)
    twos = (number_of - 1) // 2
    donor, receiver = tallies[1:1 + 2 * twos:2], tallies[2:2 + 2 * twos:2]
    room = jnp.minimum(donor - 1, most - receiver)
    passed = jax.random.randint(jax.random.fold_in(stream_key, 1), (twos,), 0, 1 << 20) % (room + 1)
    tallies = tallies.at[1:1 + 2 * twos:2].set(donor - passed).at[2:2 + 2 * twos:2].set(receiver + passed)
    return tallies[jax.random.permutation(jax.random.fold_in(stream_key, 2), number_of)]


def bell_draw(key, dims, scale, bound, cuts=(), kind=jnp.bfloat16):
    entries = scale * jax.random.normal(key, dims, jnp.float32)
    if cuts:
        entries = entries * levels(key, dims, cuts, -0.22, 0.18)
    return jnp.clip(entries, -bound, bound).astype(kind)


def setup_inputs(seed: int = 0) -> dict:
    keys = jax.random.split(jax.random.key(seed), 4)
    right_side = bell_draw(keys[0], (2, NX, NY, NZ), 1.0, 8.0, ((1, 16), (2, 2)), jnp.float32)
    diagonal = jnp.clip(jnp.exp(math.log(0.3) - 4.0943446 * jax.random.uniform(keys[1], (NX, NY, NZ), jnp.float32) ** levels(keys[1], (NX, NY, NZ), ((0, 16), (1, 2)), -0.2, 0.2)), 0.005, 0.3)
    aggregates = jnp.searchsorted(jnp.cumsum(ragged(keys[2], N_GX // 4, N_GX, N_GX // 2, 2)), jnp.arange(N_GX), side="right").astype(jnp.int32)
    return {"right_side": right_side, "diagonal": diagonal, "aggregates": aggregates}


FINE_LOWER = 3.0
FINE_UPPER = 12.4
COARSE_LOWER = 0.5
COARSE_UPPER = 13.4


def cheb_pairs(lower, upper, count):
    middle = (upper + lower) / 2.0
    halfwidth = (upper - lower) / 2.0
    ratio_mid = middle / halfwidth
    rho_old = 1.0 / ratio_mid
    result = [(0.0, 1.0 / middle)]
    for repeat in range(count - 1):
        rho_new = 1.0 / (2.0 * ratio_mid - rho_old)
        result.append((rho_new * rho_old, 2.0 * rho_new / halfwidth))
        rho_old = rho_new
    return result


def fine_apply(field, diagonal):
    padded = jnp.pad(field, ((0, 0), (1, 1), (1, 1), (1, 1)))
    nearby = padded[:, 2:, 1:-1, 1:-1] + padded[:, :-2, 1:-1, 1:-1]
    nearby = nearby + padded[:, 1:-1, 2:, 1:-1] + padded[:, 1:-1, :-2, 1:-1]
    nearby = nearby + padded[:, 1:-1, 1:-1, 2:] + padded[:, 1:-1, 1:-1, :-2]
    return (6.0 + diagonal) * field - nearby


def coarse_apply(field, coarse_diag, links):
    weights = links[None, :, None, None]
    zero_plane = jnp.zeros_like(field[:, :1])
    along_first = jnp.concatenate([field[:, 1:] * weights, zero_plane], 1)
    along_first = along_first + jnp.concatenate([zero_plane, field[:, :-1] * weights], 1)
    padded = jnp.pad(field, ((0, 0), (0, 0), (1, 1), (1, 1)))
    nearby = along_first + padded[:, :, 2:, 1:-1] + padded[:, :, :-2, 1:-1]
    nearby = nearby + padded[:, :, 1:-1, 2:] + padded[:, :, 1:-1, :-2]
    return (6.0 + coarse_diag) * field - nearby


def reference(right_side, diagonal, aggregates):
    fine_pairs = cheb_pairs(FINE_LOWER, FINE_UPPER, DEGREE)
    coarse_pairs = cheb_pairs(COARSE_LOWER, COARSE_UPPER, COARSE_DEG)
    solution = jnp.zeros_like(right_side)
    residual = right_side
    update = jnp.zeros_like(right_side)
    for scale_old, scale_res in fine_pairs:
        update = scale_old * update + scale_res * residual
        solution = solution + update
        residual = residual - fine_apply(update, diagonal)
    coarse_rhs = 0.5 * residual.reshape(2, NX // 2, 2, NY // 2, 2, NZ // 2, 2).sum((2, 4, 6))
    coarse_diag = 0.5 * diagonal.reshape(NX // 2, 2, NY // 2, 2, NZ // 2, 2).sum((1, 3, 5))
    blocks = (jnp.arange(NX // 2, dtype=jnp.int32) // (CX // 2)).astype(jnp.int32)
    links = (aggregates[blocks[:-1]] == aggregates[blocks[1:]]).astype(jnp.float32)
    correction = jnp.zeros_like(coarse_rhs)
    coarse_res = coarse_rhs
    coarse_upd = jnp.zeros_like(coarse_rhs)
    for position, (scale_old, scale_res) in enumerate(coarse_pairs):
        coarse_upd = scale_old * coarse_upd + scale_res * coarse_res
        correction = correction + coarse_upd
        if position + 1 < COARSE_DEG:
            coarse_res = coarse_res - coarse_apply(coarse_upd, coarse_diag, links)
    spread = jnp.repeat(jnp.repeat(jnp.repeat(correction, 2, axis=1), 2, axis=2), 2, axis=3)
    solution = solution + spread
    residual = right_side - fine_apply(solution, diagonal)
    update = jnp.zeros_like(right_side)
    for position, (scale_old, scale_res) in enumerate(fine_pairs):
        update = scale_old * update + scale_res * residual
        solution = solution + update
        if position + 1 < DEGREE:
            residual = residual - fine_apply(update, diagonal)
    return solution
```

```python
import functools

import jax
import jax.numpy as jnp
from jax import lax
from jax.experimental import pallas as pl
from jax.experimental.pallas import tpu as pltpu
from jax.sharding import PartitionSpec as P

DEGREE = 3
COARSE_DEG = 6


FINE_LOWER = 3.0
FINE_UPPER = 12.4
COARSE_LOWER = 0.5
COARSE_UPPER = 13.4

LANES = 128
REACH = 7
F32 = jnp.float32


def cheb_pairs(lower, upper, count):
    middle = (upper + lower) / 2.0
    halfwidth = (upper - lower) / 2.0
    ratio_mid = middle / halfwidth
    rho_old = 1.0 / ratio_mid
    result = [(0.0, 1.0 / middle)]
    for repeat in range(count - 1):
        rho_new = 1.0 / (2.0 * ratio_mid - rho_old)
        result.append((rho_new * rho_old, 2.0 * rho_new / halfwidth))
        rho_old = rho_new
    return result


FINE = cheb_pairs(FINE_LOWER, FINE_UPPER, DEGREE)
COARSE = cheb_pairs(COARSE_LOWER, COARSE_UPPER, COARSE_DEG)


class Sizes:
    def __init__(self, nx, ny, nz, n_gy):
        assert nz == 2 * LANES and n_gy >= 2 and ny % 16 == 0 and nx % 4 == 0
        self.nx, self.ny, self.nz = nx, ny, nz
        self.two = n_gy == 2
        self.sides = 1 if self.two else 2
        self.wy = ny + 8 * self.sides
        self.cx, self.cy = nx // 2, ny // 2
        self.wc = self.cy + 8 * self.sides
        self.xmsg = 3 * REACH * self.cy + 8 * ny
        self.ymsg = 3 * self.cx * 8 + 8 * nx
        self.cmsg = 3 * REACH * 8 + 8


S_PAR, S_YOFF, S_HASL, S_HASR, S_LINKL, S_LINKR, S_RLO, S_RHI, S_HI0, S_HI1 = range(10)


def rows(start, size):
    return pl.ds(pl.multiple_of(start, 8), size)


def lane_masks(height):
    lane = lax.broadcasted_iota(jnp.int32, (height, LANES), 1)
    return lane == 0, lane == LANES - 1


def y_sum(v):
    return pltpu.roll(v, 1, 0) + pltpu.roll(v, v.shape[0] - 1, 0)


def z_sum(v0, v1, masks):
    first, last = masks
    l0, l1 = pltpu.roll(v0, 1, 1), pltpu.roll(v1, 1, 1)
    r0, r1 = pltpu.roll(v0, LANES - 1, 1), pltpu.roll(v1, LANES - 1, 1)
    return (
        jnp.where(first, 0.0, l0) + jnp.where(last, r1, r0),
        jnp.where(first, l0, l1) + jnp.where(last, 0.0, r1),
    )


def row_mask(height, low, high):
    row = lax.broadcasted_iota(jnp.int32, (height, LANES), 0)
    return (row >= low) & (row < high)


def fine_operator(ref, probe, plane, diag, wy, masks):
    v = [ref[probe, h, rows(plane * wy, wy), :] for h in range(2)]
    z = z_sum(v[0], v[1], masks)
    res = []
    for h in range(2):
        x = ref[probe, h, rows((plane - 1) * wy, wy), :] + ref[probe, h, rows((plane + 1) * wy, wy), :]
        res.append(diag[h] * v[h] - ((x + y_sum(v[h])) + z[h]))
    return v, res


def edge(high, size, count):
    return jnp.where(high, size - count, 0)


def pre_kernel(sz, *refs):
    n = sz.sides
    sc, rhs, diag, xa, xb = refs[:5]
    ys = refs[5 : 5 + n]
    cas = refs[5 + n : 5 + 2 * n]
    cbs = refs[5 + 2 * n : 5 + 3 * n]
    r_out, sol_out, dw, coarse, m_a, m_b = refs[5 + 3 * n : 11 + 3 * n]
    m_ys = refs[11 + 3 * n : 11 + 4 * n]
    m_cas = refs[11 + 4 * n : 11 + 5 * n]
    m_cbs = refs[11 + 5 * n : 11 + 6 * n]
    bw, r1, u2, u3, xs, ysm = refs[11 + 6 * n :]
    nx, ny, wy, cx, cy = sz.nx, sz.ny, sz.wy, sz.cx, sz.cy
    par_even = sc[S_PAR] == 0
    yoff = pl.multiple_of(sc[S_YOFF], 8)
    has_l, has_r = sc[S_HASL] == 1, sc[S_HASR] == 1
    his = [sc[S_HI0], sc[S_HI1]]
    half = [slice(0, LANES), slice(LANES, 2 * LANES)]
    masks = lane_masks(wy)

    zero8 = jnp.zeros((8, LANES), F32)
    zero_at = [jnp.where(sc[S_YOFF] == 0, ny, 0)] if sz.two else [0, ny + 8]

    def own(p, _):
        for h in range(2):
            for probe in range(2):
                bw[probe, h, rows((p + 3) * wy + yoff, ny), :] = rhs[probe, p, :, half[h]]
                for z in zero_at:
                    bw[probe, h, rows((p + 3) * wy + z, 8), :] = zero8
            dw[h, rows((p + 2) * wy + yoff, ny), :] = 6.0 + diag[p, :, half[h]]
            for z in zero_at:
                dw[h, rows((p + 2) * wy + z, 8), :] = zero8
        return 0

    lax.fori_loop(0, nx, own, 0)
    for msg, corners, to_right in ((xa, cas, par_even), (xb, cbs, jnp.logical_not(par_even))):
        b0 = jnp.where(to_right, nx + 3, 0)
        d0 = jnp.where(to_right, nx + 2, 0)
        for h in range(2):
            for k in range(3):
                for probe in range(2):
                    bw[probe, h, rows((b0 + k) * wy + yoff, ny), :] = msg[probe * 3 + k, :, half[h]]
                    for z in zero_at:
                        bw[probe, h, rows((b0 + k) * wy + z, 8), :] = zero8
            for k in range(2):
                dw[h, rows((d0 + k) * wy + yoff, ny), :] = 6.0 + msg[6 + k, :, half[h]]
                for z in zero_at:
                    dw[h, rows((d0 + k) * wy + z, 8), :] = zero8
        for s in range(n):
            bp = jnp.where(to_right, nx + 3, 1)
            dp = jnp.where(to_right, nx + 2, 1)
            br = jnp.where(his[s] == 1, ny, -2) + yoff
            dr = jnp.where(his[s] == 1, ny, -1) + yoff
            for h in range(2):
                for probe in range(2):
                    for k in range(2):
                        for r in range(2):
                            i = probe * 4 + k * 2 + r
                            bw[probe, h, pl.ds((bp + k) * wy + br + r, 1), :] = corners[s][i : i + 1, half[h]]
                dw[h, pl.ds(dp * wy + dr, 1), :] = 6.0 + corners[s][8:9, half[h]]
    for s in range(n):
        br = jnp.where(his[s] == 1, ny, -3) + yoff
        dr = jnp.where(his[s] == 1, ny, -2) + yoff
        for h in range(2):
            for k in range(3):
                for probe in range(2):
                    bw[probe, h, pl.ds(3 * wy + br + k, nx, stride=wy), :] = ys[s][probe * 3 + k, :, half[h]]
            for k in range(2):
                dw[h, pl.ds(2 * wy + dr + k, nx, stride=wy), :] = 6.0 + ys[s][6 + k, :, half[h]]
    zero = jnp.zeros((wy, LANES), F32)
    for probe in range(2):
        for h in range(2):
            for i in (1, nx + 2):
                u2[probe, h, rows(i * wy, wy), :] = zero
                u3[probe, h, rows(i * wy, wy), :] = zero

    inside = row_mask(wy, sc[S_RLO], sc[S_RHI])
    c0, (a1, c1), (a2, c2) = FINE[0][1], FINE[1], FINE[2]
    c1 = jnp.where(inside, c1, 0.0)
    c2 = jnp.where(inside, c2, 0.0)

    def step1(p):
        at = rows((p + 2) * wy, wy)
        d = [dw[h, at, :] for h in range(2)]
        for probe in range(2):
            v, av = fine_operator(bw, probe, p + 3, d, wy, masks)
            for h in range(2):
                res = v[h] - c0 * av[h]
                r1[probe, h, at, :] = res
                u2[probe, h, at, :] = (a1 * c0) * v[h] + c1 * res

    def step2(p):
        at = rows((p + 2) * wy, wy)
        d = [dw[h, at, :] for h in range(2)]
        for probe in range(2):
            v, av = fine_operator(u2, probe, p + 2, d, wy, masks)
            for h in range(2):
                res = r1[probe, h, at, :] - av[h]
                r1[probe, h, at, :] = res
                u3[probe, h, at, :] = a2 * v[h] + c2 * res

    mine = row_mask(wy, sc[S_YOFF], sc[S_YOFF] + ny)

    def step3(p):
        at = rows((p + 2) * wy, wy)
        to = rows(p * wy, wy)
        d = [dw[h, at, :] for h in range(2)]
        res = []
        for probe in range(2):
            v, av = fine_operator(u3, probe, p + 2, d, wy, masks)
            for h in range(2):
                out = jnp.where(mine, r1[probe, h, at, :] - av[h], 0.0)
                r_out[probe, h, to, :] = out
                sol_out[probe, h, to, :] = (
                    c0 * bw[probe, h, rows((p + 3) * wy, wy), :] + u2[probe, h, at, :] + v[h]
                )
                res.append(out)
        return res, d

    def pair(step):
        def body(i, _):
            step(2 * i)
            step(2 * i + 1)
            return 0

        lax.fori_loop(0, nx // 2, body, 0)

    def pair3(i, _):
        (low, d_low), (high, d_high) = step3(2 * i), step3(2 * i + 1)
        for k, value in enumerate([a + b for a, b in zip(low + d_low, high + d_high)]):
            xs[k] = value
        for k in range(6):
            even = xs[k, pl.ds(yoff, cy, stride=2), :]
            odd = xs[k, pl.ds(yoff + 1, cy, stride=2), :]
            ysm[k // 2, rows(i * cy, cy), half[k % 2]] = even + odd
        return 0

    @pl.when(has_l)
    def _():
        step1(-2)
        step1(-1)

    @pl.when(has_r)
    def _():
        step1(nx)
        step1(nx + 1)

    pair(step1)

    @pl.when(has_l)
    def _():
        step2(-1)

    @pl.when(has_r)
    def _():
        step2(nx)

    pair(step2)
    lax.fori_loop(0, nx // 2, pair3, 0)

    pairing = (
        lax.broadcasted_iota(jnp.int32, (2 * LANES, LANES), 0) // 2
        == lax.broadcasted_iota(jnp.int32, (2 * LANES, LANES), 1)
    ).astype(jnp.bfloat16)
    for f in range(3):
        v = ysm[f]
        total = None
        for _ in range(3):
            part = v.astype(jnp.bfloat16)
            v = v - part.astype(F32)
            dot = jnp.dot(part, pairing, preferred_element_type=F32)
            total = dot if total is None else total + dot
        coarse[f] = 0.5 * total - (18.0 if f == 2 else 0.0)

    send_hi = [hi == (1 if sz.two else 0) for hi in his]
    for msg, corners, right in ((m_a, m_cas, par_even), (m_b, m_cbs, jnp.logical_not(par_even))):
        c_at = edge(right, cx, REACH)
        r_at = edge(right, nx, 2)
        for f in range(3):
            msg[pl.ds(f * REACH * cy, REACH * cy), :] = coarse[f, rows(c_at * cy, REACH * cy), :]
            for s in range(n):
                row = edge(send_hi[s], cy, 8)
                for k in range(REACH):
                    corners[s][pl.ds((f * REACH + k) * 8, 8), :] = coarse[f, rows((c_at + k) * cy + row, 8), :]
        base = 3 * REACH * cy
        for probe in range(2):
            for h in range(2):
                for k in range(2):
                    i = (probe * 2 + h) * 2 + k
                    msg[pl.ds(base + i * ny, ny), :] = r_out[probe, h, rows((r_at + k) * wy + yoff, ny), :]
        for s in range(n):
            row = edge(send_hi[s], ny, 1)
            for probe in range(2):
                for h in range(2):
                    i = probe * 2 + h
                    value = r_out[probe, h, pl.ds(edge(right, nx, 1) * wy + yoff + row, 1), :]
                    corners[s][pl.ds(3 * REACH * 8 + i, 1), :] = value
            corners[s][pl.ds(3 * REACH * 8 + 4, 4), :] = jnp.zeros((4, LANES), F32)
    for s in range(n):
        row = edge(send_hi[s], cy, 8)
        for f in range(3):
            for x in range(cx):
                m_ys[s][pl.ds((f * cx + x) * 8, 8), :] = coarse[f, rows(x * cy + row, 8), :]
        row = edge(send_hi[s], ny, 2)
        for probe in range(2):
            for h in range(2):
                for k in range(2):
                    i = (probe * 2 + h) * 2 + k
                    m_ys[s][pl.ds(3 * cx * 8 + i * nx, nx), :] = r_out[
                        probe, h, pl.ds(yoff + row + k, nx, stride=wy), :
                    ]


def post_kernel(sz, *refs):
    n = sz.sides
    sc, r_in, sol_in, dw, coarse, x_a, x_b = refs[:7]
    ys = refs[7 : 7 + n]
    cas = refs[7 + n : 7 + 2 * n]
    cbs = refs[7 + 2 * n : 7 + 3 * n]
    out = refs[7 + 3 * n]
    cw, cu, cc, uz, wz, st_g, st_u, rh, re, r1, u2, ow, sem = refs[8 + 3 * n :]
    nx, ny, wy, cx, cy, wc = sz.nx, sz.ny, sz.wy, sz.cx, sz.cy, sz.wc
    par_even = sc[S_PAR] == 0
    yoff = pl.multiple_of(sc[S_YOFF], 8)
    has_l, has_r = sc[S_HASL] == 1, sc[S_HASR] == 1
    his = [sc[S_HI0], sc[S_HI1]]
    half = [slice(0, LANES), slice(LANES, 2 * LANES)]
    masks = lane_masks(wy)
    planes = cx + 2 * REACH

    y_at = [jnp.where(his[s] == 1, yoff + cy, yoff - 8) for s in range(n)]
    for f in range(3):
        for x in range(cx):
            cw[f, rows((x + REACH) * wc + yoff, cy), :] = coarse[f, rows(x * cy, cy), :]
            for s in range(n):
                cw[f, rows((x + REACH) * wc + y_at[s], 8), :] = ys[s][rows((f * cx + x) * 8, 8), :]
        for msg, corners, to_right in ((x_a, cas, par_even), (x_b, cbs, jnp.logical_not(par_even))):
            at = jnp.where(to_right, REACH + cx, 0)
            for k in range(REACH):
                cw[f, rows((at + k) * wc + yoff, cy), :] = msg[rows((f * REACH + k) * cy, cy), :]
                for s in range(n):
                    cw[f, rows((at + k) * wc + y_at[s], 8), :] = corners[s][rows((f * REACH + k) * 8, 8), :]

    first, last = lane_masks(wc)
    if sz.two:
        low = jnp.where(sc[S_YOFF] == 0, 0, 1)
        high = jnp.where(sc[S_YOFF] == 0, wc - 1, wc)
    else:
        low = jnp.where(sc[S_RLO] > 1, 8, 1)
        high = jnp.where(sc[S_RHI] < wy - 1, wc - 8, wc - 1)
    inside = row_mask(wc, low, high)
    link_l = sc[S_LINKL].astype(F32)
    link_r = sc[S_LINKR].astype(F32)
    for p in range(planes):
        at = pl.ds(p * wc, wc)
        for probe in range(2):
            u = jnp.where(inside, COARSE[0][1], 0.0) * cw[probe, at, :]
            cu[0, probe, at, :] = u
            cc[probe, at, :] = u
    for k in range(COARSE_DEG - 1):
        a, c = COARSE[k + 1]
        c = jnp.where(inside, c, 0.0)
        old, new = k % 2, 1 - k % 2
        for p in range(1 + k, planes - 1 - k):
            at = pl.ds(p * wc, wc)
            for probe in range(2):
                u = cu[old, probe, at, :]
                before = cu[old, probe, pl.ds((p - 1) * wc, wc), :]
                after = cu[old, probe, pl.ds((p + 1) * wc, wc), :]
                if p == REACH:
                    before = before * link_l
                if p == REACH - 1:
                    after = after * link_l
                if p == REACH + cx:
                    before = before * link_r
                if p == REACH + cx - 1:
                    after = after * link_r
                z = jnp.where(first, 0.0, pltpu.roll(u, 1, 1)) + jnp.where(last, 0.0, pltpu.roll(u, LANES - 1, 1))
                near = ((before + after) + y_sum(u)) + z
                res = cw[probe, at, :] - (cw[2, at, :] * u - near)
                if k + 2 < COARSE_DEG:
                    cw[probe, at, :] = res
                u = a * u + c * res
                if k + 2 < COARSE_DEG:
                    cu[new, probe, at, :] = u
                cc[probe, at, :] = cc[probe, at, :] + u

    depth = lax.broadcasted_iota(jnp.int32, (2 * LANES, 2 * LANES), 0) % LANES
    child = lax.broadcasted_iota(jnp.int32, (2 * LANES, 2 * LANES), 1)
    up = (child // 2 == depth).astype(jnp.bfloat16)
    aside = ((child == 2 * depth + 2) | (child == 2 * depth - 1)).astype(jnp.bfloat16)
    span = (cx + 4) * wc
    for probe in range(2):
        v = cc[probe, pl.ds((REACH - 2) * wc, span), :]
        hi = v.astype(jnp.bfloat16)
        lo = (v - hi.astype(F32)).astype(jnp.bfloat16)
        both = jnp.concatenate([hi, lo], axis=1)
        wide = jnp.dot(both, up, preferred_element_type=F32)
        beside = jnp.dot(both, aside, preferred_element_type=F32)
        for h in range(2):
            uz[probe, h] = wide[:, half[h]]
            wz[probe, h] = beside[:, half[h]]

    zero8 = jnp.zeros((8, LANES), F32)
    base = 3 * REACH * cy
    for msg, corners, to_right in ((x_a, cas, par_even), (x_b, cbs, jnp.logical_not(par_even))):
        at = jnp.where(to_right, 2, 0)
        for probe in range(2):
            for h in range(2):
                for k in range(2):
                    i = (probe * 2 + h) * 2 + k
                    rh[probe, h, rows((at + k) * wy + yoff, ny), :] = msg[pl.ds(base + i * ny, ny), :]
                    for s in range(n):
                        zero_at = jnp.where(his[s] == 1, yoff + ny, yoff - 8)
                        rh[probe, h, rows((at + k) * wy + zero_at, 8), :] = zero8
                for s in range(n):
                    row = jnp.where(his[s] == 1, yoff + ny, yoff - 1)
                    i = probe * 2 + h
                    rh[probe, h, pl.ds(jnp.where(to_right, 2, 1) * wy + row, 1), :] = corners[s][
                        pl.ds(3 * REACH * 8 + i, 1), :
                    ]

    c0, (a1, c1), (a2, c2) = FINE[0][1], FINE[1], FINE[2]
    if sz.two:
        low = jnp.where(sc[S_YOFF] == 0, 0, 6)
        high = jnp.where(sc[S_YOFF] == 0, ny + 2, wy)
    else:
        low = jnp.where(sc[S_RLO] > 1, 8, 6)
        high = jnp.where(sc[S_RHI] < wy - 1, ny + 8, ny + 10)
    valid = row_mask(wy, low, high)

    def spread(q, r_ref, r_plane, own):
        at = rows((q + 2) * wc, wc)
        for probe in range(2):
            for h in range(2):
                u = uz[probe, h, at, :]
                g = 3.0 * u + wz[probe, h, at, :]
                before, after = pltpu.roll(u, 1, 0), pltpu.roll(u, wc - 1, 0)
                for k in range(2):
                    gx = g + uz[probe, h, rows((q + 1 + 2 * k) * wc, wc), :]
                    st_g[probe, h, k, pl.ds(0, wc, stride=2), :] = gx + before
                    st_g[probe, h, k, pl.ds(1, wc, stride=2), :] = gx + after
                st_u[probe, h, pl.ds(0, wc, stride=2), :] = u
                st_u[probe, h, pl.ds(1, wc, stride=2), :] = u
        for k in range(2):
            to = rows((2 * q + k + 2) * wy, wy)
            for h in range(2):
                d = dw[h, to, :]
                for probe in range(2):
                    u = st_u[probe, h, rows(yoff, wy), :]
                    old = r_ref[probe, h, rows((r_plane + k) * wy, wy), :]
                    res = (old - d * u) + st_g[probe, h, k, rows(yoff, wy), :]
                    res = jnp.where(valid, res, 0.0)
                    re[probe, h, to, :] = res
                    if own:
                        ow[probe, 2 * q + k, :, half[h]] = (
                            sol_in[probe, h, rows((2 * q + k) * wy, wy), :] + u
                        )

    def own_planes(q, _):
        spread(q, r_in, 2 * q, True)
        return 0

    lax.fori_loop(0, cx, own_planes, 0)
    zero = jnp.zeros((wy, LANES), F32)
    for has, q, at in ((has_l, -1, 0), (has_r, cx, 2)):

        @pl.when(has)
        def _():
            spread(q, rh, at, False)

        @pl.when(jnp.logical_not(has))
        def _():
            for probe in range(2):
                for h in range(2):
                    for k in range(2):
                        re[probe, h, rows((2 * q + 2 + k) * wy, wy), :] = zero
                        u2[probe, h, rows((2 * q + 2 + k) * wy, wy), :] = zero

    for s in range(n):
        row = jnp.where(his[s] == 1, yoff + ny, yoff - 2)
        for probe in range(2):
            for h in range(2):
                for k in range(2):
                    i = (probe * 2 + h) * 2 + k
                    at = pl.ds(2 * wy + row + k, nx, stride=wy)
                    re[probe, h, at, :] = re[probe, h, at, :] + ys[s][pl.ds(3 * cx * 8 + i * nx, nx), :]

    c1 = jnp.where(row_mask(wy, sc[S_RLO], sc[S_RHI]), c1, 0.0)

    def step1(p):
        at = rows((p + 2) * wy, wy)
        d = [dw[h, at, :] for h in range(2)]
        for probe in range(2):
            v, av = fine_operator(re, probe, p + 2, d, wy, masks)
            for h in range(2):
                res = v[h] - c0 * av[h]
                r1[probe, h, at, :] = res
                u2[probe, h, at, :] = (a1 * c0) * v[h] + c1 * res

    def step2(p):
        at = rows((p + 2) * wy, wy)
        d = [dw[h, at, :] for h in range(2)]
        for probe in range(2):
            v, av = fine_operator(u2, probe, p + 2, d, wy, masks)
            for h in range(2):
                res = r1[probe, h, at, :] - av[h]
                last_two = (1.0 + a2) * v[h] + c2 * res
                ow[probe, p, :, half[h]] = (ow[probe, p, :, half[h]] + c0 * re[probe, h, at, :]) + last_two

    def body1(i, _):
        step1(2 * i)
        step1(2 * i + 1)
        return 0

    def body2(i, _):
        step2(2 * i)
        step2(2 * i + 1)
        return 0

    @pl.when(has_l)
    def _():
        step1(-1)

    @pl.when(has_r)
    def _():
        step1(nx)

    lax.fori_loop(0, nx // 2, body1, 0)
    pieces = 4
    size = nx // pieces
    copies = []
    for i in range(pieces):
        lax.fori_loop(i * size // 2, (i + 1) * size // 2, body2, 0)
        copy = pltpu.make_async_copy(
            ow.at[:, pl.ds(i * size, size), rows(yoff, ny), :], out.at[:, pl.ds(i * size, size)], sem.at[i]
        )
        copy.start()
        copies.append(copy)
    for copy in copies:
        copy.wait()


def pick_entry(table, where):
    places = jnp.arange(table.shape[0], dtype=jnp.int32)
    return jnp.sum(jnp.where(places == where, table, 0))


def on_device(n_gx, n_gy, right_side, diagonal, aggregates):
    nx, ny, nz = right_side.shape[1:]
    sz = Sizes(nx, ny, nz, n_gy)
    n, wy, wc, cx, cy = sz.sides, sz.wy, sz.wc, sz.cx, sz.cy
    i, j = lax.axis_index("gx"), lax.axis_index("gy")
    even = i % 2 == 0

    pairs_a = [(k, k ^ 1) for k in range(n_gx)]
    pairs_b = [(k, k + 1) for k in range(1, n_gx - 1, 2)] + [(k + 1, k) for k in range(1, n_gx - 1, 2)]
    along = [[(0, 1), (1, 0)]] if sz.two else [
        [(k, k - 1) for k in range(1, n_gy)],
        [(k, k + 1) for k in range(n_gy - 1)],
    ]

    def both(pairs, perm):
        return [(a * n_gy + c, b * n_gy + d) for a, b in pairs for c, d in perm]

    if sz.two:
        highs = [(j == 0).astype(jnp.int32)] * 2
        sends = [j == 0]
    else:
        highs = [jnp.int32(1), jnp.int32(0)]
        sends = [jnp.bool_(False), jnp.bool_(True)]

    def exchange(m_a, m_b, m_ys, m_cas, m_cbs):
        m_a, m_b, m_ys, m_cas, m_cbs = lax.optimization_barrier((m_a, m_b, m_ys, m_cas, m_cbs))
        got = (
            lax.ppermute(m_a, "gx", pairs_a),
            lax.ppermute(m_b, "gx", pairs_b),
            [lax.ppermute(m_ys[s], "gy", along[s]) for s in range(n)],
            [lax.ppermute(m_cas[s], ("gx", "gy"), both(pairs_a, along[s])) for s in range(n)],
            [lax.ppermute(m_cbs[s], ("gx", "gy"), both(pairs_b, along[s])) for s in range(n)],
        )
        return lax.optimization_barrier(got)

    def ends(field, axis, high, count):
        return lax.dynamic_slice_in_dim(field, edge(high, field.shape[axis], count), count, axis)

    def x_message(right):
        return jnp.concatenate(
            [ends(right_side, 1, right, 3).reshape(6, ny, nz), ends(diagonal, 0, right, 2)], 0
        )

    def y_message(high):
        b = ends(right_side, 2, high, 3).transpose(0, 2, 1, 3).reshape(6, nx, nz)
        return jnp.concatenate([b, ends(diagonal, 1, high, 2).transpose(1, 0, 2)], 0)

    def corner_message(right, high):
        b = ends(ends(right_side, 1, right, 2), 2, high, 2).reshape(8, nz)
        d = ends(ends(diagonal, 0, right, 1), 1, high, 1).reshape(1, nz)
        return jnp.concatenate([b, jnp.broadcast_to(d, (8, nz))], 0)

    odd = jnp.logical_not(even)
    x_a, x_b, ys, cas, cbs = exchange(
        x_message(even),
        x_message(odd),
        [y_message(h) for h in sends],
        [corner_message(even, h) for h in sends],
        [corner_message(odd, h) for h in sends],
    )

    here = pick_entry(aggregates, i)
    link_l = (i > 0) & (pick_entry(aggregates, i - 1) == here)
    link_r = (i < n_gx - 1) & (pick_entry(aggregates, i + 1) == here)
    yoff = 8 * j if sz.two else jnp.int32(8)
    if sz.two:
        r_lo, r_hi = j, wy - 1 + j
    else:
        r_lo = jnp.where(j == 0, 8, 1)
        r_hi = jnp.where(j == n_gy - 1, ny + 8, wy - 1)
    scalars = jnp.stack(
        [i % 2, yoff, i > 0, i < n_gx - 1, link_l, link_r, r_lo, r_hi, highs[0], highs[1]]
    ).astype(jnp.int32)

    smem = pl.BlockSpec(memory_space=pltpu.SMEM)
    vmem = pl.BlockSpec(memory_space=pltpu.VMEM)

    def shape(*dims):
        return jax.ShapeDtypeStruct(dims, F32)

    results = pl.pallas_call(
        functools.partial(pre_kernel, sz),
        in_specs=[smem] + [vmem] * (4 + 3 * n),
        out_specs=[vmem] * (6 + 3 * n),
        out_shape=[
            shape(2, 2, nx * wy, LANES),
            shape(2, 2, nx * wy, LANES),
            shape(2, (nx + 4) * wy, LANES),
            shape(3, cx * cy, LANES),
            shape(sz.xmsg, LANES),
            shape(sz.xmsg, LANES),
        ]
        + [shape(sz.ymsg, LANES)] * n
        + [shape(sz.cmsg, LANES)] * (2 * n),
        scratch_shapes=[
            pltpu.VMEM((2, 2, (nx + 6) * wy, LANES), F32),
            pltpu.VMEM((2, 2, (nx + 4) * wy, LANES), F32),
            pltpu.VMEM((2, 2, (nx + 4) * wy, LANES), F32),
            pltpu.VMEM((2, 2, (nx + 4) * wy, LANES), F32),
            pltpu.VMEM((6, wy, LANES), F32),
            pltpu.VMEM((3, cx * cy, 2 * LANES), F32),
        ],
        compiler_params=pltpu.CompilerParams(vmem_limit_bytes=48 << 20),
        name="pre_smooth",
    )(scalars, right_side, diagonal, x_a, x_b, *ys, *cas, *cbs)
    r_own, sol, dw, coarse = results[:4]
    x_a, x_b, ys, cas, cbs = exchange(
        results[4],
        results[5],
        list(results[6 : 6 + n]),
        list(results[6 + n : 6 + 2 * n]),
        list(results[6 + 2 * n :]),
    )
    planes = cx + 2 * REACH
    return pl.pallas_call(
        functools.partial(post_kernel, sz),
        in_specs=[smem] + [vmem] * (6 + 3 * n),
        out_specs=pl.BlockSpec(memory_space=pl.ANY),
        out_shape=shape(2, nx, ny, nz),
        scratch_shapes=[
            pltpu.VMEM((3, planes * wc, LANES), F32),
            pltpu.VMEM((2, 2, planes * wc, LANES), F32),
            pltpu.VMEM((2, planes * wc, LANES), F32),
            pltpu.VMEM((2, 2, (cx + 4) * wc, LANES), F32),
            pltpu.VMEM((2, 2, (cx + 4) * wc, LANES), F32),
            pltpu.VMEM((2, 2, 2, 2 * wc, LANES), F32),
            pltpu.VMEM((2, 2, 2 * wc, LANES), F32),
            pltpu.VMEM((2, 2, 4 * wy, LANES), F32),
            pltpu.VMEM((2, 2, (nx + 4) * wy, LANES), F32),
            pltpu.VMEM((2, 2, (nx + 4) * wy, LANES), F32),
            pltpu.VMEM((2, 2, (nx + 4) * wy, LANES), F32),
            pltpu.VMEM((2, nx, wy, nz), F32),
            pltpu.SemaphoreType.DMA((4,)),
        ],
        compiler_params=pltpu.CompilerParams(vmem_limit_bytes=48 << 20),
        name="correct_and_smooth",
    )(scalars, r_own, sol, dw, coarse, x_a, x_b, *ys, *cas, *cbs)


def solution(mesh):
    return jax.shard_map(
        functools.partial(on_device, mesh.shape["gx"], mesh.shape["gy"]),
        mesh=mesh,
        in_specs=(P(None, "gx", "gy", None), P("gx", "gy", None), P()),
        out_specs=P(None, "gx", "gy", None),
        check_vma=False,
    )
```

```python
import functools

import jax
import jax.numpy as jnp
from jax import lax
from jax.experimental import pallas as pl
from jax.experimental.pallas import tpu as pltpu
from jax.sharding import PartitionSpec as P

DEGREE = 3
COARSE_DEG = 6


FINE_LOWER = 3.0
FINE_UPPER = 12.4
COARSE_LOWER = 0.5
COARSE_UPPER = 13.4

LANES = 128
REACH = 7
F32 = jnp.float32


def cheb_pairs(lower, upper, count):
    middle = (upper + lower) / 2.0
    halfwidth = (upper - lower) / 2.0
    ratio_mid = middle / halfwidth
    rho_old = 1.0 / ratio_mid
    result = [(0.0, 1.0 / middle)]
    for repeat in range(count - 1):
        rho_new = 1.0 / (2.0 * ratio_mid - rho_old)
        result.append((rho_new * rho_old, 2.0 * rho_new / halfwidth))
        rho_old = rho_new
    return result


FINE = cheb_pairs(FINE_LOWER, FINE_UPPER, DEGREE)
COARSE = cheb_pairs(COARSE_LOWER, COARSE_UPPER, COARSE_DEG)


class Sizes:
    def __init__(self, nx, ny, nz, n_gx, n_gy):
        assert nz == 2 * LANES and n_gy >= 2 and ny % 16 == 0 and nx % 4 == 0
        self.nx, self.ny, self.nz = nx, ny, nz
        self.n_gx, self.n_gy = n_gx, n_gy
        self.two = n_gy == 2
        self.sides = 1 if self.two else 2
        self.wy = ny + 8 * self.sides
        self.cx, self.cy = nx // 2, ny // 2
        self.wc = self.cy + 8 * self.sides
        self.bw = (2, 2, (nx + 6) * self.wy, LANES)
        self.dw = (2, (nx + 4) * self.wy, LANES)
        self.brick = (2, 2, nx * self.wy, LANES)
        self.coarse = self.cx * self.cy
        self.x1 = 8 * 2 * ny
        self.y1 = 8 * 2 * nx
        self.c1 = 16
        self.x2_base = (3 * REACH - 1) * self.cy
        self.x2 = self.x2_base + 8 * ny
        self.y2_base = (3 * REACH - 1) * self.cx
        self.y2 = self.y2_base + 8 * nx
        self.c2 = 64


class Place:
    def __init__(self, sz):
        i, j = lax.axis_index("gx"), lax.axis_index("gy")
        self.i = i
        self.even = i % 2 == 0
        self.odd = i % 2 != 0
        self.has_l, self.has_r = i > 0, i < sz.n_gx - 1
        if sz.two:
            self.yoff = pl.multiple_of(8 * j, 8)
            self.high_in = [j == 0]
            self.high_out = [j == 0]
            self.fine = (j, sz.wy - 1 + j)
            self.crs = (j, sz.wc - 1 + j)
            self.valid = (6 * j, sz.ny + 2 + 6 * j)
        else:
            first, last = j == 0, j == sz.n_gy - 1
            self.yoff = 8
            self.high_in = [True, False]
            self.high_out = [False, True]
            self.fine = (jnp.where(first, 8, 1), jnp.where(last, sz.ny + 8, sz.wy - 1))
            self.crs = (jnp.where(first, 8, 1), jnp.where(last, sz.cy + 8, sz.wc - 1))
            self.valid = (jnp.where(first, 8, 6), jnp.where(last, sz.ny + 8, sz.ny + 10))


def pick(condition, yes, no):
    if isinstance(condition, bool):
        return yes if condition else no
    return jnp.where(condition, yes, no)


def edge(high, size, count):
    return pick(high, size - count, 0)


def rows(start, size):
    return pl.ds(pl.multiple_of(start, 8), size)


def lane_masks(height):
    lane = lax.broadcasted_iota(jnp.int32, (height, LANES), 1)
    return lane == 0, lane == LANES - 1


def row_mask(height, span):
    row = lax.broadcasted_iota(jnp.int32, (height, LANES), 0)
    return (row >= span[0]) & (row < span[1])


def y_sum(v):
    return pltpu.roll(v, 1, 0) + pltpu.roll(v, v.shape[0] - 1, 0)


def below(v, masks):
    return jnp.where(masks[0], 0.0, pltpu.roll(v, 1, 1))


def above(v, masks):
    return jnp.where(masks[1], 0.0, pltpu.roll(v, LANES - 1, 1))


def z_sum(even, odd, masks):
    return odd + below(odd, masks), even + above(even, masks)


def parity_matrix(transposed):
    row = lax.broadcasted_iota(jnp.int32, (2 * LANES, 2 * LANES), 0)
    col = lax.broadcasted_iota(jnp.int32, (2 * LANES, 2 * LANES), 1)
    if transposed:
        row, col = col, row
    return (row == 2 * (col % LANES) + col // LANES).astype(jnp.bfloat16)


def permute_lanes(v, matrix, terms):
    total = None
    for k in range(terms):
        part = v.astype(jnp.bfloat16)
        if k + 1 < terms:
            v = v - part.astype(F32)
        dot = jnp.dot(part, matrix, preferred_element_type=F32)
        total = dot if total is None else total + dot
    return total


def fine_operator(ref, probe, plane, diag, wy, masks):
    v = [ref[probe, h, rows(plane * wy, wy), :] for h in range(2)]
    z = z_sum(v[0], v[1], masks)
    res = []
    for h in range(2):
        x = ref[probe, h, rows((plane - 1) * wy, wy), :] + ref[probe, h, rows((plane + 1) * wy, wy), :]
        res.append(diag[h] * v[h] - ((x + y_sum(v[h])) + z[h]))
    return v, res


def looped(step, count, width=4):
    def body(i, _):
        for k in range(width):
            step(width * i + k)
        return 0

    lax.fori_loop(0, count // width, body, 0)


HALF = [slice(0, LANES), slice(LANES, 2 * LANES)]
CORNER1 = [(0, 0), (0, 1), (1, 0)]
CORNER2 = [(f, p, q) for f in range(3) for p in range(6) for q in range(6 - p - f // 2)]


def pack_kernel(sz, *refs):
    n = sz.sides
    rhs, diag, m_a, m_b = refs[:4]
    m_ys, m_cas, m_cbs = refs[4 : 4 + n], refs[4 + n : 4 + 2 * n], refs[4 + 2 * n : 4 + 3 * n]
    xr, xd, yr, yd, tr, td, sem = refs[4 + 3 * n :]
    nx, ny = sz.nx, sz.ny
    at = Place(sz)
    copies = []

    def fetch(src, dst):
        copy = pltpu.make_async_copy(src, dst, sem.at[len(copies)])
        copy.start()
        copies.append(copy)

    for s in range(n):
        slab = rows(edge(at.high_out[s], ny, 8), 8)
        fetch(rhs.at[:, :, slab, :], yr.at[s])
        fetch(diag.at[:, slab, :], yd.at[s])
    for e, right in enumerate((at.even, at.odd)):
        fetch(rhs.at[:, pl.ds(edge(right, nx, 3), 3)], xr.at[e])
        fetch(diag.at[pl.ds(edge(right, nx, 2), 2)], xd.at[e])
    split = parity_matrix(False)
    for copy in copies[: 2 * n]:
        copy.wait()
    for s in range(n):
        v = permute_lanes(yr[s].reshape(2 * nx * 8, 2 * LANES), split, 3)
        d = permute_lanes(yd[s].reshape(nx * 8, 2 * LANES), split, 3)
        for h in range(2):
            tr[s, h] = v[:, HALF[h]]
            td[s, h] = d[:, HALF[h]]
        high = at.high_out[s]
        for h in range(2):
            for k in range(3):
                for probe in range(2):
                    i = (probe * 3 + k) * 2 + h
                    row = edge(high, 8, 3) + k + probe * nx * 8
                    m_ys[s][pl.ds(i * nx, nx), :] = tr[s, h, pl.ds(row, nx, stride=8), :]
            for k in range(2):
                row = edge(high, 8, 2) + k
                m_ys[s][pl.ds((12 + 2 * k + h) * nx, nx), :] = td[s, h, pl.ds(row, nx, stride=8), :]
            for msgs, right in ((m_cas, at.even), (m_cbs, at.odd)):
                for m, (p, q) in enumerate(CORNER1):
                    row = pick(high, 7 - q, q) + pick(right, nx - 1 - p, p) * 8
                    for probe in range(2):
                        msgs[s][pl.ds((m * 2 + probe) * 2 + h, 1), :] = tr[s, h, pl.ds(row + probe * nx * 8, 1), :]
                row = pick(high, 7, 0) + pick(right, nx - 1, 0) * 8
                msgs[s][pl.ds(12 + h, 1), :] = td[s, h, pl.ds(row, 1), :]
                msgs[s][pl.ds(14 + h, 1), :] = td[s, h, pl.ds(row, 1), :]
    for copy in copies[2 * n :]:
        copy.wait()
    for e, msg in enumerate((m_a, m_b)):
        v = permute_lanes(xr[e].reshape(6 * ny, 2 * LANES), split, 3)
        d = permute_lanes(xd[e].reshape(2 * ny, 2 * LANES), split, 3)
        for k in range(6):
            for h in range(2):
                msg[pl.ds((2 * k + h) * ny, ny), :] = v[k * ny : (k + 1) * ny, HALF[h]]
        for k in range(2):
            for h in range(2):
                msg[pl.ds((12 + 2 * k + h) * ny, ny), :] = d[k * ny : (k + 1) * ny, HALF[h]]


def open_kernel(sz, first, rhs, diag, bw, dw, cd, rb, db, xs, sem):
    del first
    nx, ny, wy, cy = sz.nx, sz.ny, sz.wy, sz.cy
    at = Place(sz)
    split = parity_matrix(False)
    zero8 = jnp.zeros((8, LANES), F32)
    zero_at = [pick(at.high_in[s], at.yoff + ny, at.yoff - 8) for s in range(sz.sides)]
    width = 4
    pieces = 4
    size = nx // pieces
    copies = []
    for i in range(pieces):
        part = pl.ds(i * size, size)
        copies.append(
            (
                pltpu.make_async_copy(rhs.at[:, part], rb.at[:, part], sem.at[i, 0]),
                pltpu.make_async_copy(diag.at[part], db.at[part], sem.at[i, 1]),
            )
        )
        for copy in copies[-1]:
            copy.start()

    def body(i, _):
        for f in range(3):
            src = db[pl.ds(width * i, width)] if f == 2 else rb[f, pl.ds(width * i, width)]
            v = permute_lanes(src.reshape(width * ny, 2 * LANES), split, 3)
            if f == 2:
                v = v + 6.0
            for k in range(width):
                for h in range(2):
                    if f == 2:
                        ref, base = dw.at[h], (width * i + k + 2) * wy
                    else:
                        ref, base = bw.at[f, h], (width * i + k + 3) * wy
                    ref[rows(base + at.yoff, ny), :] = v[k * ny : (k + 1) * ny, HALF[h]]
                    for z in zero_at:
                        ref[rows(base + z, 8), :] = zero8
            if f == 2:
                for k in range(width // 2):
                    low, high = v[2 * k * ny : (2 * k + 1) * ny], v[(2 * k + 1) * ny : (2 * k + 2) * ny]
                    total = low + high
                    xs[k] = total[:, HALF[0]] + total[:, HALF[1]]
                    pair = xs[k, pl.ds(0, cy, stride=2), :] + xs[k, pl.ds(1, cy, stride=2), :]
                    cd[rows((i * (width // 2) + k) * cy, cy), :] = 0.5 * pair - 18.0
        return 0

    for i in range(pieces):
        for copy in copies[i]:
            copy.wait()
        lax.fori_loop(i * size // width, (i + 1) * size // width, body, 0)


def pre_kernel(sz, *refs):
    n = sz.sides
    cd, xa, xb = refs[2:5]
    ys, cas, cbs = refs[5 : 5 + n], refs[5 + n : 5 + 2 * n], refs[5 + 2 * n : 5 + 3 * n]
    outs = refs[5 + 3 * n :]
    bw, dw, r_out, sol_out, coarse, m_a, m_b = outs[:7]
    m_ys, m_cas, m_cbs = outs[7 : 7 + n], outs[7 + n : 7 + 2 * n], outs[7 + 2 * n : 7 + 3 * n]
    r1, u2, u3, xs = outs[7 + 3 * n :]
    nx, ny, wy, cx, cy = sz.nx, sz.ny, sz.wy, sz.cx, sz.cy
    at = Place(sz)
    yoff = at.yoff
    masks = lane_masks(wy)

    zero8 = jnp.zeros((8, LANES), F32)
    zero_at = [pick(at.high_in[s], yoff + ny, yoff - 8) for s in range(n)]
    for msg, corners, to_right in ((xa, cas, at.even), (xb, cbs, at.odd)):
        b0 = jnp.where(to_right, nx + 3, 0)
        d0 = jnp.where(to_right, nx + 2, 0)
        for h in range(2):
            for k in range(3):
                for probe in range(2):
                    i = (probe * 3 + k) * 2 + h
                    bw[probe, h, rows((b0 + k) * wy + yoff, ny), :] = msg[pl.ds(i * ny, ny), :]
                    for z in zero_at:
                        bw[probe, h, rows((b0 + k) * wy + z, 8), :] = zero8
            for k in range(2):
                dw[h, rows((d0 + k) * wy + yoff, ny), :] = 6.0 + msg[pl.ds((12 + 2 * k + h) * ny, ny), :]
                for z in zero_at:
                    dw[h, rows((d0 + k) * wy + z, 8), :] = zero8
            for s in range(n):
                for m, (p, q) in enumerate(CORNER1):
                    row = pick(at.high_in[s], yoff + ny + q, yoff - 1 - q)
                    row = row + jnp.where(to_right, nx + 3 + p, 2 - p) * wy
                    for probe in range(2):
                        bw[probe, h, pl.ds(row, 1), :] = corners[s][pl.ds((m * 2 + probe) * 2 + h, 1), :]
                row = pick(at.high_in[s], yoff + ny, yoff - 1) + jnp.where(to_right, nx + 2, 1) * wy
                dw[h, pl.ds(row, 1), :] = 6.0 + corners[s][pl.ds(12 + h, 1), :]
    for s in range(n):
        br = pick(at.high_in[s], ny, -3) + yoff
        dr = pick(at.high_in[s], ny, -2) + yoff
        for h in range(2):
            for k in range(3):
                for probe in range(2):
                    i = (probe * 3 + k) * 2 + h
                    bw[probe, h, pl.ds(3 * wy + br + k, nx, stride=wy), :] = ys[s][pl.ds(i * nx, nx), :]
            for k in range(2):
                i = 12 + 2 * k + h
                dw[h, pl.ds(2 * wy + dr + k, nx, stride=wy), :] = 6.0 + ys[s][pl.ds(i * nx, nx), :]
    zero = jnp.zeros((wy, LANES), F32)
    for probe in range(2):
        for h in range(2):
            for i in (1, nx + 2):
                u2[probe, h, rows(i * wy, wy), :] = zero
                u3[probe, h, rows(i * wy, wy), :] = zero

    inside = row_mask(wy, at.fine)
    c0, (a1, c1), (a2, c2) = FINE[0][1], FINE[1], FINE[2]
    c1 = jnp.where(inside, c1, 0.0)
    c2 = jnp.where(inside, c2, 0.0)

    def step1(p):
        to = rows((p + 2) * wy, wy)
        d = [dw[h, to, :] for h in range(2)]
        for probe in range(2):
            v, av = fine_operator(bw, probe, p + 3, d, wy, masks)
            for h in range(2):
                res = v[h] - c0 * av[h]
                r1[probe, h, to, :] = res
                u2[probe, h, to, :] = (a1 * c0) * v[h] + c1 * res

    def step2(p):
        to = rows((p + 2) * wy, wy)
        d = [dw[h, to, :] for h in range(2)]
        for probe in range(2):
            v, av = fine_operator(u2, probe, p + 2, d, wy, masks)
            for h in range(2):
                res = r1[probe, h, to, :] - av[h]
                r1[probe, h, to, :] = res
                u3[probe, h, to, :] = a2 * v[h] + c2 * res

    mine = row_mask(wy, (yoff, yoff + ny))

    def step3(p):
        src = rows((p + 2) * wy, wy)
        to = rows(p * wy, wy)
        d = [dw[h, src, :] for h in range(2)]
        sums = []
        for probe in range(2):
            v, av = fine_operator(u3, probe, p + 2, d, wy, masks)
            total = None
            for h in range(2):
                out = jnp.where(mine, r1[probe, h, src, :] - av[h], 0.0)
                r_out[probe, h, to, :] = out
                sol_out[probe, h, to, :] = (
                    c0 * bw[probe, h, rows((p + 3) * wy, wy), :] + u2[probe, h, src, :] + v[h]
                )
                total = out if total is None else total + out
            sums.append(total)
        return sums

    def steps3(i, _):
        for k in range(2):
            low, high = step3(4 * i + 2 * k), step3(4 * i + 2 * k + 1)
            for probe in range(2):
                xs[k, probe] = low[probe] + high[probe]
        for k in range(2):
            for probe in range(2):
                pair = (
                    xs[k, probe, pl.ds(yoff, cy, stride=2), :] + xs[k, probe, pl.ds(yoff + 1, cy, stride=2), :]
                )
                coarse[probe, rows((2 * i + k) * cy, cy), :] = 0.5 * pair
        return 0

    @pl.when(at.has_l)
    def _():
        step1(-2)
        step1(-1)

    @pl.when(at.has_r)
    def _():
        step1(nx)
        step1(nx + 1)

    looped(step1, nx)

    @pl.when(at.has_l)
    def _():
        step2(-1)

    @pl.when(at.has_r)
    def _():
        step2(nx)

    looped(step2, nx)
    lax.fori_loop(0, nx // 4, steps3, 0)

    field = [coarse.at[0], coarse.at[1], cd]
    depth = [REACH, REACH, REACH - 1]
    for msg, corners, right in ((m_a, m_cas, at.even), (m_b, m_cbs, at.odd)):
        for f in range(3):
            size = depth[f] * cy
            msg[pl.ds(f * REACH * cy, size), :] = field[f][rows(edge(right, cx, depth[f]) * cy, size), :]
        for s in range(n):
            for m, (f, p, q) in enumerate(CORNER2):
                row = pick(at.high_out[s], cy - 1 - q, q) + pick(right, cx - 1 - p, p) * cy
                corners[s][pl.ds(m, 1), :] = field[f][pl.ds(row, 1), :]
            row = pick(at.high_out[s], yoff + ny - 1, yoff) + pick(right, nx - 1, 0) * wy
            for probe in range(2):
                for h in range(2):
                    i = len(CORNER2) + probe * 2 + h
                    corners[s][pl.ds(i, 1), :] = r_out[probe, h, pl.ds(row, 1), :]
            corners[s][pl.ds(sz.c2 - 3, 3), :] = jnp.zeros((3, LANES), F32)
        for probe in range(2):
            for h in range(2):
                for k in range(2):
                    i = (probe * 2 + h) * 2 + k
                    row = (edge(right, nx, 2) + k) * wy + yoff
                    msg[pl.ds(sz.x2_base + i * ny, ny), :] = r_out[probe, h, rows(row, ny), :]
    for s in range(n):
        for f in range(3):
            for k in range(depth[f]):
                row = edge(at.high_out[s], cy, depth[f]) + k
                m_ys[s][pl.ds((f * REACH + k) * cx, cx), :] = field[f][pl.ds(row, cx, stride=cy), :]
        row = edge(at.high_out[s], ny, 2) + yoff
        for probe in range(2):
            for h in range(2):
                for k in range(2):
                    i = (probe * 2 + h) * 2 + k
                    m_ys[s][pl.ds(sz.y2_base + i * nx, nx), :] = r_out[probe, h, pl.ds(row + k, nx, stride=wy), :]


def post_kernel(sz, *refs):
    n = sz.sides
    agg, r_in, sol_in, dw, coarse, cd, x_a, x_b = refs[:8]
    ys, cas, cbs = refs[8 : 8 + n], refs[8 + n : 8 + 2 * n], refs[8 + 2 * n : 8 + 3 * n]
    out = refs[8 + 3 * n]
    cw, cu, cc, st_g, st_u, rh, re, r1, u2, acc, ow, sem = refs[9 + 3 * n :]
    nx, ny, wy, cx, cy, wc = sz.nx, sz.ny, sz.wy, sz.cx, sz.cy, sz.wc
    at = Place(sz)
    yoff = at.yoff
    masks = lane_masks(wy)
    planes = cx + 2 * REACH

    zero8 = jnp.zeros((8, LANES), F32)
    zero_at = [pick(at.high_in[s], yoff + cy, yoff - 8) for s in range(n)]
    field = [coarse.at[0], coarse.at[1], cd]
    depth = [REACH, REACH, REACH - 1]
    for f in range(3):
        for p in range(planes):
            for z in zero_at:
                cw[f, rows(p * wc + z, 8), :] = zero8
        for x in range(cx):
            cw[f, rows((x + REACH) * wc + yoff, cy), :] = field[f][rows(x * cy, cy), :]
        for s in range(n):
            for k in range(depth[f]):
                row = pick(at.high_in[s], yoff + cy, yoff - depth[f]) + k
                cw[f, pl.ds(REACH * wc + row, cx, stride=wc), :] = ys[s][rows((f * REACH + k) * cx, cx), :]
        for msg, to_right in ((x_a, at.even), (x_b, at.odd)):
            first = jnp.where(to_right, REACH + cx, REACH - depth[f])
            for k in range(depth[f]):
                cw[f, rows((first + k) * wc + yoff, cy), :] = msg[rows((f * REACH + k) * cy, cy), :]
    for corners, to_right in ((cas, at.even), (cbs, at.odd)):
        for s in range(n):
            for m, (f, p, q) in enumerate(CORNER2):
                row = pick(at.high_in[s], yoff + cy + q, yoff - 1 - q)
                row = row + jnp.where(to_right, REACH + cx + p, REACH - 1 - p) * wc
                cw[f, pl.ds(row, 1), :] = corners[s][pl.ds(m, 1), :]

    cmasks = lane_masks(wc)
    inside = row_mask(wc, at.crs)
    i = at.i
    here = agg[i]
    link_l = (at.has_l & (agg[jnp.maximum(i - 1, 0)] == here)).astype(F32)
    link_r = (at.has_r & (agg[jnp.minimum(i + 1, sz.n_gx - 1)] == here)).astype(F32)
    for p in range(planes):
        to = pl.ds(p * wc, wc)
        for probe in range(2):
            u = jnp.where(inside, COARSE[0][1], 0.0) * cw[probe, to, :]
            cu[0, probe, to, :] = u
            cc[probe, to, :] = u
    for k in range(COARSE_DEG - 1):
        a, c = COARSE[k + 1]
        c = jnp.where(inside, c, 0.0)
        old, new = k % 2, 1 - k % 2
        for p in range(1 + k, planes - 1 - k):
            to = pl.ds(p * wc, wc)
            for probe in range(2):
                u = cu[old, probe, to, :]
                before = cu[old, probe, pl.ds((p - 1) * wc, wc), :]
                after = cu[old, probe, pl.ds((p + 1) * wc, wc), :]
                if p == REACH:
                    before = before * link_l
                if p == REACH - 1:
                    after = after * link_l
                if p == REACH + cx:
                    before = before * link_r
                if p == REACH + cx - 1:
                    after = after * link_r
                near = ((before + after) + y_sum(u)) + (below(u, cmasks) + above(u, cmasks))
                res = cw[probe, to, :] - (cw[2, to, :] * u - near)
                u = a * u + c * res
                if k + 2 < COARSE_DEG:
                    cw[probe, to, :] = res
                    cu[new, probe, to, :] = u
                cc[probe, to, :] = cc[probe, to, :] + u

    for msg, corners, to_right in ((x_a, cas, at.even), (x_b, cbs, at.odd)):
        for probe in range(2):
            for h in range(2):
                for k in range(2):
                    i = (probe * 2 + h) * 2 + k
                    base = (jnp.where(to_right, 2, 0) + k) * wy
                    rh[probe, h, rows(base + yoff, ny), :] = msg[pl.ds(sz.x2_base + i * ny, ny), :]
                    for s in range(n):
                        zero_row = pick(at.high_in[s], yoff + ny, yoff - 8)
                        rh[probe, h, rows(base + zero_row, 8), :] = zero8
                for s in range(n):
                    row = pick(at.high_in[s], yoff + ny, yoff - 1) + jnp.where(to_right, 2, 1) * wy
                    i = len(CORNER2) + probe * 2 + h
                    rh[probe, h, pl.ds(row, 1), :] = corners[s][pl.ds(i, 1), :]

    c0, (a1, c1), (a2, c2) = FINE[0][1], FINE[1], FINE[2]
    valid = row_mask(wy, at.valid)

    def spread(q, r_ref, r_plane, own):
        for probe in range(2):
            u = cc[probe, rows((q + REACH) * wc, wc), :]
            sides = [cc[probe, rows((q + REACH - 1 + 2 * k) * wc, wc), :] for k in range(2)]
            u3 = 3.0 * u
            shifted = [pltpu.roll(u, 1, 0), pltpu.roll(u, wc - 1, 0)]
            for row in range(2):
                st_u[probe, pl.ds(row, wc, stride=2), :] = u
            for h in range(2):
                g = u3 + (above(u, cmasks) if h else below(u, cmasks))
                for k in range(2):
                    for row in range(2):
                        st_g[probe, h, k, pl.ds(row, wc, stride=2), :] = (g + sides[k]) + shifted[row]
        for k in range(2):
            to = rows((2 * q + k + 2) * wy, wy)
            for h in range(2):
                d = dw[h, to, :]
                for probe in range(2):
                    u = st_u[probe, rows(yoff, wy), :]
                    old = r_ref[probe, h, rows((r_plane + k) * wy, wy), :]
                    res = (old - d * u) + st_g[probe, h, k, rows(yoff, wy), :]
                    res = jnp.where(valid, res, 0.0)
                    re[probe, h, to, :] = res
                    if own:
                        mine = rows((2 * q + k) * wy, wy)
                        acc[probe, h, mine, :] = (sol_in[probe, h, mine, :] + u) + c0 * res

    def own_planes(q):
        spread(q, r_in, 2 * q, True)

    looped(own_planes, cx, 2)
    zero = jnp.zeros((wy, LANES), F32)
    for has, q, first in ((at.has_l, -1, 0), (at.has_r, cx, 2)):

        @pl.when(has)
        def _():
            spread(q, rh, first, False)

        @pl.when(jnp.logical_not(has))
        def _():
            for probe in range(2):
                for h in range(2):
                    for k in range(2):
                        re[probe, h, rows((2 * q + 2 + k) * wy, wy), :] = zero
                        u2[probe, h, rows((2 * q + 2 + k) * wy, wy), :] = zero

    for s in range(n):
        row = pick(at.high_in[s], yoff + ny, yoff - 2)
        for probe in range(2):
            for h in range(2):
                for k in range(2):
                    i = (probe * 2 + h) * 2 + k
                    to = pl.ds(2 * wy + row + k, nx, stride=wy)
                    re[probe, h, to, :] = re[probe, h, to, :] + ys[s][pl.ds(sz.y2_base + i * nx, nx), :]

    c1 = jnp.where(row_mask(wy, at.fine), c1, 0.0)

    def step1(p):
        to = rows((p + 2) * wy, wy)
        d = [dw[h, to, :] for h in range(2)]
        for probe in range(2):
            v, av = fine_operator(re, probe, p + 2, d, wy, masks)
            for h in range(2):
                res = v[h] - c0 * av[h]
                r1[probe, h, to, :] = res
                u2[probe, h, to, :] = (a1 * c0) * v[h] + c1 * res

    join = parity_matrix(True)

    def steps2(i, _):
        width = 4
        for probe in range(2):
            done = []
            for k in range(width):
                p = width * i + k
                to = rows((p + 2) * wy, wy)
                d = [dw[h, to, :] for h in range(2)]
                v, av = fine_operator(u2, probe, p + 2, d, wy, masks)
                parts = []
                for h in range(2):
                    res = r1[probe, h, to, :] - av[h]
                    parts.append(acc[probe, h, rows(p * wy, wy), :] + ((1.0 + a2) * v[h] + c2 * res))
                done.append(jnp.concatenate(parts, axis=1))
            joined = permute_lanes(jnp.concatenate(done, axis=0), join, 2)
            for k in range(width):
                ow[probe, width * i + k] = joined[k * wy : (k + 1) * wy]
        return 0

    @pl.when(at.has_l)
    def _():
        step1(-1)

    @pl.when(at.has_r)
    def _():
        step1(nx)

    looped(step1, nx)
    pieces = 4
    size = nx // pieces
    copies = []
    for i in range(pieces):
        lax.fori_loop(i * size // 4, (i + 1) * size // 4, steps2, 0)
        copy = pltpu.make_async_copy(
            ow.at[:, pl.ds(i * size, size), rows(yoff, ny), :], out.at[:, pl.ds(i * size, size)], sem.at[i]
        )
        copy.start()
        copies.append(copy)
    for copy in copies:
        copy.wait()


def on_device(n_gx, n_gy, right_side, diagonal, aggregates):
    nx, ny, nz = right_side.shape[1:]
    sz = Sizes(nx, ny, nz, n_gx, n_gy)
    n, wy, wc, cx = sz.sides, sz.wy, sz.wc, sz.cx

    pairs_a = [(k, k ^ 1) for k in range(n_gx)]
    pairs_b = [(k, k + 1) for k in range(1, n_gx - 1, 2)] + [(k + 1, k) for k in range(1, n_gx - 1, 2)]
    along = [[(0, 1), (1, 0)]] if sz.two else [
        [(k, k - 1) for k in range(1, n_gy)],
        [(k, k + 1) for k in range(n_gy - 1)],
    ]

    def both(pairs, perm):
        return [(a * n_gy + c, b * n_gy + d) for a, b in pairs for c, d in perm]

    def exchange(messages):
        m_a, m_b, rest = messages[0], messages[1], messages[2:]
        got = [lax.ppermute(m_a, "gx", pairs_a), lax.ppermute(m_b, "gx", pairs_b)]
        got += [lax.ppermute(rest[s], "gy", along[s]) for s in range(n)]
        got += [lax.ppermute(rest[n + s], ("gx", "gy"), both(pairs_a, along[s])) for s in range(n)]
        got += [lax.ppermute(rest[2 * n + s], ("gx", "gy"), both(pairs_b, along[s])) for s in range(n)]
        return got

    smem = pl.BlockSpec(memory_space=pltpu.SMEM)
    vmem = pl.BlockSpec(memory_space=pltpu.VMEM)
    hbm = pl.BlockSpec(memory_space=pltpu.HBM)
    params = pltpu.CompilerParams(vmem_limit_bytes=24 << 20)

    def shape(*dims):
        return jax.ShapeDtypeStruct(dims, F32)

    def messages(x, y, c):
        return [shape(x, LANES)] * 2 + [shape(y, LANES)] * n + [shape(c, LANES)] * (2 * n)

    packed = pl.pallas_call(
        functools.partial(pack_kernel, sz),
        in_specs=[hbm] * 2,
        out_specs=[vmem] * (2 + 3 * n),
        out_shape=messages(sz.x1, sz.y1, sz.c1),
        scratch_shapes=[
            pltpu.VMEM((2, 2, 3, ny, nz), F32),
            pltpu.VMEM((2, 2, ny, nz), F32),
            pltpu.VMEM((n, 2, nx, 8, nz), F32),
            pltpu.VMEM((n, nx, 8, nz), F32),
            pltpu.VMEM((n, 2, 2 * nx * 8, LANES), F32),
            pltpu.VMEM((n, 2, nx * 8, LANES), F32),
            pltpu.SemaphoreType.DMA((2 * n + 4,)),
        ],
        compiler_params=pltpu.CompilerParams(vmem_limit_bytes=120 << 19),
        name="pack_kernel",
    )(right_side, diagonal)
    halos = exchange(packed)
    bw, dw, cd = pl.pallas_call(
        functools.partial(open_kernel, sz),
        in_specs=[pl.BlockSpec(memory_space=pl.ANY), hbm, hbm],
        out_specs=[vmem] * 3,
        out_shape=[shape(*sz.bw), shape(*sz.dw), shape(sz.coarse, LANES)],
        scratch_shapes=[
            pltpu.VMEM((2, nx, ny, nz), F32),
            pltpu.VMEM((nx, ny, nz), F32),
            pltpu.VMEM((2, ny, LANES), F32),
            pltpu.SemaphoreType.DMA((4, 2)),
        ],
        compiler_params=params,
        name="open_kernel",
    )(packed[-1], right_side, diagonal)
    results = pl.pallas_call(
        functools.partial(pre_kernel, sz),
        in_specs=[vmem] * (5 + 3 * n),
        out_specs=[vmem] * (7 + 3 * n),
        out_shape=[shape(*sz.bw), shape(*sz.dw), shape(*sz.brick), shape(*sz.brick), shape(2, sz.coarse, LANES)]
        + messages(sz.x2, sz.y2, sz.c2),
        scratch_shapes=[pltpu.VMEM((2, 2, (nx + 4) * wy, LANES), F32)] * 3 + [pltpu.VMEM((2, 2, wy, LANES), F32)],
        input_output_aliases={0: 0, 1: 1},
        compiler_params=params,
        name="pre_smooth",
    )(bw, dw, cd, *halos)
    dw, r_own, sol, coarse = results[1:5]
    halos = exchange(results[5:])
    planes = cx + 2 * REACH
    return pl.pallas_call(
        functools.partial(post_kernel, sz),
        in_specs=[smem] + [vmem] * (7 + 3 * n),
        out_specs=hbm,
        out_shape=shape(2, nx, ny, nz),
        scratch_shapes=[
            pltpu.VMEM((3, planes * wc, LANES), F32),
            pltpu.VMEM((2, 2, planes * wc, LANES), F32),
            pltpu.VMEM((2, planes * wc, LANES), F32),
            pltpu.VMEM((2, 2, 2, 2 * wc, LANES), F32),
            pltpu.VMEM((2, 2 * wc, LANES), F32),
            pltpu.VMEM((2, 2, 4 * wy, LANES), F32),
        ]
        + [pltpu.VMEM((2, 2, (nx + 4) * wy, LANES), F32)] * 3
        + [
            pltpu.VMEM(sz.brick, F32),
            pltpu.VMEM((2, nx, wy, nz), F32),
            pltpu.SemaphoreType.DMA((4,)),
        ],
        compiler_params=params,
        name="correct_and_smooth",
    )(aggregates, r_own, sol, dw, coarse, cd, *halos)


def solution(mesh):
    return jax.shard_map(
        functools.partial(on_device, mesh.shape["gx"], mesh.shape["gy"]),
        mesh=mesh,
        in_specs=(P(None, "gx", "gy", None), P("gx", "gy", None), P()),
        out_specs=P(None, "gx", "gy", None),
        check_vma=False,
    )
```

```python
import functools

import jax
import jax.numpy as jnp
from jax import lax
from jax.experimental import pallas as pl
from jax.experimental.pallas import tpu as pltpu
from jax.sharding import PartitionSpec as P

DEGREE = 3
COARSE_DEG = 6


FINE_LOWER = 3.0
FINE_UPPER = 12.4
COARSE_LOWER = 0.5
COARSE_UPPER = 13.4

LANES = 128
REACH = 7
F32 = jnp.float32


def cheb_pairs(lower, upper, count):
    middle = (upper + lower) / 2.0
    halfwidth = (upper - lower) / 2.0
    ratio_mid = middle / halfwidth
    rho_old = 1.0 / ratio_mid
    result = [(0.0, 1.0 / middle)]
    for repeat in range(count - 1):
        rho_new = 1.0 / (2.0 * ratio_mid - rho_old)
        result.append((rho_new * rho_old, 2.0 * rho_new / halfwidth))
        rho_old = rho_new
    return result


FINE = cheb_pairs(FINE_LOWER, FINE_UPPER, DEGREE)
COARSE = cheb_pairs(COARSE_LOWER, COARSE_UPPER, COARSE_DEG)


class Sizes:
    def __init__(self, nx, ny, nz, n_gx, n_gy):
        assert nz == 2 * LANES and n_gy >= 2 and ny % 16 == 0 and nx % 4 == 0
        self.nx, self.ny, self.nz = nx, ny, nz
        self.n_gx, self.n_gy = n_gx, n_gy
        self.two = n_gy == 2
        self.sides = 1 if self.two else 2
        self.wy = ny + 8 * self.sides
        self.cx, self.cy = nx // 2, ny // 2
        self.wc = self.cy + 8 * self.sides
        self.bw = (2, 2, (nx + 6) * self.wy, LANES)
        self.dw = (2, (nx + 4) * self.wy, LANES)
        self.brick = (2, 2, nx * self.wy, LANES)
        self.coarse = self.cx * self.cy
        self.x1 = 8 * 2 * ny
        self.y1 = 8 * 2 * nx
        self.c1 = 16
        self.x2_base = (3 * REACH - 1) * self.cy
        self.x2 = self.x2_base + 8 * ny
        self.y2_base = (3 * REACH - 1) * self.cx
        self.y2 = self.y2_base + 8 * nx
        self.c2 = 64


class Place:
    def __init__(self, sz):
        i, j = lax.axis_index("gx"), lax.axis_index("gy")
        self.i = i
        self.even = i % 2 == 0
        self.odd = i % 2 != 0
        self.has_l, self.has_r = i > 0, i < sz.n_gx - 1
        if sz.two:
            self.yoff = pl.multiple_of(8 * j, 8)
            self.high_in = [j == 0]
            self.high_out = [j == 0]
            self.fine = (j, sz.wy - 1 + j)
            self.crs = (j, sz.wc - 1 + j)
            self.valid = (6 * j, sz.ny + 2 + 6 * j)
        else:
            first, last = j == 0, j == sz.n_gy - 1
            self.yoff = 8
            self.high_in = [True, False]
            self.high_out = [False, True]
            self.fine = (jnp.where(first, 8, 1), jnp.where(last, sz.ny + 8, sz.wy - 1))
            self.crs = (jnp.where(first, 8, 1), jnp.where(last, sz.cy + 8, sz.wc - 1))
            self.valid = (jnp.where(first, 8, 6), jnp.where(last, sz.ny + 8, sz.ny + 10))


def pick(condition, yes, no):
    if isinstance(condition, bool):
        return yes if condition else no
    return jnp.where(condition, yes, no)


def edge(high, size, count):
    return pick(high, size - count, 0)


def rows(start, size):
    return pl.ds(pl.multiple_of(start, 8), size)


def lane_masks(height):
    lane = lax.broadcasted_iota(jnp.int32, (height, LANES), 1)
    return lane == 0, lane == LANES - 1


def row_mask(height, span):
    row = lax.broadcasted_iota(jnp.int32, (height, LANES), 0)
    return (row >= span[0]) & (row < span[1])


def y_sum(v):
    return pltpu.roll(v, 1, 0) + pltpu.roll(v, v.shape[0] - 1, 0)


def below(v, masks):
    return jnp.where(masks[0], 0.0, pltpu.roll(v, 1, 1))


def above(v, masks):
    return jnp.where(masks[1], 0.0, pltpu.roll(v, LANES - 1, 1))


def z_sum(even, odd, masks):
    return odd + below(odd, masks), even + above(even, masks)


def parity_matrix(transposed):
    row = lax.broadcasted_iota(jnp.int32, (2 * LANES, 2 * LANES), 0)
    col = lax.broadcasted_iota(jnp.int32, (2 * LANES, 2 * LANES), 1)
    if transposed:
        row, col = col, row
    return (row == 2 * (col % LANES) + col // LANES).astype(jnp.bfloat16)


def permute_lanes(v, matrix, terms):
    total = None
    for k in range(terms):
        part = v.astype(jnp.bfloat16)
        if k + 1 < terms:
            v = v - part.astype(F32)
        dot = jnp.dot(part, matrix, preferred_element_type=F32)
        total = dot if total is None else total + dot
    return total


def sweep(ref, shift, dw, first, count, wy, masks, use):
    for probe in range(2):

        def load(plane):
            return [ref[probe, h, rows((plane + shift) * wy, wy), :] for h in range(2)]

        before, now = load(first - 1), load(first)
        for k in range(count):
            plane = first + k
            at = plane + shift
            after = load(plane + 1)
            z = z_sum(now[0], now[1], masks)
            res = []
            for h in range(2):
                y = pltpu.roll(now[h], 1, 0) + ref[probe, h, pl.ds(at * wy + 1, wy), :]
                d = dw[h, rows((plane + 2) * wy, wy), :]
                res.append(d * now[h] - (((before[h] + after[h]) + y) + z[h]))
            use(probe, plane, now, res)
            before, now = now, after


def looped(step, count, width=4):
    def body(i, _):
        step(width * i, width)
        return 0

    lax.fori_loop(0, count // width, body, 0)


ORDER1 = "aby"
ORDER2 = "yba"


def sorted_messages(sz, order, refs):
    found, k = {}, 0
    for name in order:
        count = sz.sides if name == "y" else 1
        found[name] = refs[k : k + count]
        k += count
    return found["y"], found["b"][0], found["a"][0]


HALF = [slice(0, LANES), slice(LANES, 2 * LANES)]
CORNER1 = [(0, 0), (0, 1), (1, 0)]
CORNER2 = [(f, p, q) for f in range(3) for p in range(6) for q in range(6 - p - f // 2)]


def pack_kernel(sz, *refs):
    n = sz.sides
    rhs, diag = refs[:2]
    m_ys, m_b, m_a = sorted_messages(sz, ORDER1, refs[2 : 4 + n])
    m_cas, m_cbs = refs[4 + n : 4 + 2 * n], refs[4 + 2 * n : 4 + 3 * n]
    xr, xd, yr, yd, tr, td, sem = refs[4 + 3 * n :]
    nx, ny = sz.nx, sz.ny
    at = Place(sz)
    copies = []

    def fetch(src, dst):
        copy = pltpu.make_async_copy(src, dst, sem.at[len(copies)])
        copy.start()
        copies.append(copy)

    for s in range(n):
        slab = rows(edge(at.high_out[s], ny, 8), 8)
        fetch(rhs.at[:, :, slab, :], yr.at[s])
        fetch(diag.at[:, slab, :], yd.at[s])
    for e, right in enumerate((at.even, at.odd)):
        fetch(rhs.at[:, pl.ds(edge(right, nx, 3), 3)], xr.at[e])
        fetch(diag.at[pl.ds(edge(right, nx, 2), 2)], xd.at[e])
    split = parity_matrix(False)
    for copy in copies[: 2 * n]:
        copy.wait()
    for s in range(n):
        v = permute_lanes(yr[s].reshape(2 * nx * 8, 2 * LANES), split, 2)
        d = permute_lanes(yd[s].reshape(nx * 8, 2 * LANES), split, 2)
        for h in range(2):
            tr[s, h] = v[:, HALF[h]]
            td[s, h] = d[:, HALF[h]]
        high = at.high_out[s]
        for h in range(2):
            for k in range(3):
                for probe in range(2):
                    i = (probe * 3 + k) * 2 + h
                    row = edge(high, 8, 3) + k + probe * nx * 8
                    m_ys[s][pl.ds(i * nx, nx), :] = tr[s, h, pl.ds(row, nx, stride=8), :]
            for k in range(2):
                row = edge(high, 8, 2) + k
                m_ys[s][pl.ds((12 + 2 * k + h) * nx, nx), :] = td[s, h, pl.ds(row, nx, stride=8), :]
            for msgs, right in ((m_cas, at.even), (m_cbs, at.odd)):
                for m, (p, q) in enumerate(CORNER1):
                    row = pick(high, 7 - q, q) + pick(right, nx - 1 - p, p) * 8
                    for probe in range(2):
                        msgs[s][pl.ds((m * 2 + probe) * 2 + h, 1), :] = tr[s, h, pl.ds(row + probe * nx * 8, 1), :]
                row = pick(high, 7, 0) + pick(right, nx - 1, 0) * 8
                msgs[s][pl.ds(12 + h, 1), :] = td[s, h, pl.ds(row, 1), :]
                msgs[s][pl.ds(14 + h, 1), :] = td[s, h, pl.ds(row, 1), :]
    for copy in copies[2 * n :]:
        copy.wait()
    for e, msg in enumerate((m_a, m_b)):
        v = permute_lanes(xr[e].reshape(6 * ny, 2 * LANES), split, 2)
        d = permute_lanes(xd[e].reshape(2 * ny, 2 * LANES), split, 2)
        for k in range(6):
            for h in range(2):
                msg[pl.ds((2 * k + h) * ny, ny), :] = v[k * ny : (k + 1) * ny, HALF[h]]
        for k in range(2):
            for h in range(2):
                msg[pl.ds((12 + 2 * k + h) * ny, ny), :] = d[k * ny : (k + 1) * ny, HALF[h]]


def open_kernel(sz, rhs, diag, bw, dw, cd, xs):
    nx, ny, wy, cy = sz.nx, sz.ny, sz.wy, sz.cy
    at = Place(sz)
    split = parity_matrix(False)
    zero8 = jnp.zeros((8, LANES), F32)
    zero_at = [pick(at.high_in[s], at.yoff + ny, at.yoff - 8) for s in range(sz.sides)]
    width = 4

    def body(i, _):
        for f in range(3):
            src = diag[pl.ds(width * i, width)] if f == 2 else rhs[f, pl.ds(width * i, width)]
            v = permute_lanes(src.reshape(width * ny, 2 * LANES), split, 2)
            if f == 2:
                v = v + 6.0
            for k in range(width):
                for h in range(2):
                    if f == 2:
                        ref, base = dw.at[h], (width * i + k + 2) * wy
                    else:
                        ref, base = bw.at[f, h], (width * i + k + 3) * wy
                    ref[rows(base + at.yoff, ny), :] = v[k * ny : (k + 1) * ny, HALF[h]]
                    for z in zero_at:
                        ref[rows(base + z, 8), :] = zero8
            if f == 2:
                for k in range(width // 2):
                    low, high = v[2 * k * ny : (2 * k + 1) * ny], v[(2 * k + 1) * ny : (2 * k + 2) * ny]
                    total = low + high
                    xs[k] = total[:, HALF[0]] + total[:, HALF[1]]
                    pair = xs[k, pl.ds(0, cy, stride=2), :] + xs[k, pl.ds(1, cy, stride=2), :]
                    cd[rows((i * (width // 2) + k) * cy, cy), :] = 0.5 * pair - 18.0
        return 0

    lax.fori_loop(0, nx // width, body, 0)


def pre_kernel(sz, *refs):
    n = sz.sides
    cd = refs[2]
    ys, xb, xa = sorted_messages(sz, ORDER1, refs[3 : 5 + n])
    cas, cbs = refs[5 + n : 5 + 2 * n], refs[5 + 2 * n : 5 + 3 * n]
    outs = refs[5 + 3 * n :]
    bw, dw, r_out, sol_out, coarse = outs[:5]
    m_ys, m_b, m_a = sorted_messages(sz, ORDER2, outs[5 : 7 + n])
    m_cas, m_cbs = outs[7 + n : 7 + 2 * n], outs[7 + 2 * n : 7 + 3 * n]
    r1, u2, u3, xs = outs[7 + 3 * n :]
    nx, ny, wy, cx, cy = sz.nx, sz.ny, sz.wy, sz.cx, sz.cy
    at = Place(sz)
    yoff = at.yoff
    masks = lane_masks(wy)

    zero8 = jnp.zeros((8, LANES), F32)
    zero_at = [pick(at.high_in[s], yoff + ny, yoff - 8) for s in range(n)]
    for msg, corners, to_right in ((xa, cas, at.even), (xb, cbs, at.odd)):
        b0 = jnp.where(to_right, nx + 3, 0)
        d0 = jnp.where(to_right, nx + 2, 0)
        for h in range(2):
            for k in range(3):
                for probe in range(2):
                    i = (probe * 3 + k) * 2 + h
                    bw[probe, h, rows((b0 + k) * wy + yoff, ny), :] = msg[pl.ds(i * ny, ny), :]
                    for z in zero_at:
                        bw[probe, h, rows((b0 + k) * wy + z, 8), :] = zero8
            for k in range(2):
                dw[h, rows((d0 + k) * wy + yoff, ny), :] = 6.0 + msg[pl.ds((12 + 2 * k + h) * ny, ny), :]
                for z in zero_at:
                    dw[h, rows((d0 + k) * wy + z, 8), :] = zero8
            for s in range(n):
                for m, (p, q) in enumerate(CORNER1):
                    row = pick(at.high_in[s], yoff + ny + q, yoff - 1 - q)
                    row = row + jnp.where(to_right, nx + 3 + p, 2 - p) * wy
                    for probe in range(2):
                        bw[probe, h, pl.ds(row, 1), :] = corners[s][pl.ds((m * 2 + probe) * 2 + h, 1), :]
                row = pick(at.high_in[s], yoff + ny, yoff - 1) + jnp.where(to_right, nx + 2, 1) * wy
                dw[h, pl.ds(row, 1), :] = 6.0 + corners[s][pl.ds(12 + h, 1), :]
    for s in range(n):
        br = pick(at.high_in[s], ny, -3) + yoff
        dr = pick(at.high_in[s], ny, -2) + yoff
        for h in range(2):
            for k in range(3):
                for probe in range(2):
                    i = (probe * 3 + k) * 2 + h
                    bw[probe, h, pl.ds(3 * wy + br + k, nx, stride=wy), :] = ys[s][pl.ds(i * nx, nx), :]
            for k in range(2):
                i = 12 + 2 * k + h
                dw[h, pl.ds(2 * wy + dr + k, nx, stride=wy), :] = 6.0 + ys[s][pl.ds(i * nx, nx), :]
    zero = jnp.zeros((wy, LANES), F32)
    for probe in range(2):
        for h in range(2):
            for i in (1, nx + 2):
                u2[probe, h, rows(i * wy, wy), :] = zero
                u3[probe, h, rows(i * wy, wy), :] = zero

    inside = row_mask(wy, at.fine)
    c0, (a1, c1), (a2, c2) = FINE[0][1], FINE[1], FINE[2]
    c1 = jnp.where(inside, c1, 0.0)
    c2 = jnp.where(inside, c2, 0.0)

    def step1(first, count):
        def use(probe, p, v, av):
            to = rows((p + 2) * wy, wy)
            for h in range(2):
                res = v[h] - c0 * av[h]
                r1[probe, h, to, :] = res
                u2[probe, h, to, :] = (a1 * c0) * v[h] + c1 * res

        sweep(bw, 3, dw, first, count, wy, masks, use)

    def step2(first, count):
        def use(probe, p, v, av):
            to = rows((p + 2) * wy, wy)
            for h in range(2):
                res = r1[probe, h, to, :] - av[h]
                r1[probe, h, to, :] = res
                u3[probe, h, to, :] = a2 * v[h] + c2 * res

        sweep(u2, 2, dw, first, count, wy, masks, use)

    mine = row_mask(wy, (yoff, yoff + ny))

    def steps3(i, _):
        totals = {}

        def use(probe, p, v, av):
            src = rows((p + 2) * wy, wy)
            to = rows(p * wy, wy)
            total = None
            for h in range(2):
                out = jnp.where(mine, r1[probe, h, src, :] - av[h], 0.0)
                r_out[probe, h, to, :] = out
                sol_out[probe, h, to, :] = (
                    c0 * bw[probe, h, rows((p + 3) * wy, wy), :] + u2[probe, h, src, :] + v[h]
                )
                total = out if total is None else total + out
            k = len(totals.setdefault(probe, []))
            totals[probe].append(total)
            if k % 2:
                xs[k // 2, probe] = totals[probe][k - 1] + total

        sweep(u3, 2, dw, 4 * i, 4, wy, masks, use)
        for k in range(2):
            for probe in range(2):
                pair = (
                    xs[k, probe, pl.ds(yoff, cy, stride=2), :] + xs[k, probe, pl.ds(yoff + 1, cy, stride=2), :]
                )
                coarse[probe, rows((2 * i + k) * cy, cy), :] = 0.5 * pair
        return 0

    @pl.when(at.has_l)
    def _():
        step1(-2, 2)

    @pl.when(at.has_r)
    def _():
        step1(nx, 2)

    looped(step1, nx)

    @pl.when(at.has_l)
    def _():
        step2(-1, 1)

    @pl.when(at.has_r)
    def _():
        step2(nx, 1)

    looped(step2, nx)
    lax.fori_loop(0, nx // 4, steps3, 0)

    field = [coarse.at[0], coarse.at[1], cd]
    depth = [REACH, REACH, REACH - 1]
    for msg, corners, right in ((m_a, m_cas, at.even), (m_b, m_cbs, at.odd)):
        for f in range(3):
            size = depth[f] * cy
            msg[pl.ds(f * REACH * cy, size), :] = field[f][rows(edge(right, cx, depth[f]) * cy, size), :]
        for s in range(n):
            for m, (f, p, q) in enumerate(CORNER2):
                row = pick(at.high_out[s], cy - 1 - q, q) + pick(right, cx - 1 - p, p) * cy
                corners[s][pl.ds(m, 1), :] = field[f][pl.ds(row, 1), :]
            row = pick(at.high_out[s], yoff + ny - 1, yoff) + pick(right, nx - 1, 0) * wy
            for probe in range(2):
                for h in range(2):
                    i = len(CORNER2) + probe * 2 + h
                    corners[s][pl.ds(i, 1), :] = r_out[probe, h, pl.ds(row, 1), :]
            corners[s][pl.ds(sz.c2 - 3, 3), :] = jnp.zeros((3, LANES), F32)
        for probe in range(2):
            for h in range(2):
                for k in range(2):
                    i = (probe * 2 + h) * 2 + k
                    row = (edge(right, nx, 2) + k) * wy + yoff
                    msg[pl.ds(sz.x2_base + i * ny, ny), :] = r_out[probe, h, rows(row, ny), :]
    for s in range(n):
        for f in range(3):
            for k in range(depth[f]):
                row = edge(at.high_out[s], cy, depth[f]) + k
                m_ys[s][pl.ds((f * REACH + k) * cx, cx), :] = field[f][pl.ds(row, cx, stride=cy), :]
        row = edge(at.high_out[s], ny, 2) + yoff
        for probe in range(2):
            for h in range(2):
                for k in range(2):
                    i = (probe * 2 + h) * 2 + k
                    m_ys[s][pl.ds(sz.y2_base + i * nx, nx), :] = r_out[probe, h, pl.ds(row + k, nx, stride=wy), :]


def post_kernel(sz, *refs):
    n = sz.sides
    agg, r_in, sol_in, dw, coarse, cd = refs[:6]
    ys, x_b, x_a = sorted_messages(sz, ORDER2, refs[6 : 8 + n])
    cas, cbs = refs[8 + n : 8 + 2 * n], refs[8 + 2 * n : 8 + 3 * n]
    out = refs[8 + 3 * n]
    cw, cu, cc, st_g, st_u, rh, re, r1, u2, acc, pj, ow, sem = refs[9 + 3 * n :]
    nx, ny, wy, cx, cy, wc = sz.nx, sz.ny, sz.wy, sz.cx, sz.cy, sz.wc
    at = Place(sz)
    yoff = at.yoff
    masks = lane_masks(wy)
    planes = cx + 2 * REACH

    zero8 = jnp.zeros((8, LANES), F32)
    zero_at = [pick(at.high_in[s], yoff + cy, yoff - 8) for s in range(n)]
    field = [coarse.at[0], coarse.at[1], cd]
    depth = [REACH, REACH, REACH - 1]
    for f in range(3):
        for p in range(planes):
            for z in zero_at:
                cw[f, rows(p * wc + z, 8), :] = zero8
        for x in range(cx):
            cw[f, rows((x + REACH) * wc + yoff, cy), :] = field[f][rows(x * cy, cy), :]
        for s in range(n):
            for k in range(depth[f]):
                row = pick(at.high_in[s], yoff + cy, yoff - depth[f]) + k
                cw[f, pl.ds(REACH * wc + row, cx, stride=wc), :] = ys[s][rows((f * REACH + k) * cx, cx), :]
        for msg, to_right in ((x_a, at.even), (x_b, at.odd)):
            first = jnp.where(to_right, REACH + cx, REACH - depth[f])
            for k in range(depth[f]):
                cw[f, rows((first + k) * wc + yoff, cy), :] = msg[rows((f * REACH + k) * cy, cy), :]
    for corners, to_right in ((cas, at.even), (cbs, at.odd)):
        for s in range(n):
            for m, (f, p, q) in enumerate(CORNER2):
                row = pick(at.high_in[s], yoff + cy + q, yoff - 1 - q)
                row = row + jnp.where(to_right, REACH + cx + p, REACH - 1 - p) * wc
                cw[f, pl.ds(row, 1), :] = corners[s][pl.ds(m, 1), :]

    cmasks = lane_masks(wc)
    inside = row_mask(wc, at.crs)
    i = at.i
    here = agg[i]
    link_l = (at.has_l & (agg[jnp.maximum(i - 1, 0)] == here)).astype(F32)
    link_r = (at.has_r & (agg[jnp.minimum(i + 1, sz.n_gx - 1)] == here)).astype(F32)
    for p in range(planes):
        to = pl.ds(p * wc, wc)
        for probe in range(2):
            u = jnp.where(inside, COARSE[0][1], 0.0) * cw[probe, to, :]
            cu[0, probe, to, :] = u
            cc[probe, to, :] = u
    for k in range(COARSE_DEG - 1):
        a, c = COARSE[k + 1]
        c = jnp.where(inside, c, 0.0)
        old, new = k % 2, 1 - k % 2
        for p in range(1 + k, planes - 1 - k):
            to = pl.ds(p * wc, wc)
            for probe in range(2):
                u = cu[old, probe, to, :]
                before = cu[old, probe, pl.ds((p - 1) * wc, wc), :]
                after = cu[old, probe, pl.ds((p + 1) * wc, wc), :]
                if p == REACH:
                    before = before * link_l
                if p == REACH - 1:
                    after = after * link_l
                if p == REACH + cx:
                    before = before * link_r
                if p == REACH + cx - 1:
                    after = after * link_r
                near = ((before + after) + y_sum(u)) + (below(u, cmasks) + above(u, cmasks))
                res = cw[probe, to, :] - (cw[2, to, :] * u - near)
                u = a * u + c * res
                if k + 2 < COARSE_DEG:
                    cw[probe, to, :] = res
                    cu[new, probe, to, :] = u
                cc[probe, to, :] = cc[probe, to, :] + u

    for msg, corners, to_right in ((x_a, cas, at.even), (x_b, cbs, at.odd)):
        for probe in range(2):
            for h in range(2):
                for k in range(2):
                    i = (probe * 2 + h) * 2 + k
                    base = (jnp.where(to_right, 2, 0) + k) * wy
                    rh[probe, h, rows(base + yoff, ny), :] = msg[pl.ds(sz.x2_base + i * ny, ny), :]
                    for s in range(n):
                        zero_row = pick(at.high_in[s], yoff + ny, yoff - 8)
                        rh[probe, h, rows(base + zero_row, 8), :] = zero8
                for s in range(n):
                    row = pick(at.high_in[s], yoff + ny, yoff - 1) + jnp.where(to_right, 2, 1) * wy
                    i = len(CORNER2) + probe * 2 + h
                    rh[probe, h, pl.ds(row, 1), :] = corners[s][pl.ds(i, 1), :]

    c0, (a1, c1), (a2, c2) = FINE[0][1], FINE[1], FINE[2]
    valid = row_mask(wy, at.valid)

    def spread(q, r_ref, r_plane, own, slot=0):
        for probe in range(2):
            u = cc[probe, rows((q + REACH) * wc, wc), :]
            sides = [cc[probe, rows((q + REACH - 1 + 2 * k) * wc, wc), :] for k in range(2)]
            u3 = 3.0 * u
            shifted = [pltpu.roll(u, 1, 0), pltpu.roll(u, wc - 1, 0)]
            for row in range(2):
                st_u[slot, probe, pl.ds(row, wc, stride=2), :] = u
            for h in range(2):
                g = u3 + (above(u, cmasks) if h else below(u, cmasks))
                for k in range(2):
                    for row in range(2):
                        st_g[slot, probe, h, k, pl.ds(row, wc, stride=2), :] = (g + sides[k]) + shifted[row]
        for k in range(2):
            to = rows((2 * q + k + 2) * wy, wy)
            for h in range(2):
                d = dw[h, to, :]
                for probe in range(2):
                    u = st_u[slot, probe, rows(yoff, wy), :]
                    old = r_ref[probe, h, rows((r_plane + k) * wy, wy), :]
                    res = (old - d * u) + st_g[slot, probe, h, k, rows(yoff, wy), :]
                    res = jnp.where(valid, res, 0.0)
                    re[probe, h, to, :] = res
                    if own:
                        mine = rows((2 * q + k) * wy, wy)
                        acc[probe, h, mine, :] = (sol_in[probe, h, mine, :] + u) + c0 * res

    def own_planes(i, _):
        for k in range(4):
            spread(4 * i + k, r_in, 2 * (4 * i + k), True, k)
        return 0

    lax.fori_loop(0, cx // 4, own_planes, 0)
    zero = jnp.zeros((wy, LANES), F32)
    for has, q, first in ((at.has_l, -1, 0), (at.has_r, cx, 2)):

        @pl.when(has)
        def _():
            spread(q, rh, first, False)

        @pl.when(jnp.logical_not(has))
        def _():
            for probe in range(2):
                for h in range(2):
                    for k in range(2):
                        re[probe, h, rows((2 * q + 2 + k) * wy, wy), :] = zero
                        u2[probe, h, rows((2 * q + 2 + k) * wy, wy), :] = zero

    for s in range(n):
        row = pick(at.high_in[s], yoff + ny, yoff - 2)
        for probe in range(2):
            for h in range(2):
                for k in range(2):
                    i = (probe * 2 + h) * 2 + k
                    to = pl.ds(2 * wy + row + k, nx, stride=wy)
                    re[probe, h, to, :] = re[probe, h, to, :] + ys[s][pl.ds(sz.y2_base + i * nx, nx), :]

    c1 = jnp.where(row_mask(wy, at.fine), c1, 0.0)

    def step1(first, count):
        def use(probe, p, v, av):
            to = rows((p + 2) * wy, wy)
            for h in range(2):
                res = v[h] - c0 * av[h]
                r1[probe, h, to, :] = res
                u2[probe, h, to, :] = (a1 * c0) * v[h] + c1 * res

        sweep(re, 2, dw, first, count, wy, masks, use)

    join = parity_matrix(True)
    width = 4

    def close(i):
        slot = i % 2
        planes = [(probe, k) for probe in range(2) for k in range(width)]
        own = [
            jnp.concatenate([pj[slot, probe, h, rows(k * wy + yoff, ny), :] for h in range(2)], axis=1)
            for probe, k in planes
        ]
        joined = permute_lanes(jnp.concatenate(own, axis=0), join, 2)
        for m, (probe, k) in enumerate(planes):
            ow[probe, width * i + k] = joined[m * ny : (m + 1) * ny]

    def send(i):
        part = pl.ds(width * i, width)
        return pltpu.make_async_copy(ow.at[:, part], out.at[:, part], sem.at[i])

    def step2(i):
        slot = i % 2

        def use(probe, p, v, av):
            to = rows((p + 2) * wy, wy)
            for h in range(2):
                res = r1[probe, h, to, :] - av[h]
                pj[slot, probe, h, rows((p - width * i) * wy, wy), :] = acc[probe, h, rows(p * wy, wy), :] + (
                    (1.0 + a2) * v[h] + c2 * res
                )

        sweep(u2, 2, dw, width * i, width, wy, masks, use)

    def steps2(i, _):
        close(i - 1)
        step2(i)
        send(i - 1).start()
        return 0

    @pl.when(at.has_l)
    def _():
        step1(-1, 1)

    @pl.when(at.has_r)
    def _():
        step1(nx, 1)

    looped(step1, nx)
    step2(0)
    lax.fori_loop(1, nx // width, steps2, 0)
    close(nx // width - 1)
    send(nx // width - 1).start()
    for i in range(nx // width):
        send(i).wait()


def on_device(n_gx, n_gy, right_side, diagonal, aggregates):
    nx, ny, nz = right_side.shape[1:]
    sz = Sizes(nx, ny, nz, n_gx, n_gy)
    n, wy, wc, cx = sz.sides, sz.wy, sz.wc, sz.cx

    pairs_a = [(k, k ^ 1) for k in range(n_gx)]
    pairs_b = [(k, k + 1) for k in range(1, n_gx - 1, 2)] + [(k + 1, k) for k in range(1, n_gx - 1, 2)]
    along = [[(0, 1), (1, 0)]] if sz.two else [
        [(k, k - 1) for k in range(1, n_gy)],
        [(k, k + 1) for k in range(n_gy - 1)],
    ]

    def both(pairs, perm):
        return [(a * n_gy + c, b * n_gy + d) for a, b in pairs for c, d in perm]

    perms = {"a": [("gx", pairs_a)], "b": [("gx", pairs_b)], "y": [("gy", perm) for perm in along]}
    corner_perms = [(("gx", "gy"), both(pairs, perm)) for pairs in (pairs_a, pairs_b) for perm in along]

    def exchange(order, messages):
        lines = [line for name in order for line in perms[name]] + corner_perms
        return [lax.ppermute(m, *line) for m, line in zip(messages, lines)]

    smem = pl.BlockSpec(memory_space=pltpu.SMEM)
    vmem = pl.BlockSpec(memory_space=pltpu.VMEM)
    hbm = pl.BlockSpec(memory_space=pltpu.HBM)
    params = pltpu.CompilerParams(vmem_limit_bytes=24 << 20)

    def shape(*dims):
        return jax.ShapeDtypeStruct(dims, F32)

    def messages(order, x, y, c):
        sizes = [y if name == "y" else x for name in order for _ in perms[name]]
        return [shape(size, LANES) for size in sizes + [c] * (2 * n)]

    packed = pl.pallas_call(
        functools.partial(pack_kernel, sz),
        in_specs=[hbm] * 2,
        out_specs=[vmem] * (2 + 3 * n),
        out_shape=messages(ORDER1, sz.x1, sz.y1, sz.c1),
        scratch_shapes=[
            pltpu.VMEM((2, 2, 3, ny, nz), F32),
            pltpu.VMEM((2, 2, ny, nz), F32),
            pltpu.VMEM((n, 2, nx, 8, nz), F32),
            pltpu.VMEM((n, nx, 8, nz), F32),
            pltpu.VMEM((n, 2, 2 * nx * 8, LANES), F32),
            pltpu.VMEM((n, 2, nx * 8, LANES), F32),
            pltpu.SemaphoreType.DMA((2 * n + 4,)),
        ],
        compiler_params=pltpu.CompilerParams(vmem_limit_bytes=120 << 19),
        name="pack_kernel",
    )(right_side, diagonal)
    halos = exchange(ORDER1, packed)
    bw, dw, cd = pl.pallas_call(
        functools.partial(open_kernel, sz),
        in_specs=[vmem] * 2,
        out_specs=[vmem] * 3,
        out_shape=[shape(*sz.bw), shape(*sz.dw), shape(sz.coarse, LANES)],
        scratch_shapes=[
            pltpu.VMEM((2, ny, LANES), F32),
        ],
        compiler_params=params,
        name="open_kernel",
    )(right_side, diagonal)
    results = pl.pallas_call(
        functools.partial(pre_kernel, sz),
        in_specs=[vmem] * (5 + 3 * n),
        out_specs=[vmem] * (7 + 3 * n),
        out_shape=[shape(*sz.bw), shape(*sz.dw), shape(*sz.brick), shape(*sz.brick), shape(2, sz.coarse, LANES)]
        + messages(ORDER2, sz.x2, sz.y2, sz.c2),
        scratch_shapes=[pltpu.VMEM((2, 2, (nx + 4) * wy, LANES), F32)] * 3 + [pltpu.VMEM((2, 2, wy, LANES), F32)],
        input_output_aliases={0: 0, 1: 1},
        compiler_params=params,
        name="pre_smooth",
    )(bw, dw, cd, *halos)
    dw, r_own, sol, coarse = results[1:5]
    halos = exchange(ORDER2, results[5:])
    planes = cx + 2 * REACH
    return pl.pallas_call(
        functools.partial(post_kernel, sz),
        in_specs=[smem] + [vmem] * (7 + 3 * n),
        out_specs=hbm,
        out_shape=shape(2, nx, ny, nz),
        scratch_shapes=[
            pltpu.VMEM((3, planes * wc, LANES), F32),
            pltpu.VMEM((2, 2, planes * wc, LANES), F32),
            pltpu.VMEM((2, planes * wc, LANES), F32),
            pltpu.VMEM((4, 2, 2, 2, 2 * wc, LANES), F32),
            pltpu.VMEM((4, 2, 2 * wc, LANES), F32),
            pltpu.VMEM((2, 2, 4 * wy, LANES), F32),
        ]
        + [pltpu.VMEM((2, 2, (nx + 4) * wy, LANES), F32)] * 3
        + [
            pltpu.VMEM(sz.brick, F32),
            pltpu.VMEM((2, 2, 2, 4 * wy, LANES), F32),
            pltpu.VMEM((2, nx, ny, nz), F32),
            pltpu.SemaphoreType.DMA((nx // 4,)),
        ],
        compiler_params=params,
        name="correct_and_smooth",
    )(aggregates, r_own, sol, dw, coarse, cd, *halos)


def solution(mesh):
    return jax.shard_map(
        functools.partial(on_device, mesh.shape["gx"], mesh.shape["gy"]),
        mesh=mesh,
        in_specs=(P(None, "gx", "gy", None), P("gx", "gy", None), P()),
        out_specs=P(None, "gx", "gy", None),
        check_vma=False,
    )
```

```python
import functools

import jax
import jax.numpy as jnp
from jax import lax
from jax.experimental import pallas as pl
from jax.experimental.pallas import tpu as pltpu
from jax.sharding import PartitionSpec as P

DEGREE = 3
COARSE_DEG = 6


FINE_LOWER = 3.0
FINE_UPPER = 12.4
COARSE_LOWER = 0.5
COARSE_UPPER = 13.4

LANES = 128
REACH = 7
F32 = jnp.float32


def cheb_pairs(lower, upper, count):
    middle = (upper + lower) / 2.0
    halfwidth = (upper - lower) / 2.0
    ratio_mid = middle / halfwidth
    rho_old = 1.0 / ratio_mid
    result = [(0.0, 1.0 / middle)]
    for repeat in range(count - 1):
        rho_new = 1.0 / (2.0 * ratio_mid - rho_old)
        result.append((rho_new * rho_old, 2.0 * rho_new / halfwidth))
        rho_old = rho_new
    return result


FINE = cheb_pairs(FINE_LOWER, FINE_UPPER, DEGREE)
COARSE = cheb_pairs(COARSE_LOWER, COARSE_UPPER, COARSE_DEG)


class Sizes:
    def __init__(self, nx, ny, nz, n_gx, n_gy):
        assert nz == 2 * LANES and n_gy >= 2 and ny % 16 == 0 and nx % 4 == 0
        self.nx, self.ny, self.nz = nx, ny, nz
        self.n_gx, self.n_gy = n_gx, n_gy
        self.two = n_gy == 2
        self.sides = 1 if self.two else 2
        self.wy = ny + 8 * self.sides
        self.cx, self.cy = nx // 2, ny // 2
        self.wc = self.cy + 8 * self.sides
        self.bw = (2, 2, (nx + 6) * self.wy, LANES)
        self.dw = (2, (nx + 4) * self.wy, LANES)
        self.brick = (2, 2, nx * self.wy, LANES)
        self.coarse = self.cx * self.cy
        self.x1 = 8 * 2 * ny
        self.y1 = 8 * 2 * nx
        self.c1 = 16
        self.x2_base = (3 * REACH - 1) * self.cy
        self.x2 = self.x2_base + 8 * ny
        self.y2_base = (3 * REACH - 1) * self.cx
        self.y2 = self.y2_base + 8 * nx
        self.c2 = 64


class Place:
    def __init__(self, sz):
        i, j = lax.axis_index("gx"), lax.axis_index("gy")
        self.i = i
        self.even = i % 2 == 0
        self.odd = i % 2 != 0
        self.has_l, self.has_r = i > 0, i < sz.n_gx - 1
        if sz.two:
            self.yoff = pl.multiple_of(8 * j, 8)
            self.high_in = [j == 0]
            self.high_out = [j == 0]
            self.fine = (j, sz.wy - 1 + j)
            self.crs = (j, sz.wc - 1 + j)
            self.valid = (6 * j, sz.ny + 2 + 6 * j)
        else:
            first, last = j == 0, j == sz.n_gy - 1
            self.yoff = 8
            self.high_in = [True, False]
            self.high_out = [False, True]
            self.fine = (jnp.where(first, 8, 1), jnp.where(last, sz.ny + 8, sz.wy - 1))
            self.crs = (jnp.where(first, 8, 1), jnp.where(last, sz.cy + 8, sz.wc - 1))
            self.valid = (jnp.where(first, 8, 6), jnp.where(last, sz.ny + 8, sz.ny + 10))


def pick(condition, yes, no):
    if isinstance(condition, bool):
        return yes if condition else no
    return jnp.where(condition, yes, no)


def edge(high, size, count):
    return pick(high, size - count, 0)


def rows(start, size):
    return pl.ds(pl.multiple_of(start, 8), size)


def lane_masks(height):
    lane = lax.broadcasted_iota(jnp.int32, (height, LANES), 1)
    return lane == 0, lane == LANES - 1


def row_mask(height, span):
    row = lax.broadcasted_iota(jnp.int32, (height, LANES), 0)
    return (row >= span[0]) & (row < span[1])


def y_sum(v):
    return pltpu.roll(v, 1, 0) + pltpu.roll(v, v.shape[0] - 1, 0)


def below(v, masks):
    return jnp.where(masks[0], 0.0, pltpu.roll(v, 1, 1))


def above(v, masks):
    return jnp.where(masks[1], 0.0, pltpu.roll(v, LANES - 1, 1))


def z_sum(even, odd, masks):
    return odd + below(odd, masks), even + above(even, masks)


def parity_matrix(transposed):
    row = lax.broadcasted_iota(jnp.int32, (2 * LANES, 2 * LANES), 0)
    col = lax.broadcasted_iota(jnp.int32, (2 * LANES, 2 * LANES), 1)
    if transposed:
        row, col = col, row
    return (row == 2 * (col % LANES) + col // LANES).astype(jnp.bfloat16)


def permute_lanes(v, matrix, terms):
    total = None
    for k in range(terms):
        part = v.astype(jnp.bfloat16)
        if k + 1 < terms:
            v = v - part.astype(F32)
        dot = jnp.dot(part, matrix, preferred_element_type=F32)
        total = dot if total is None else total + dot
    return total


def sweep(ref, shift, dw, first, count, wy, masks, use):
    for probe in range(2):

        def load(plane):
            return [ref[probe, h, rows((plane + shift) * wy, wy), :] for h in range(2)]

        before, now = load(first - 1), load(first)
        for k in range(count):
            plane = first + k
            at = plane + shift
            after = load(plane + 1)
            z = z_sum(now[0], now[1], masks)
            res = []
            for h in range(2):
                y = pltpu.roll(now[h], 1, 0) + ref[probe, h, pl.ds(at * wy + 1, wy), :]
                d = dw[h, rows((plane + 2) * wy, wy), :]
                res.append(d * now[h] - (((before[h] + after[h]) + y) + z[h]))
            use(probe, plane, now, res)
            before, now = now, after


def looped(step, count, width=4):
    def body(i, _):
        step(width * i, width)
        return 0

    lax.fori_loop(0, count // width, body, 0)


ORDER1 = "aby"
ORDER2 = "yba"


def sorted_messages(sz, order, refs):
    found, k = {}, 0
    for name in order:
        count = sz.sides if name == "y" else 1
        found[name] = refs[k : k + count]
        k += count
    return found["y"], found["b"][0], found["a"][0]


HALF = [slice(0, LANES), slice(LANES, 2 * LANES)]
CORNER1 = [(0, 0), (0, 1), (1, 0)]
CORNER2 = [(f, p, q) for f in range(3) for p in range(6) for q in range(6 - p - f // 2)]


def pack_kernel(sz, *refs):
    n = sz.sides
    rhs, diag = refs[:2]
    m_ys, m_b, m_a = sorted_messages(sz, ORDER1, refs[2 : 4 + n])
    m_cas, m_cbs = refs[4 + n : 4 + 2 * n], refs[4 + 2 * n : 4 + 3 * n]
    xr, xd, yr, yd, tr, td, sem = refs[4 + 3 * n :]
    nx, ny = sz.nx, sz.ny
    at = Place(sz)
    copies = []

    def fetch(src, dst):
        copy = pltpu.make_async_copy(src, dst, sem.at[len(copies)])
        copy.start()
        copies.append(copy)

    for s in range(n):
        slab = rows(edge(at.high_out[s], ny, 8), 8)
        fetch(rhs.at[:, :, slab, :], yr.at[s])
        fetch(diag.at[:, slab, :], yd.at[s])
    for e, right in enumerate((at.even, at.odd)):
        fetch(rhs.at[:, pl.ds(edge(right, nx, 3), 3)], xr.at[e])
        fetch(diag.at[pl.ds(edge(right, nx, 2), 2)], xd.at[e])
    split = parity_matrix(False)
    for copy in copies[: 2 * n]:
        copy.wait()
    for s in range(n):
        v = permute_lanes(yr[s].reshape(2 * nx * 8, 2 * LANES), split, 2)
        d = permute_lanes(yd[s].reshape(nx * 8, 2 * LANES), split, 2)
        for h in range(2):
            tr[s, h] = v[:, HALF[h]]
            td[s, h] = d[:, HALF[h]]
        high = at.high_out[s]
        for h in range(2):
            for k in range(3):
                for probe in range(2):
                    i = (probe * 3 + k) * 2 + h
                    row = edge(high, 8, 3) + k + probe * nx * 8
                    m_ys[s][pl.ds(i * nx, nx), :] = tr[s, h, pl.ds(row, nx, stride=8), :]
            for k in range(2):
                row = edge(high, 8, 2) + k
                m_ys[s][pl.ds((12 + 2 * k + h) * nx, nx), :] = td[s, h, pl.ds(row, nx, stride=8), :]
            for msgs, right in ((m_cas, at.even), (m_cbs, at.odd)):
                for m, (p, q) in enumerate(CORNER1):
                    row = pick(high, 7 - q, q) + pick(right, nx - 1 - p, p) * 8
                    for probe in range(2):
                        msgs[s][pl.ds((m * 2 + probe) * 2 + h, 1), :] = tr[s, h, pl.ds(row + probe * nx * 8, 1), :]
                row = pick(high, 7, 0) + pick(right, nx - 1, 0) * 8
                msgs[s][pl.ds(12 + h, 1), :] = td[s, h, pl.ds(row, 1), :]
                msgs[s][pl.ds(14 + h, 1), :] = td[s, h, pl.ds(row, 1), :]
    for copy in copies[2 * n :]:
        copy.wait()
    for e, msg in enumerate((m_a, m_b)):
        v = permute_lanes(xr[e].reshape(6 * ny, 2 * LANES), split, 2)
        d = permute_lanes(xd[e].reshape(2 * ny, 2 * LANES), split, 2)
        for k in range(6):
            for h in range(2):
                msg[pl.ds((2 * k + h) * ny, ny), :] = v[k * ny : (k + 1) * ny, HALF[h]]
        for k in range(2):
            for h in range(2):
                msg[pl.ds((12 + 2 * k + h) * ny, ny), :] = d[k * ny : (k + 1) * ny, HALF[h]]


def open_kernel(sz, rhs, diag, bw, dw, cd, xs):
    nx, ny, wy, cy = sz.nx, sz.ny, sz.wy, sz.cy
    at = Place(sz)
    split = parity_matrix(False)
    zero8 = jnp.zeros((8, LANES), F32)
    zero_at = [pick(at.high_in[s], at.yoff + ny, at.yoff - 8) for s in range(sz.sides)]
    width = 4

    def body(i, _):
        for f in range(3):
            src = diag[pl.ds(width * i, width)] if f == 2 else rhs[f, pl.ds(width * i, width)]
            v = permute_lanes(src.reshape(width * ny, 2 * LANES), split, 2)
            if f == 2:
                v = v + 6.0
            for k in range(width):
                for h in range(2):
                    if f == 2:
                        ref, base = dw.at[h], (width * i + k + 2) * wy
                    else:
                        ref, base = bw.at[f, h], (width * i + k + 3) * wy
                    ref[rows(base + at.yoff, ny), :] = v[k * ny : (k + 1) * ny, HALF[h]]
                    for z in zero_at:
                        ref[rows(base + z, 8), :] = zero8
            if f == 2:
                for k in range(width // 2):
                    low, high = v[2 * k * ny : (2 * k + 1) * ny], v[(2 * k + 1) * ny : (2 * k + 2) * ny]
                    total = low + high
                    xs[k] = total[:, HALF[0]] + total[:, HALF[1]]
                    pair = xs[k, pl.ds(0, cy, stride=2), :] + xs[k, pl.ds(1, cy, stride=2), :]
                    cd[rows((i * (width // 2) + k) * cy, cy), :] = 0.5 * pair - 18.0
        return 0

    lax.fori_loop(0, nx // width, body, 0)


def pre_kernel(sz, *refs):
    n = sz.sides
    cd = refs[2]
    ys, xb, xa = sorted_messages(sz, ORDER1, refs[3 : 5 + n])
    cas, cbs = refs[5 + n : 5 + 2 * n], refs[5 + 2 * n : 5 + 3 * n]
    outs = refs[5 + 3 * n :]
    bw, dw, r_out, sol_out, coarse = outs[:5]
    m_ys, m_b, m_a = sorted_messages(sz, ORDER2, outs[5 : 7 + n])
    m_cas, m_cbs = outs[7 + n : 7 + 2 * n], outs[7 + 2 * n : 7 + 3 * n]
    r1, u2, u3, xs = outs[7 + 3 * n :]
    nx, ny, wy, cx, cy = sz.nx, sz.ny, sz.wy, sz.cx, sz.cy
    at = Place(sz)
    yoff = at.yoff
    masks = lane_masks(wy)

    zero8 = jnp.zeros((8, LANES), F32)
    zero_at = [pick(at.high_in[s], yoff + ny, yoff - 8) for s in range(n)]
    for msg, corners, to_right in ((xa, cas, at.even), (xb, cbs, at.odd)):
        b0 = jnp.where(to_right, nx + 3, 0)
        d0 = jnp.where(to_right, nx + 2, 0)
        for h in range(2):
            for k in range(3):
                for probe in range(2):
                    i = (probe * 3 + k) * 2 + h
                    bw[probe, h, rows((b0 + k) * wy + yoff, ny), :] = msg[pl.ds(i * ny, ny), :]
                    for z in zero_at:
                        bw[probe, h, rows((b0 + k) * wy + z, 8), :] = zero8
            for k in range(2):
                dw[h, rows((d0 + k) * wy + yoff, ny), :] = 6.0 + msg[pl.ds((12 + 2 * k + h) * ny, ny), :]
                for z in zero_at:
                    dw[h, rows((d0 + k) * wy + z, 8), :] = zero8
            for s in range(n):
                for m, (p, q) in enumerate(CORNER1):
                    row = pick(at.high_in[s], yoff + ny + q, yoff - 1 - q)
                    row = row + jnp.where(to_right, nx + 3 + p, 2 - p) * wy
                    for probe in range(2):
                        bw[probe, h, pl.ds(row, 1), :] = corners[s][pl.ds((m * 2 + probe) * 2 + h, 1), :]
                row = pick(at.high_in[s], yoff + ny, yoff - 1) + jnp.where(to_right, nx + 2, 1) * wy
                dw[h, pl.ds(row, 1), :] = 6.0 + corners[s][pl.ds(12 + h, 1), :]
    for s in range(n):
        br = pick(at.high_in[s], ny, -3) + yoff
        dr = pick(at.high_in[s], ny, -2) + yoff
        for h in range(2):
            for k in range(3):
                for probe in range(2):
                    i = (probe * 3 + k) * 2 + h
                    bw[probe, h, pl.ds(3 * wy + br + k, nx, stride=wy), :] = ys[s][pl.ds(i * nx, nx), :]
            for k in range(2):
                i = 12 + 2 * k + h
                dw[h, pl.ds(2 * wy + dr + k, nx, stride=wy), :] = 6.0 + ys[s][pl.ds(i * nx, nx), :]
    zero = jnp.zeros((wy, LANES), F32)
    for probe in range(2):
        for h in range(2):
            for i in (1, nx + 2):
                u2[probe, h, rows(i * wy, wy), :] = zero
                u3[probe, h, rows(i * wy, wy), :] = zero

    inside = row_mask(wy, at.fine)
    c0, (a1, c1), (a2, c2) = FINE[0][1], FINE[1], FINE[2]
    c1 = jnp.where(inside, c1, 0.0)
    c2 = jnp.where(inside, c2, 0.0)

    def step1(first, count):
        def use(probe, p, v, av):
            to = rows((p + 2) * wy, wy)
            for h in range(2):
                res = v[h] - c0 * av[h]
                r1[probe, h, to, :] = res
                u2[probe, h, to, :] = (a1 * c0) * v[h] + c1 * res

        sweep(bw, 3, dw, first, count, wy, masks, use)

    def step2(first, count):
        def use(probe, p, v, av):
            to = rows((p + 2) * wy, wy)
            for h in range(2):
                res = r1[probe, h, to, :] - av[h]
                r1[probe, h, to, :] = res
                u3[probe, h, to, :] = a2 * v[h] + c2 * res

        sweep(u2, 2, dw, first, count, wy, masks, use)

    mine = row_mask(wy, (yoff, yoff + ny))

    def steps3(i, _):
        totals = {}

        def use(probe, p, v, av):
            src = rows((p + 2) * wy, wy)
            to = rows(p * wy, wy)
            total = None
            for h in range(2):
                out = jnp.where(mine, r1[probe, h, src, :] - av[h], 0.0)
                r_out[probe, h, to, :] = out
                sol_out[probe, h, to, :] = (
                    c0 * bw[probe, h, rows((p + 3) * wy, wy), :] + u2[probe, h, src, :] + v[h]
                )
                total = out if total is None else total + out
            k = len(totals.setdefault(probe, []))
            totals[probe].append(total)
            if k % 2:
                xs[k // 2, probe] = totals[probe][k - 1] + total

        sweep(u3, 2, dw, 4 * i, 4, wy, masks, use)
        for k in range(2):
            for probe in range(2):
                pair = (
                    xs[k, probe, pl.ds(yoff, cy, stride=2), :] + xs[k, probe, pl.ds(yoff + 1, cy, stride=2), :]
                )
                coarse[probe, rows((2 * i + k) * cy, cy), :] = 0.5 * pair
        return 0

    @pl.when(at.has_l)
    def _():
        step1(-2, 2)

    @pl.when(at.has_r)
    def _():
        step1(nx, 2)

    looped(step1, nx)

    @pl.when(at.has_l)
    def _():
        step2(-1, 1)

    @pl.when(at.has_r)
    def _():
        step2(nx, 1)

    looped(step2, nx)
    lax.fori_loop(0, nx // 4, steps3, 0)

    field = [coarse.at[0], coarse.at[1], cd]
    depth = [REACH, REACH, REACH - 1]
    for msg, corners, right in ((m_a, m_cas, at.even), (m_b, m_cbs, at.odd)):
        for f in range(3):
            size = depth[f] * cy
            msg[pl.ds(f * REACH * cy, size), :] = field[f][rows(edge(right, cx, depth[f]) * cy, size), :]
        for s in range(n):
            for m, (f, p, q) in enumerate(CORNER2):
                row = pick(at.high_out[s], cy - 1 - q, q) + pick(right, cx - 1 - p, p) * cy
                corners[s][pl.ds(m, 1), :] = field[f][pl.ds(row, 1), :]
            row = pick(at.high_out[s], yoff + ny - 1, yoff) + pick(right, nx - 1, 0) * wy
            for probe in range(2):
                for h in range(2):
                    i = len(CORNER2) + probe * 2 + h
                    corners[s][pl.ds(i, 1), :] = r_out[probe, h, pl.ds(row, 1), :]
            corners[s][pl.ds(sz.c2 - 3, 3), :] = jnp.zeros((3, LANES), F32)
        for probe in range(2):
            for h in range(2):
                for k in range(2):
                    i = (probe * 2 + h) * 2 + k
                    row = (edge(right, nx, 2) + k) * wy + yoff
                    msg[pl.ds(sz.x2_base + i * ny, ny), :] = r_out[probe, h, rows(row, ny), :]
    for s in range(n):
        for f in range(3):
            for k in range(depth[f]):
                row = edge(at.high_out[s], cy, depth[f]) + k
                m_ys[s][pl.ds((f * REACH + k) * cx, cx), :] = field[f][pl.ds(row, cx, stride=cy), :]
        row = edge(at.high_out[s], ny, 2) + yoff
        for probe in range(2):
            for h in range(2):
                for k in range(2):
                    i = (probe * 2 + h) * 2 + k
                    m_ys[s][pl.ds(sz.y2_base + i * nx, nx), :] = r_out[probe, h, pl.ds(row + k, nx, stride=wy), :]


def post_kernel(sz, *refs):
    n = sz.sides
    agg, r_in, sol_in, dw, coarse, cd = refs[:6]
    ys, x_b, x_a = sorted_messages(sz, ORDER2, refs[6 : 8 + n])
    cas, cbs = refs[8 + n : 8 + 2 * n], refs[8 + 2 * n : 8 + 3 * n]
    out = refs[8 + 3 * n]
    cw, cu, cc, st_g, st_u, rh, re, r1, u2, acc, pj, ow, sem = refs[9 + 3 * n :]
    nx, ny, wy, cx, cy, wc = sz.nx, sz.ny, sz.wy, sz.cx, sz.cy, sz.wc
    at = Place(sz)
    yoff = at.yoff
    masks = lane_masks(wy)
    planes = cx + 2 * REACH

    zero8 = jnp.zeros((8, LANES), F32)
    zero_at = [pick(at.high_in[s], yoff + cy, yoff - 8) for s in range(n)]
    field = [coarse.at[0], coarse.at[1], cd]
    depth = [REACH, REACH, REACH - 1]
    for f in range(3):
        for p in range(planes):
            for z in zero_at:
                cw[f, rows(p * wc + z, 8), :] = zero8
        for x in range(cx):
            cw[f, rows((x + REACH) * wc + yoff, cy), :] = field[f][rows(x * cy, cy), :]
        for s in range(n):
            for k in range(depth[f]):
                row = pick(at.high_in[s], yoff + cy, yoff - depth[f]) + k
                cw[f, pl.ds(REACH * wc + row, cx, stride=wc), :] = ys[s][rows((f * REACH + k) * cx, cx), :]
        for msg, to_right in ((x_a, at.even), (x_b, at.odd)):
            first = jnp.where(to_right, REACH + cx, REACH - depth[f])
            for k in range(depth[f]):
                cw[f, rows((first + k) * wc + yoff, cy), :] = msg[rows((f * REACH + k) * cy, cy), :]
    for corners, to_right in ((cas, at.even), (cbs, at.odd)):
        for s in range(n):
            for m, (f, p, q) in enumerate(CORNER2):
                row = pick(at.high_in[s], yoff + cy + q, yoff - 1 - q)
                row = row + jnp.where(to_right, REACH + cx + p, REACH - 1 - p) * wc
                cw[f, pl.ds(row, 1), :] = corners[s][pl.ds(m, 1), :]

    cmasks = lane_masks(wc)
    inside = row_mask(wc, at.crs)
    i = at.i
    here = agg[i]
    link_l = (at.has_l & (agg[jnp.maximum(i - 1, 0)] == here)).astype(F32)
    link_r = (at.has_r & (agg[jnp.minimum(i + 1, sz.n_gx - 1)] == here)).astype(F32)
    for p in range(planes):
        to = pl.ds(p * wc, wc)
        for probe in range(2):
            u = jnp.where(inside, COARSE[0][1], 0.0) * cw[probe, to, :]
            cu[0, probe, to, :] = u
            cc[probe, to, :] = u
    for k in range(COARSE_DEG - 1):
        a, c = COARSE[k + 1]
        c = jnp.where(inside, c, 0.0)
        old, new = k % 2, 1 - k % 2
        for p in range(1 + k, planes - 1 - k):
            to = pl.ds(p * wc, wc)
            for probe in range(2):
                u = cu[old, probe, to, :]
                before = cu[old, probe, pl.ds((p - 1) * wc, wc), :]
                after = cu[old, probe, pl.ds((p + 1) * wc, wc), :]
                if p == REACH:
                    before = before * link_l
                if p == REACH - 1:
                    after = after * link_l
                if p == REACH + cx:
                    before = before * link_r
                if p == REACH + cx - 1:
                    after = after * link_r
                row = p * wc
                beside = cu[old, probe, pl.ds(row - 1, wc), :] + cu[old, probe, pl.ds(row + 1, wc), :]
                near = ((before + after) + beside) + (below(u, cmasks) + above(u, cmasks))
                res = cw[probe, to, :] - (cw[2, to, :] * u - near)
                u = a * u + c * res
                if k + 2 < COARSE_DEG:
                    cw[probe, to, :] = res
                    cu[new, probe, to, :] = u
                cc[probe, to, :] = cc[probe, to, :] + u

    for msg, corners, to_right in ((x_a, cas, at.even), (x_b, cbs, at.odd)):
        for probe in range(2):
            for h in range(2):
                for k in range(2):
                    i = (probe * 2 + h) * 2 + k
                    base = (jnp.where(to_right, 2, 0) + k) * wy
                    rh[probe, h, rows(base + yoff, ny), :] = msg[pl.ds(sz.x2_base + i * ny, ny), :]
                    for s in range(n):
                        zero_row = pick(at.high_in[s], yoff + ny, yoff - 8)
                        rh[probe, h, rows(base + zero_row, 8), :] = zero8
                for s in range(n):
                    row = pick(at.high_in[s], yoff + ny, yoff - 1) + jnp.where(to_right, 2, 1) * wy
                    i = len(CORNER2) + probe * 2 + h
                    rh[probe, h, pl.ds(row, 1), :] = corners[s][pl.ds(i, 1), :]

    c0, (a1, c1), (a2, c2) = FINE[0][1], FINE[1], FINE[2]
    valid = row_mask(wy, at.valid)

    def spread(q, r_ref, r_plane, own, slot=0):
        for probe in range(2):
            u = cc[probe, rows((q + REACH) * wc, wc), :]
            sides = [cc[probe, rows((q + REACH - 1 + 2 * k) * wc, wc), :] for k in range(2)]
            u3 = 3.0 * u
            shifted = [pltpu.roll(u, 1, 0), pltpu.roll(u, wc - 1, 0)]
            for row in range(2):
                st_u[slot, probe, pl.ds(row, wc, stride=2), :] = u
            for h in range(2):
                g = u3 + (above(u, cmasks) if h else below(u, cmasks))
                for k in range(2):
                    for row in range(2):
                        st_g[slot, probe, h, k, pl.ds(row, wc, stride=2), :] = (g + sides[k]) + shifted[row]
        for k in range(2):
            to = rows((2 * q + k + 2) * wy, wy)
            for h in range(2):
                d = dw[h, to, :]
                for probe in range(2):
                    u = st_u[slot, probe, rows(yoff, wy), :]
                    old = r_ref[probe, h, rows((r_plane + k) * wy, wy), :]
                    res = (old - d * u) + st_g[slot, probe, h, k, rows(yoff, wy), :]
                    res = jnp.where(valid, res, 0.0)
                    re[probe, h, to, :] = res
                    if own:
                        mine = rows((2 * q + k) * wy, wy)
                        acc[probe, h, mine, :] = (sol_in[probe, h, mine, :] + u) + c0 * res

    def own_planes(i, _):
        for k in range(4):
            spread(4 * i + k, r_in, 2 * (4 * i + k), True, k)
        return 0

    lax.fori_loop(0, cx // 4, own_planes, 0)
    zero = jnp.zeros((wy, LANES), F32)
    for has, q, first in ((at.has_l, -1, 0), (at.has_r, cx, 2)):

        @pl.when(has)
        def _():
            spread(q, rh, first, False)

        @pl.when(jnp.logical_not(has))
        def _():
            for probe in range(2):
                for h in range(2):
                    for k in range(2):
                        re[probe, h, rows((2 * q + 2 + k) * wy, wy), :] = zero
                        u2[probe, h, rows((2 * q + 2 + k) * wy, wy), :] = zero

    for s in range(n):
        row = pick(at.high_in[s], yoff + ny, yoff - 2)
        for probe in range(2):
            for h in range(2):
                for k in range(2):
                    i = (probe * 2 + h) * 2 + k
                    to = pl.ds(2 * wy + row + k, nx, stride=wy)
                    re[probe, h, to, :] = re[probe, h, to, :] + ys[s][pl.ds(sz.y2_base + i * nx, nx), :]

    c1 = jnp.where(row_mask(wy, at.fine), c1, 0.0)

    def step1(first, count):
        def use(probe, p, v, av):
            to = rows((p + 2) * wy, wy)
            for h in range(2):
                res = v[h] - c0 * av[h]
                r1[probe, h, to, :] = res
                u2[probe, h, to, :] = (a1 * c0) * v[h] + c1 * res

        sweep(re, 2, dw, first, count, wy, masks, use)

    join = parity_matrix(True)
    width = 4

    def close(i):
        slot = i % 2
        planes = [(probe, k) for probe in range(2) for k in range(width)]
        own = [
            jnp.concatenate([pj[slot, probe, h, rows(k * wy + yoff, ny), :] for h in range(2)], axis=1)
            for probe, k in planes
        ]
        joined = permute_lanes(jnp.concatenate(own, axis=0), join, 2)
        for m, (probe, k) in enumerate(planes):
            ow[probe, width * i + k] = joined[m * ny : (m + 1) * ny]

    def send(i):
        part = pl.ds(width * i, width)
        return pltpu.make_async_copy(ow.at[:, part], out.at[:, part], sem.at[i])

    def step2(i):
        slot = i % 2

        def use(probe, p, v, av):
            to = rows((p + 2) * wy, wy)
            for h in range(2):
                res = r1[probe, h, to, :] - av[h]
                pj[slot, probe, h, rows((p - width * i) * wy, wy), :] = acc[probe, h, rows(p * wy, wy), :] + (
                    (1.0 + a2) * v[h] + c2 * res
                )

        sweep(u2, 2, dw, width * i, width, wy, masks, use)

    def steps2(i, _):
        close(i - 1)
        step2(i)
        send(i - 1).start()
        return 0

    @pl.when(at.has_l)
    def _():
        step1(-1, 1)

    @pl.when(at.has_r)
    def _():
        step1(nx, 1)

    looped(step1, nx)
    step2(0)
    lax.fori_loop(1, nx // width, steps2, 0)
    close(nx // width - 1)
    send(nx // width - 1).start()
    for i in range(nx // width):
        send(i).wait()


def on_device(n_gx, n_gy, right_side, diagonal, aggregates):
    nx, ny, nz = right_side.shape[1:]
    sz = Sizes(nx, ny, nz, n_gx, n_gy)
    n, wy, wc, cx = sz.sides, sz.wy, sz.wc, sz.cx

    pairs_a = [(k, k ^ 1) for k in range(n_gx)]
    pairs_b = [(k, k + 1) for k in range(1, n_gx - 1, 2)] + [(k + 1, k) for k in range(1, n_gx - 1, 2)]
    along = [[(0, 1), (1, 0)]] if sz.two else [
        [(k, k - 1) for k in range(1, n_gy)],
        [(k, k + 1) for k in range(n_gy - 1)],
    ]

    def both(pairs, perm):
        return [(a * n_gy + c, b * n_gy + d) for a, b in pairs for c, d in perm]

    perms = {"a": [("gx", pairs_a)], "b": [("gx", pairs_b)], "y": [("gy", perm) for perm in along]}
    corner_perms = [(("gx", "gy"), both(pairs, perm)) for pairs in (pairs_a, pairs_b) for perm in along]

    def exchange(order, messages):
        lines = [line for name in order for line in perms[name]] + corner_perms
        return [lax.ppermute(m, *line) for m, line in zip(messages, lines)]

    smem = pl.BlockSpec(memory_space=pltpu.SMEM)
    vmem = pl.BlockSpec(memory_space=pltpu.VMEM)
    hbm = pl.BlockSpec(memory_space=pltpu.HBM)
    params = pltpu.CompilerParams(vmem_limit_bytes=24 << 20)

    def shape(*dims):
        return jax.ShapeDtypeStruct(dims, F32)

    def messages(order, x, y, c):
        sizes = [y if name == "y" else x for name in order for _ in perms[name]]
        return [shape(size, LANES) for size in sizes + [c] * (2 * n)]

    packed = pl.pallas_call(
        functools.partial(pack_kernel, sz),
        in_specs=[hbm] * 2,
        out_specs=[vmem] * (2 + 3 * n),
        out_shape=messages(ORDER1, sz.x1, sz.y1, sz.c1),
        scratch_shapes=[
            pltpu.VMEM((2, 2, 3, ny, nz), F32),
            pltpu.VMEM((2, 2, ny, nz), F32),
            pltpu.VMEM((n, 2, nx, 8, nz), F32),
            pltpu.VMEM((n, nx, 8, nz), F32),
            pltpu.VMEM((n, 2, 2 * nx * 8, LANES), F32),
            pltpu.VMEM((n, 2, nx * 8, LANES), F32),
            pltpu.SemaphoreType.DMA((2 * n + 4,)),
        ],
        compiler_params=pltpu.CompilerParams(vmem_limit_bytes=105 << 19),
        name="pack_kernel",
    )(right_side, diagonal)
    halos = exchange(ORDER1, packed)
    bw, dw, cd = pl.pallas_call(
        functools.partial(open_kernel, sz),
        in_specs=[vmem] * 2,
        out_specs=[vmem] * 3,
        out_shape=[shape(*sz.bw), shape(*sz.dw), shape(sz.coarse, LANES)],
        scratch_shapes=[
            pltpu.VMEM((2, ny, LANES), F32),
        ],
        compiler_params=params,
        name="open_kernel",
    )(right_side, diagonal)
    results = pl.pallas_call(
        functools.partial(pre_kernel, sz),
        in_specs=[vmem] * (5 + 3 * n),
        out_specs=[vmem] * (7 + 3 * n),
        out_shape=[shape(*sz.bw), shape(*sz.dw), shape(*sz.brick), shape(*sz.brick), shape(2, sz.coarse, LANES)]
        + messages(ORDER2, sz.x2, sz.y2, sz.c2),
        scratch_shapes=[pltpu.VMEM((2, 2, (nx + 4) * wy, LANES), F32)] * 3 + [pltpu.VMEM((2, 2, wy, LANES), F32)],
        input_output_aliases={0: 0, 1: 1},
        compiler_params=params,
        name="pre_smooth",
    )(bw, dw, cd, *halos)
    dw, r_own, sol, coarse = results[1:5]
    halos = exchange(ORDER2, results[5:])
    planes = cx + 2 * REACH
    return pl.pallas_call(
        functools.partial(post_kernel, sz),
        in_specs=[smem] + [vmem] * (7 + 3 * n),
        out_specs=hbm,
        out_shape=shape(2, nx, ny, nz),
        scratch_shapes=[
            pltpu.VMEM((3, planes * wc, LANES), F32),
            pltpu.VMEM((2, 2, planes * wc, LANES), F32),
            pltpu.VMEM((2, planes * wc, LANES), F32),
            pltpu.VMEM((4, 2, 2, 2, 2 * wc, LANES), F32),
            pltpu.VMEM((4, 2, 2 * wc, LANES), F32),
            pltpu.VMEM((2, 2, 4 * wy, LANES), F32),
        ]
        + [pltpu.VMEM((2, 2, (nx + 4) * wy, LANES), F32)] * 3
        + [
            pltpu.VMEM(sz.brick, F32),
            pltpu.VMEM((2, 2, 2, 4 * wy, LANES), F32),
            pltpu.VMEM((2, nx, ny, nz), F32),
            pltpu.SemaphoreType.DMA((nx // 4,)),
        ],
        compiler_params=params,
        name="correct_and_smooth",
    )(aggregates, r_own, sol, dw, coarse, cd, *halos)


def solution(mesh):
    return jax.shard_map(
        functools.partial(on_device, mesh.shape["gx"], mesh.shape["gy"]),
        mesh=mesh,
        in_specs=(P(None, "gx", "gy", None), P("gx", "gy", None), P()),
        out_specs=P(None, "gx", "gy", None),
        check_vma=False,
    )
```

```python
import functools

import jax
import jax.numpy as jnp
from jax import lax
from jax.experimental import pallas as pl
from jax.experimental.pallas import tpu as pltpu
from jax.sharding import PartitionSpec as P

DEGREE = 3
COARSE_DEG = 6


FINE_LOWER = 3.0
FINE_UPPER = 12.4
COARSE_LOWER = 0.5
COARSE_UPPER = 13.4

LANES = 128
REACH = 7
F32 = jnp.float32


def cheb_pairs(lower, upper, count):
    middle = (upper + lower) / 2.0
    halfwidth = (upper - lower) / 2.0
    ratio_mid = middle / halfwidth
    rho_old = 1.0 / ratio_mid
    result = [(0.0, 1.0 / middle)]
    for repeat in range(count - 1):
        rho_new = 1.0 / (2.0 * ratio_mid - rho_old)
        result.append((rho_new * rho_old, 2.0 * rho_new / halfwidth))
        rho_old = rho_new
    return result


FINE = cheb_pairs(FINE_LOWER, FINE_UPPER, DEGREE)
COARSE = cheb_pairs(COARSE_LOWER, COARSE_UPPER, COARSE_DEG)


class Sizes:
    def __init__(self, nx, ny, nz, n_gx, n_gy):
        assert nz == 2 * LANES and n_gy >= 2 and ny % 16 == 0 and nx % 4 == 0
        self.nx, self.ny, self.nz = nx, ny, nz
        self.n_gx, self.n_gy = n_gx, n_gy
        self.two = n_gy == 2
        self.sides = 1 if self.two else 2
        self.wy = ny + 8 * self.sides
        self.cx, self.cy = nx // 2, ny // 2
        self.wc = self.cy + 8 * self.sides
        self.bw = (2, 2, (nx + 6) * self.wy, LANES)
        self.dw = (2, (nx + 4) * self.wy, LANES)
        self.brick = (2, 2, nx * self.wy, LANES)
        self.coarse = self.cx * self.cy
        self.x1 = 8 * 2 * ny
        self.y1 = 8 * 2 * nx
        self.c1 = 16
        self.x2_base = (3 * REACH - 4) * self.cy
        self.x2 = self.x2_base + 8 * ny
        self.y2_base = (3 * REACH - 4) * self.cx
        self.y2 = self.y2_base + 8 * nx
        self.c2 = 64


class Place:
    def __init__(self, sz):
        i, j = lax.axis_index("gx"), lax.axis_index("gy")
        self.i = i
        self.even = i % 2 == 0
        self.odd = i % 2 != 0
        self.has_l, self.has_r = i > 0, i < sz.n_gx - 1
        if sz.two:
            self.yoff = pl.multiple_of(8 * j, 8)
            self.high_in = [j == 0]
            self.high_out = [j == 0]
            self.fine = (j, sz.wy - 1 + j)
            self.crs = (j, sz.wc - 1 + j)
            self.valid = (6 * j, sz.ny + 2 + 6 * j)
        else:
            first, last = j == 0, j == sz.n_gy - 1
            self.yoff = 8
            self.high_in = [True, False]
            self.high_out = [False, True]
            self.fine = (jnp.where(first, 8, 1), jnp.where(last, sz.ny + 8, sz.wy - 1))
            self.crs = (jnp.where(first, 8, 1), jnp.where(last, sz.cy + 8, sz.wc - 1))
            self.valid = (jnp.where(first, 8, 6), jnp.where(last, sz.ny + 8, sz.ny + 10))


def pick(condition, yes, no):
    if isinstance(condition, bool):
        return yes if condition else no
    return jnp.where(condition, yes, no)


def edge(high, size, count):
    return pick(high, size - count, 0)


def rows(start, size):
    return pl.ds(pl.multiple_of(start, 8), size)


def lane_masks(height):
    lane = lax.broadcasted_iota(jnp.int32, (height, LANES), 1)
    return lane == 0, lane == LANES - 1


def row_mask(height, span):
    row = lax.broadcasted_iota(jnp.int32, (height, LANES), 0)
    return (row >= span[0]) & (row < span[1])


def y_sum(v):
    return pltpu.roll(v, 1, 0) + pltpu.roll(v, v.shape[0] - 1, 0)


def below(v, masks):
    return jnp.where(masks[0], 0.0, pltpu.roll(v, 1, 1))


def above(v, masks):
    return jnp.where(masks[1], 0.0, pltpu.roll(v, LANES - 1, 1))


def z_sum(even, odd, masks):
    return odd + below(odd, masks), even + above(even, masks)


def parity_matrix(transposed):
    row = lax.broadcasted_iota(jnp.int32, (2 * LANES, 2 * LANES), 0)
    col = lax.broadcasted_iota(jnp.int32, (2 * LANES, 2 * LANES), 1)
    if transposed:
        row, col = col, row
    return (row == 2 * (col % LANES) + col // LANES).astype(jnp.bfloat16)


def permute_lanes(v, matrix, terms):
    total = None
    for k in range(terms):
        part = v.astype(jnp.bfloat16)
        if k + 1 < terms:
            v = v - part.astype(F32)
        dot = jnp.dot(part, matrix, preferred_element_type=F32)
        total = dot if total is None else total + dot
    return total


def sweep(ref, shift, dw, first, count, wy, masks, use):
    for probe in range(2):

        def load(plane):
            return [ref[probe, h, rows((plane + shift) * wy, wy), :] for h in range(2)]

        before, now = load(first - 1), load(first)
        for k in range(count):
            plane = first + k
            at = plane + shift
            after = load(plane + 1)
            z = z_sum(now[0], now[1], masks)
            res = []
            for h in range(2):
                y = pltpu.roll(now[h], 1, 0) + ref[probe, h, pl.ds(at * wy + 1, wy), :]
                d = dw[h, rows((plane + 2) * wy, wy), :]
                res.append(d * now[h] - (((before[h] + after[h]) + y) + z[h]))
            use(probe, plane, now, res)
            before, now = now, after


def looped(step, count, width=4):
    def body(i, _):
        step(width * i, width)
        return 0

    lax.fori_loop(0, count // width, body, 0)


ORDER1 = "aby"
ORDER2 = "yba"


def sorted_messages(sz, order, refs):
    found, k = {}, 0
    for name in order:
        count = sz.sides if name == "y" else 1
        found[name] = refs[k : k + count]
        k += count
    return found["y"], found["b"][0], found["a"][0]


HALF = [slice(0, LANES), slice(LANES, 2 * LANES)]
CORNER1 = [(0, 0), (0, 1), (1, 0)]
CORNER2 = [(f, p, q) for f in range(3) for p in range(6) for q in range(6 - p - f // 2)]


def pack_kernel(sz, *refs):
    n = sz.sides
    rhs, diag = refs[:2]
    m_ys, m_b, m_a = sorted_messages(sz, ORDER1, refs[2 : 4 + n])
    m_cas, m_cbs = refs[4 + n : 4 + 2 * n], refs[4 + 2 * n : 4 + 3 * n]
    xr, xd, yr, yd, tr, td, sem = refs[4 + 3 * n :]
    nx, ny = sz.nx, sz.ny
    at = Place(sz)
    copies = []

    def fetch(src, dst):
        copy = pltpu.make_async_copy(src, dst, sem.at[len(copies)])
        copy.start()
        copies.append(copy)

    for s in range(n):
        slab = rows(edge(at.high_out[s], ny, 8), 8)
        fetch(rhs.at[:, :, slab, :], yr.at[s])
        fetch(diag.at[:, slab, :], yd.at[s])
    for e, right in enumerate((at.even, at.odd)):
        fetch(rhs.at[:, pl.ds(edge(right, nx, 3), 3)], xr.at[e])
        fetch(diag.at[pl.ds(edge(right, nx, 2), 2)], xd.at[e])
    split = parity_matrix(False)
    for copy in copies[: 2 * n]:
        copy.wait()
    for s in range(n):
        v = permute_lanes(yr[s].reshape(2 * nx * 8, 2 * LANES), split, 2)
        d = permute_lanes(yd[s].reshape(nx * 8, 2 * LANES), split, 2)
        for h in range(2):
            tr[s, h] = v[:, HALF[h]]
            td[s, h] = d[:, HALF[h]]
        high = at.high_out[s]
        for h in range(2):
            for k in range(3):
                for probe in range(2):
                    i = (probe * 3 + k) * 2 + h
                    row = edge(high, 8, 3) + k + probe * nx * 8
                    m_ys[s][pl.ds(i * nx, nx), :] = tr[s, h, pl.ds(row, nx, stride=8), :]
            for k in range(2):
                row = edge(high, 8, 2) + k
                m_ys[s][pl.ds((12 + 2 * k + h) * nx, nx), :] = td[s, h, pl.ds(row, nx, stride=8), :]
            for msgs, right in ((m_cas, at.even), (m_cbs, at.odd)):
                for m, (p, q) in enumerate(CORNER1):
                    row = pick(high, 7 - q, q) + pick(right, nx - 1 - p, p) * 8
                    for probe in range(2):
                        msgs[s][pl.ds((m * 2 + probe) * 2 + h, 1), :] = tr[s, h, pl.ds(row + probe * nx * 8, 1), :]
                row = pick(high, 7, 0) + pick(right, nx - 1, 0) * 8
                msgs[s][pl.ds(12 + h, 1), :] = td[s, h, pl.ds(row, 1), :]
                msgs[s][pl.ds(14 + h, 1), :] = td[s, h, pl.ds(row, 1), :]
    for copy in copies[2 * n :]:
        copy.wait()
    for e, msg in enumerate((m_a, m_b)):
        v = permute_lanes(xr[e].reshape(6 * ny, 2 * LANES), split, 2)
        d = permute_lanes(xd[e].reshape(2 * ny, 2 * LANES), split, 2)
        for k in range(6):
            for h in range(2):
                msg[pl.ds((2 * k + h) * ny, ny), :] = v[k * ny : (k + 1) * ny, HALF[h]]
        for k in range(2):
            for h in range(2):
                msg[pl.ds((12 + 2 * k + h) * ny, ny), :] = d[k * ny : (k + 1) * ny, HALF[h]]


def open_kernel(sz, rhs, diag, bw, dw, cd, xs):
    nx, ny, wy, cy = sz.nx, sz.ny, sz.wy, sz.cy
    at = Place(sz)
    split = parity_matrix(False)
    zero8 = jnp.zeros((8, LANES), F32)
    zero_at = [pick(at.high_in[s], at.yoff + ny, at.yoff - 8) for s in range(sz.sides)]
    width = 4

    def body(i, _):
        for f in range(3):
            src = diag[pl.ds(width * i, width)] if f == 2 else rhs[f, pl.ds(width * i, width)]
            v = permute_lanes(src.reshape(width * ny, 2 * LANES), split, 2)
            if f == 2:
                v = v + 6.0
            for k in range(width):
                for h in range(2):
                    if f == 2:
                        ref, base = dw.at[h], (width * i + k + 2) * wy
                    else:
                        ref, base = bw.at[f, h], (width * i + k + 3) * wy
                    ref[rows(base + at.yoff, ny), :] = v[k * ny : (k + 1) * ny, HALF[h]]
                    for z in zero_at:
                        ref[rows(base + z, 8), :] = zero8
            if f == 2:
                for k in range(width // 2):
                    low, high = v[2 * k * ny : (2 * k + 1) * ny], v[(2 * k + 1) * ny : (2 * k + 2) * ny]
                    total = low + high
                    xs[k] = total[:, HALF[0]] + total[:, HALF[1]]
                    pair = xs[k, pl.ds(0, cy, stride=2), :] + xs[k, pl.ds(1, cy, stride=2), :]
                    cd[rows((i * (width // 2) + k) * cy, cy), :] = 0.5 * pair - 18.0
        return 0

    lax.fori_loop(0, nx // width, body, 0)


def pre_kernel(sz, *refs):
    n = sz.sides
    cd = refs[2]
    ys, xb, xa = sorted_messages(sz, ORDER1, refs[3 : 5 + n])
    cas, cbs = refs[5 + n : 5 + 2 * n], refs[5 + 2 * n : 5 + 3 * n]
    outs = refs[5 + 3 * n :]
    bw, dw, r_out, sol_out, coarse = outs[:5]
    m_ys, m_b, m_a = sorted_messages(sz, ORDER2, outs[5 : 7 + n])
    m_cas, m_cbs = outs[7 + n : 7 + 2 * n], outs[7 + 2 * n : 7 + 3 * n]
    r1, u2, u3, xs = outs[7 + 3 * n :]
    nx, ny, wy, cx, cy = sz.nx, sz.ny, sz.wy, sz.cx, sz.cy
    at = Place(sz)
    yoff = at.yoff
    masks = lane_masks(wy)

    zero8 = jnp.zeros((8, LANES), F32)
    zero_at = [pick(at.high_in[s], yoff + ny, yoff - 8) for s in range(n)]
    for msg, corners, to_right in ((xa, cas, at.even), (xb, cbs, at.odd)):
        b0 = jnp.where(to_right, nx + 3, 0)
        d0 = jnp.where(to_right, nx + 2, 0)
        for h in range(2):
            for k in range(3):
                for probe in range(2):
                    i = (probe * 3 + k) * 2 + h
                    bw[probe, h, rows((b0 + k) * wy + yoff, ny), :] = msg[pl.ds(i * ny, ny), :]
                    for z in zero_at:
                        bw[probe, h, rows((b0 + k) * wy + z, 8), :] = zero8
            for k in range(2):
                dw[h, rows((d0 + k) * wy + yoff, ny), :] = 6.0 + msg[pl.ds((12 + 2 * k + h) * ny, ny), :]
                for z in zero_at:
                    dw[h, rows((d0 + k) * wy + z, 8), :] = zero8
            for s in range(n):
                for m, (p, q) in enumerate(CORNER1):
                    row = pick(at.high_in[s], yoff + ny + q, yoff - 1 - q)
                    row = row + jnp.where(to_right, nx + 3 + p, 2 - p) * wy
                    for probe in range(2):
                        bw[probe, h, pl.ds(row, 1), :] = corners[s][pl.ds((m * 2 + probe) * 2 + h, 1), :]
                row = pick(at.high_in[s], yoff + ny, yoff - 1) + jnp.where(to_right, nx + 2, 1) * wy
                dw[h, pl.ds(row, 1), :] = 6.0 + corners[s][pl.ds(12 + h, 1), :]
    for s in range(n):
        br = pick(at.high_in[s], ny, -3) + yoff
        dr = pick(at.high_in[s], ny, -2) + yoff
        for h in range(2):
            for k in range(3):
                for probe in range(2):
                    i = (probe * 3 + k) * 2 + h
                    bw[probe, h, pl.ds(3 * wy + br + k, nx, stride=wy), :] = ys[s][pl.ds(i * nx, nx), :]
            for k in range(2):
                i = 12 + 2 * k + h
                dw[h, pl.ds(2 * wy + dr + k, nx, stride=wy), :] = 6.0 + ys[s][pl.ds(i * nx, nx), :]
    zero = jnp.zeros((wy, LANES), F32)
    for probe in range(2):
        for h in range(2):
            for i in (1, nx + 2):
                u2[probe, h, rows(i * wy, wy), :] = zero
                u3[probe, h, rows(i * wy, wy), :] = zero

    inside = row_mask(wy, at.fine)
    c0, (a1, c1), (a2, c2) = FINE[0][1], FINE[1], FINE[2]
    c1 = jnp.where(inside, c1, 0.0)
    c2 = jnp.where(inside, c2, 0.0)

    def step1(first, count):
        def use(probe, p, v, av):
            to = rows((p + 2) * wy, wy)
            for h in range(2):
                res = v[h] - c0 * av[h]
                r1[probe, h, to, :] = res
                u2[probe, h, to, :] = (a1 * c0) * v[h] + c1 * res

        sweep(bw, 3, dw, first, count, wy, masks, use)

    def step2(first, count):
        def use(probe, p, v, av):
            to = rows((p + 2) * wy, wy)
            for h in range(2):
                res = r1[probe, h, to, :] - av[h]
                r1[probe, h, to, :] = res
                u3[probe, h, to, :] = a2 * v[h] + c2 * res

        sweep(u2, 2, dw, first, count, wy, masks, use)

    mine = row_mask(wy, (yoff, yoff + ny))

    def steps3(i, _):
        totals = {}

        def use(probe, p, v, av):
            src = rows((p + 2) * wy, wy)
            to = rows(p * wy, wy)
            total = None
            for h in range(2):
                out = jnp.where(mine, r1[probe, h, src, :] - av[h], 0.0)
                r_out[probe, h, to, :] = out
                sol_out[probe, h, to, :] = (
                    c0 * bw[probe, h, rows((p + 3) * wy, wy), :] + u2[probe, h, src, :] + v[h]
                )
                total = out if total is None else total + out
            k = len(totals.setdefault(probe, []))
            totals[probe].append(total)
            if k % 2:
                xs[k // 2, probe] = totals[probe][k - 1] + total

        sweep(u3, 2, dw, 4 * i, 4, wy, masks, use)
        for k in range(2):
            for probe in range(2):
                pair = (
                    xs[k, probe, pl.ds(yoff, cy, stride=2), :] + xs[k, probe, pl.ds(yoff + 1, cy, stride=2), :]
                )
                coarse[probe, rows((2 * i + k) * cy, cy), :] = 0.5 * pair
        return 0

    @pl.when(at.has_l)
    def _():
        step1(-2, 2)

    @pl.when(at.has_r)
    def _():
        step1(nx, 2)

    looped(step1, nx)

    @pl.when(at.has_l)
    def _():
        step2(-1, 1)

    @pl.when(at.has_r)
    def _():
        step2(nx, 1)

    looped(step2, nx)
    lax.fori_loop(0, nx // 4, steps3, 0)

    field = [coarse.at[0], coarse.at[1], cd]
    depth = [REACH, REACH, REACH - 1]
    for msg, corners, right in ((m_a, m_cas, at.even), (m_b, m_cbs, at.odd)):
        for f in range(3):
            size = (depth[f] - 1) * cy
            first = pick(right, cx - depth[f], 1)
            msg[pl.ds(f * (REACH - 1) * cy, size), :] = field[f][rows(first * cy, size), :]
        for s in range(n):
            for m, (f, p, q) in enumerate(CORNER2):
                row = pick(at.high_out[s], cy - 1 - q, q) + pick(right, cx - 1 - p, p) * cy
                corners[s][pl.ds(m, 1), :] = field[f][pl.ds(row, 1), :]
            row = pick(at.high_out[s], yoff + ny - 1, yoff) + pick(right, nx - 1, 0) * wy
            for probe in range(2):
                for h in range(2):
                    i = len(CORNER2) + probe * 2 + h
                    corners[s][pl.ds(i, 1), :] = r_out[probe, h, pl.ds(row, 1), :]
            corners[s][pl.ds(sz.c2 - 3, 3), :] = jnp.zeros((3, LANES), F32)
        for probe in range(2):
            for h in range(2):
                for k in range(2):
                    i = (probe * 2 + h) * 2 + k
                    row = (edge(right, nx, 2) + k) * wy + yoff
                    msg[pl.ds(sz.x2_base + i * ny, ny), :] = r_out[probe, h, rows(row, ny), :]
    for s in range(n):
        for f in range(3):
            for k in range(depth[f] - 1):
                row = pick(at.high_out[s], cy - depth[f], 1) + k
                m_ys[s][pl.ds((f * (REACH - 1) + k) * cx, cx), :] = field[f][pl.ds(row, cx, stride=cy), :]
        row = edge(at.high_out[s], ny, 2) + yoff
        for probe in range(2):
            for h in range(2):
                for k in range(2):
                    i = (probe * 2 + h) * 2 + k
                    m_ys[s][pl.ds(sz.y2_base + i * nx, nx), :] = r_out[probe, h, pl.ds(row + k, nx, stride=wy), :]


def post_kernel(sz, *refs):
    n = sz.sides
    agg, r_in, sol_in, dw, coarse, cd = refs[:6]
    ys, x_b, x_a = sorted_messages(sz, ORDER2, refs[6 : 8 + n])
    cas, cbs = refs[8 + n : 8 + 2 * n], refs[8 + 2 * n : 8 + 3 * n]
    out = refs[8 + 3 * n]
    cw, cu, cc, pt, st_g, st_u, rh, re, r1, u2, acc, pj, ow, sem = refs[9 + 3 * n :]
    nx, ny, wy, cx, cy, wc = sz.nx, sz.ny, sz.wy, sz.cx, sz.cy, sz.wc
    at = Place(sz)
    yoff = at.yoff
    masks = lane_masks(wy)
    planes = cx + 2 * REACH

    zero8 = jnp.zeros((8, LANES), F32)
    zero_at = [pick(at.high_in[s], yoff + cy, yoff - 8) for s in range(n)]
    field = [coarse.at[0], coarse.at[1], cd]
    depth = [REACH, REACH, REACH - 1]
    for f in range(3):
        for p in range(planes):
            for z in zero_at:
                cw[f, rows(p * wc + z, 8), :] = zero8
        for x in range(cx):
            cw[f, rows((x + REACH) * wc + yoff, cy), :] = field[f][rows(x * cy, cy), :]
        for s in range(n):
            for k in range(depth[f] - 1):
                row = pick(at.high_in[s], yoff + cy + 1, yoff - depth[f]) + k
                cw[f, pl.ds(REACH * wc + row, cx, stride=wc), :] = ys[s][rows((f * (REACH - 1) + k) * cx, cx), :]
            total = None
            for h in range(2):
                for k in range(2):
                    if f == 2:
                        row = pick(at.high_in[s], yoff + ny, yoff - 2) + k
                        part = dw[h, pl.ds(2 * wy + row, nx, stride=wy), :]
                    else:
                        part = ys[s][pl.ds(sz.y2_base + ((f * 2 + h) * 2 + k) * nx, nx), :]
                    total = part if total is None else total + part
            slot = 6 + s * 3 + f
            pt[slot, pl.ds(0, nx), :] = total
            pair = pt[slot, pl.ds(0, cx, stride=2), :] + pt[slot, pl.ds(1, cx, stride=2), :]
            row = pick(at.high_in[s], yoff + cy, yoff - 1)
            cw[f, pl.ds(REACH * wc + row, cx, stride=wc), :] = 0.5 * pair - (18.0 if f == 2 else 0.0)
        for side, (msg, to_right) in enumerate(((x_a, at.even), (x_b, at.odd))):
            first = jnp.where(to_right, REACH + cx + 1, REACH - depth[f])
            for k in range(depth[f] - 1):
                cw[f, rows((first + k) * wc + yoff, cy), :] = msg[rows((f * (REACH - 1) + k) * cy, cy), :]
            total = None
            for h in range(2):
                for k in range(2):
                    if f == 2:
                        plane = jnp.where(to_right, nx + 2, 0) + k
                        part = dw[h, rows(plane * wy + yoff, ny), :]
                    else:
                        part = msg[pl.ds(sz.x2_base + ((f * 2 + h) * 2 + k) * ny, ny), :]
                    total = part if total is None else total + part
            slot = side * 3 + f
            pt[slot, pl.ds(0, ny), :] = total
            pair = pt[slot, pl.ds(0, cy, stride=2), :] + pt[slot, pl.ds(1, cy, stride=2), :]
            plane = jnp.where(to_right, REACH + cx, REACH - 1)
            cw[f, rows(plane * wc + yoff, cy), :] = 0.5 * pair - (18.0 if f == 2 else 0.0)
    for corners, to_right in ((cas, at.even), (cbs, at.odd)):
        for s in range(n):
            for m, (f, p, q) in enumerate(CORNER2):
                row = pick(at.high_in[s], yoff + cy + q, yoff - 1 - q)
                row = row + jnp.where(to_right, REACH + cx + p, REACH - 1 - p) * wc
                cw[f, pl.ds(row, 1), :] = corners[s][pl.ds(m, 1), :]

    cmasks = lane_masks(wc)
    inside = row_mask(wc, at.crs)
    i = at.i
    here = agg[i]
    link_l = (at.has_l & (agg[jnp.maximum(i - 1, 0)] == here)).astype(F32)
    link_r = (at.has_r & (agg[jnp.minimum(i + 1, sz.n_gx - 1)] == here)).astype(F32)
    for p in range(planes):
        to = pl.ds(p * wc, wc)
        for probe in range(2):
            u = jnp.where(inside, COARSE[0][1], 0.0) * cw[probe, to, :]
            cu[0, probe, to, :] = u
            cc[probe, to, :] = u
    for k in range(COARSE_DEG - 1):
        a, c = COARSE[k + 1]
        c = jnp.where(inside, c, 0.0)
        old, new = k % 2, 1 - k % 2
        for p in range(1 + k, planes - 1 - k):
            to = pl.ds(p * wc, wc)
            for probe in range(2):
                u = cu[old, probe, to, :]
                before = cu[old, probe, pl.ds((p - 1) * wc, wc), :]
                after = cu[old, probe, pl.ds((p + 1) * wc, wc), :]
                if p == REACH:
                    before = before * link_l
                if p == REACH - 1:
                    after = after * link_l
                if p == REACH + cx:
                    before = before * link_r
                if p == REACH + cx - 1:
                    after = after * link_r
                row = p * wc
                beside = cu[old, probe, pl.ds(row - 1, wc), :] + cu[old, probe, pl.ds(row + 1, wc), :]
                near = ((before + after) + beside) + (below(u, cmasks) + above(u, cmasks))
                res = cw[probe, to, :] - (cw[2, to, :] * u - near)
                u = a * u + c * res
                if k + 2 < COARSE_DEG:
                    cw[probe, to, :] = res
                    cu[new, probe, to, :] = u
                cc[probe, to, :] = cc[probe, to, :] + u

    for msg, corners, to_right in ((x_a, cas, at.even), (x_b, cbs, at.odd)):
        for probe in range(2):
            for h in range(2):
                for k in range(2):
                    i = (probe * 2 + h) * 2 + k
                    base = (jnp.where(to_right, 2, 0) + k) * wy
                    rh[probe, h, rows(base + yoff, ny), :] = msg[pl.ds(sz.x2_base + i * ny, ny), :]
                    for s in range(n):
                        zero_row = pick(at.high_in[s], yoff + ny, yoff - 8)
                        rh[probe, h, rows(base + zero_row, 8), :] = zero8
                for s in range(n):
                    row = pick(at.high_in[s], yoff + ny, yoff - 1) + jnp.where(to_right, 2, 1) * wy
                    i = len(CORNER2) + probe * 2 + h
                    rh[probe, h, pl.ds(row, 1), :] = corners[s][pl.ds(i, 1), :]

    c0, (a1, c1), (a2, c2) = FINE[0][1], FINE[1], FINE[2]
    valid = row_mask(wy, at.valid)

    def spread(q, r_ref, r_plane, own, slot=0):
        for probe in range(2):
            u = cc[probe, rows((q + REACH) * wc, wc), :]
            sides = [cc[probe, rows((q + REACH - 1 + 2 * k) * wc, wc), :] for k in range(2)]
            u3 = 3.0 * u
            shifted = [pltpu.roll(u, 1, 0), pltpu.roll(u, wc - 1, 0)]
            for row in range(2):
                st_u[slot, probe, pl.ds(row, wc, stride=2), :] = u
            for h in range(2):
                g = u3 + (above(u, cmasks) if h else below(u, cmasks))
                for k in range(2):
                    for row in range(2):
                        st_g[slot, probe, h, k, pl.ds(row, wc, stride=2), :] = (g + sides[k]) + shifted[row]
        for k in range(2):
            to = rows((2 * q + k + 2) * wy, wy)
            for h in range(2):
                d = dw[h, to, :]
                for probe in range(2):
                    u = st_u[slot, probe, rows(yoff, wy), :]
                    old = r_ref[probe, h, rows((r_plane + k) * wy, wy), :]
                    res = (old - d * u) + st_g[slot, probe, h, k, rows(yoff, wy), :]
                    res = jnp.where(valid, res, 0.0)
                    re[probe, h, to, :] = res
                    if own:
                        mine = rows((2 * q + k) * wy, wy)
                        acc[probe, h, mine, :] = (sol_in[probe, h, mine, :] + u) + c0 * res

    def own_planes(i, _):
        for k in range(4):
            spread(4 * i + k, r_in, 2 * (4 * i + k), True, k)
        return 0

    lax.fori_loop(0, cx // 4, own_planes, 0)
    zero = jnp.zeros((wy, LANES), F32)
    for has, q, first in ((at.has_l, -1, 0), (at.has_r, cx, 2)):

        @pl.when(has)
        def _():
            spread(q, rh, first, False)

        @pl.when(jnp.logical_not(has))
        def _():
            for probe in range(2):
                for h in range(2):
                    for k in range(2):
                        re[probe, h, rows((2 * q + 2 + k) * wy, wy), :] = zero
                        u2[probe, h, rows((2 * q + 2 + k) * wy, wy), :] = zero

    for s in range(n):
        row = pick(at.high_in[s], yoff + ny, yoff - 2)
        for probe in range(2):
            for h in range(2):
                for k in range(2):
                    i = (probe * 2 + h) * 2 + k
                    to = pl.ds(2 * wy + row + k, nx, stride=wy)
                    re[probe, h, to, :] = re[probe, h, to, :] + ys[s][pl.ds(sz.y2_base + i * nx, nx), :]

    c1 = jnp.where(row_mask(wy, at.fine), c1, 0.0)

    def step1(first, count):
        def use(probe, p, v, av):
            to = rows((p + 2) * wy, wy)
            for h in range(2):
                res = v[h] - c0 * av[h]
                r1[probe, h, to, :] = res
                u2[probe, h, to, :] = (a1 * c0) * v[h] + c1 * res

        sweep(re, 2, dw, first, count, wy, masks, use)

    join = parity_matrix(True)
    width = 4

    def close(i):
        slot = i % 2
        planes = [(probe, k) for probe in range(2) for k in range(width)]
        own = [
            jnp.concatenate([pj[slot, probe, h, rows(k * wy + yoff, ny), :] for h in range(2)], axis=1)
            for probe, k in planes
        ]
        joined = permute_lanes(jnp.concatenate(own, axis=0), join, 2)
        for m, (probe, k) in enumerate(planes):
            ow[probe, width * i + k] = joined[m * ny : (m + 1) * ny]

    def send(i):
        part = pl.ds(width * i, width)
        return pltpu.make_async_copy(ow.at[:, part], out.at[:, part], sem.at[i])

    def step2(i):
        slot = i % 2

        def use(probe, p, v, av):
            to = rows((p + 2) * wy, wy)
            for h in range(2):
                res = r1[probe, h, to, :] - av[h]
                pj[slot, probe, h, rows((p - width * i) * wy, wy), :] = acc[probe, h, rows(p * wy, wy), :] + (
                    (1.0 + a2) * v[h] + c2 * res
                )

        sweep(u2, 2, dw, width * i, width, wy, masks, use)

    def steps2(i, _):
        close(i - 1)
        step2(i)
        send(i - 1).start()
        return 0

    @pl.when(at.has_l)
    def _():
        step1(-1, 1)

    @pl.when(at.has_r)
    def _():
        step1(nx, 1)

    looped(step1, nx)
    step2(0)
    lax.fori_loop(1, nx // width, steps2, 0)
    close(nx // width - 1)
    send(nx // width - 1).start()
    for i in range(nx // width):
        send(i).wait()


def on_device(n_gx, n_gy, right_side, diagonal, aggregates):
    nx, ny, nz = right_side.shape[1:]
    sz = Sizes(nx, ny, nz, n_gx, n_gy)
    n, wy, wc, cx = sz.sides, sz.wy, sz.wc, sz.cx

    pairs_a = [(k, k ^ 1) for k in range(n_gx)]
    pairs_b = [(k, k + 1) for k in range(1, n_gx - 1, 2)] + [(k + 1, k) for k in range(1, n_gx - 1, 2)]
    along = [[(0, 1), (1, 0)]] if sz.two else [
        [(k, k - 1) for k in range(1, n_gy)],
        [(k, k + 1) for k in range(n_gy - 1)],
    ]

    def both(pairs, perm):
        return [(a * n_gy + c, b * n_gy + d) for a, b in pairs for c, d in perm]

    perms = {"a": [("gx", pairs_a)], "b": [("gx", pairs_b)], "y": [("gy", perm) for perm in along]}
    corner_perms = [(("gx", "gy"), both(pairs, perm)) for pairs in (pairs_a, pairs_b) for perm in along]

    def exchange(order, messages):
        lines = [line for name in order for line in perms[name]] + corner_perms
        return [lax.ppermute(m, *line) for m, line in zip(messages, lines)]

    smem = pl.BlockSpec(memory_space=pltpu.SMEM)
    vmem = pl.BlockSpec(memory_space=pltpu.VMEM)
    hbm = pl.BlockSpec(memory_space=pltpu.HBM)
    params = pltpu.CompilerParams(vmem_limit_bytes=24 << 20)

    def shape(*dims):
        return jax.ShapeDtypeStruct(dims, F32)

    def messages(order, x, y, c):
        sizes = [y if name == "y" else x for name in order for _ in perms[name]]
        return [shape(size, LANES) for size in sizes + [c] * (2 * n)]

    packed = pl.pallas_call(
        functools.partial(pack_kernel, sz),
        in_specs=[hbm] * 2,
        out_specs=[vmem] * (2 + 3 * n),
        out_shape=messages(ORDER1, sz.x1, sz.y1, sz.c1),
        scratch_shapes=[
            pltpu.VMEM((2, 2, 3, ny, nz), F32),
            pltpu.VMEM((2, 2, ny, nz), F32),
            pltpu.VMEM((n, 2, nx, 8, nz), F32),
            pltpu.VMEM((n, nx, 8, nz), F32),
            pltpu.VMEM((n, 2, 2 * nx * 8, LANES), F32),
            pltpu.VMEM((n, 2, nx * 8, LANES), F32),
            pltpu.SemaphoreType.DMA((2 * n + 4,)),
        ],
        compiler_params=pltpu.CompilerParams(vmem_limit_bytes=105 << 19),
        name="pack_kernel",
    )(right_side, diagonal)
    halos = exchange(ORDER1, packed)
    bw, dw, cd = pl.pallas_call(
        functools.partial(open_kernel, sz),
        in_specs=[vmem] * 2,
        out_specs=[vmem] * 3,
        out_shape=[shape(*sz.bw), shape(*sz.dw), shape(sz.coarse, LANES)],
        scratch_shapes=[
            pltpu.VMEM((2, ny, LANES), F32),
        ],
        compiler_params=params,
        name="open_kernel",
    )(right_side, diagonal)
    results = pl.pallas_call(
        functools.partial(pre_kernel, sz),
        in_specs=[vmem] * (5 + 3 * n),
        out_specs=[vmem] * (7 + 3 * n),
        out_shape=[shape(*sz.bw), shape(*sz.dw), shape(*sz.brick), shape(*sz.brick), shape(2, sz.coarse, LANES)]
        + messages(ORDER2, sz.x2, sz.y2, sz.c2),
        scratch_shapes=[pltpu.VMEM((2, 2, (nx + 4) * wy, LANES), F32)] * 3 + [pltpu.VMEM((2, 2, wy, LANES), F32)],
        input_output_aliases={0: 0, 1: 1},
        compiler_params=params,
        name="pre_smooth",
    )(bw, dw, cd, *halos)
    dw, r_own, sol, coarse = results[1:5]
    halos = exchange(ORDER2, results[5:])
    planes = cx + 2 * REACH
    return pl.pallas_call(
        functools.partial(post_kernel, sz),
        in_specs=[smem] + [vmem] * (7 + 3 * n),
        out_specs=hbm,
        out_shape=shape(2, nx, ny, nz),
        scratch_shapes=[
            pltpu.VMEM((3, planes * wc, LANES), F32),
            pltpu.VMEM((2, 2, planes * wc, LANES), F32),
            pltpu.VMEM((2, planes * wc, LANES), F32),
            pltpu.VMEM((6 + 3 * n, max(nx, ny), LANES), F32),
            pltpu.VMEM((4, 2, 2, 2, 2 * wc, LANES), F32),
            pltpu.VMEM((4, 2, 2 * wc, LANES), F32),
            pltpu.VMEM((2, 2, 4 * wy, LANES), F32),
        ]
        + [pltpu.VMEM((2, 2, (nx + 4) * wy, LANES), F32)] * 3
        + [
            pltpu.VMEM(sz.brick, F32),
            pltpu.VMEM((2, 2, 2, 4 * wy, LANES), F32),
            pltpu.VMEM((2, nx, ny, nz), F32),
            pltpu.SemaphoreType.DMA((nx // 4,)),
        ],
        compiler_params=params,
        name="correct_and_smooth",
    )(aggregates, r_own, sol, dw, coarse, cd, *halos)


def solution(mesh):
    return jax.shard_map(
        functools.partial(on_device, mesh.shape["gx"], mesh.shape["gy"]),
        mesh=mesh,
        in_specs=(P(None, "gx", "gy", None), P("gx", "gy", None), P()),
        out_specs=P(None, "gx", "gy", None),
        check_vma=False,
    )
```

```python
import functools

import jax
import jax.numpy as jnp
from jax import lax
from jax.experimental import pallas as pl
from jax.experimental.pallas import tpu as pltpu
from jax.sharding import PartitionSpec as P

DEGREE = 3
COARSE_DEG = 6


FINE_LOWER = 3.0
FINE_UPPER = 12.4
COARSE_LOWER = 0.5
COARSE_UPPER = 13.4

LANES = 128
REACH = 7
F32 = jnp.float32


def cheb_pairs(lower, upper, count):
    middle = (upper + lower) / 2.0
    halfwidth = (upper - lower) / 2.0
    ratio_mid = middle / halfwidth
    rho_old = 1.0 / ratio_mid
    result = [(0.0, 1.0 / middle)]
    for repeat in range(count - 1):
        rho_new = 1.0 / (2.0 * ratio_mid - rho_old)
        result.append((rho_new * rho_old, 2.0 * rho_new / halfwidth))
        rho_old = rho_new
    return result


FINE = cheb_pairs(FINE_LOWER, FINE_UPPER, DEGREE)
COARSE = cheb_pairs(COARSE_LOWER, COARSE_UPPER, COARSE_DEG)


class Sizes:
    def __init__(self, nx, ny, nz, n_gx, n_gy):
        assert nz == 2 * LANES and n_gy >= 2 and ny % 16 == 0 and nx % 8 == 0
        self.nx, self.ny, self.nz = nx, ny, nz
        self.n_gx, self.n_gy = n_gx, n_gy
        self.two = n_gy == 2
        self.sides = 1 if self.two else 2
        self.wy = ny + 8 * self.sides
        self.cx, self.cy = nx // 2, ny // 2
        self.wc = self.cy + 8 * self.sides
        self.bw = (2, 2, (nx + 6) * self.wy, LANES)
        self.dw = (2, (nx + 4) * self.wy, LANES)
        self.brick = (2, 2, nx * self.wy, LANES)
        self.coarse = self.cx * self.cy
        self.x1 = 8 * 2 * ny
        self.y1 = 8 * 2 * nx
        self.c1 = 16
        self.x2_base = (3 * REACH - 4) * self.cy
        self.x2 = self.x2_base + 8 * ny
        self.y2_base = (3 * REACH - 4) * self.cx
        self.y2 = self.y2_base + 8 * nx
        self.c2 = 64


class Place:
    def __init__(self, sz):
        i, j = lax.axis_index("gx"), lax.axis_index("gy")
        self.i = i
        self.even = i % 2 == 0
        self.odd = i % 2 != 0
        self.has_l, self.has_r = i > 0, i < sz.n_gx - 1
        if sz.two:
            self.yoff = pl.multiple_of(8 * j, 8)
            self.high_in = [j == 0]
            self.high_out = [j == 0]
            self.fine = (j, sz.wy - 1 + j)
            self.crs = (j, sz.wc - 1 + j)
            self.valid = (6 * j, sz.ny + 2 + 6 * j)
        else:
            first, last = j == 0, j == sz.n_gy - 1
            self.yoff = 8
            self.high_in = [True, False]
            self.high_out = [False, True]
            self.fine = (jnp.where(first, 8, 1), jnp.where(last, sz.ny + 8, sz.wy - 1))
            self.crs = (jnp.where(first, 8, 1), jnp.where(last, sz.cy + 8, sz.wc - 1))
            self.valid = (jnp.where(first, 8, 6), jnp.where(last, sz.ny + 8, sz.ny + 10))


def pick(condition, yes, no):
    if isinstance(condition, bool):
        return yes if condition else no
    return jnp.where(condition, yes, no)


def edge(high, size, count):
    return pick(high, size - count, 0)


def rows(start, size):
    return pl.ds(pl.multiple_of(start, 8), size)


def lane_masks(height):
    lane = lax.broadcasted_iota(jnp.int32, (height, LANES), 1)
    return lane == 0, lane == LANES - 1


def row_mask(height, span):
    row = lax.broadcasted_iota(jnp.int32, (height, LANES), 0)
    return (row >= span[0]) & (row < span[1])


def y_sum(v):
    return pltpu.roll(v, 1, 0) + pltpu.roll(v, v.shape[0] - 1, 0)


def below(v, masks):
    return jnp.where(masks[0], 0.0, pltpu.roll(v, 1, 1))


def above(v, masks):
    return jnp.where(masks[1], 0.0, pltpu.roll(v, LANES - 1, 1))


def z_sum(even, odd, masks):
    return odd + below(odd, masks), even + above(even, masks)


def parity_matrix(transposed):
    row = lax.broadcasted_iota(jnp.int32, (2 * LANES, 2 * LANES), 0)
    col = lax.broadcasted_iota(jnp.int32, (2 * LANES, 2 * LANES), 1)
    if transposed:
        row, col = col, row
    return (row == 2 * (col % LANES) + col // LANES).astype(jnp.bfloat16)


def permute_lanes(v, matrix, terms):
    total = None
    for k in range(terms):
        part = v.astype(jnp.bfloat16)
        if k + 1 < terms:
            v = v - part.astype(F32)
        dot = jnp.dot(part, matrix, preferred_element_type=F32)
        total = dot if total is None else total + dot
    return total


def sweep(ref, shift, dw, first, count, wy, masks, use):
    for probe in range(2):

        def load(plane):
            return [ref[probe, h, rows((plane + shift) * wy, wy), :] for h in range(2)]

        before, now = load(first - 1), load(first)
        for k in range(count):
            plane = first + k
            at = plane + shift
            after = load(plane + 1)
            z = z_sum(now[0], now[1], masks)
            res = []
            for h in range(2):
                y = pltpu.roll(now[h], 1, 0) + ref[probe, h, pl.ds(at * wy + 1, wy), :]
                d = dw[h, rows((plane + 2) * wy, wy), :]
                res.append(d * now[h] - (((before[h] + after[h]) + y) + z[h]))
            use(probe, plane, now, res)
            before, now = now, after


def looped(step, count, width=8):
    def body(i, _):
        step(width * i, width)
        return 0

    lax.fori_loop(0, count // width, body, 0)


ORDER1 = "aby"
ORDER2 = "yba"


def sorted_messages(sz, order, refs):
    found, k = {}, 0
    for name in order:
        count = sz.sides if name == "y" else 1
        found[name] = refs[k : k + count]
        k += count
    return found["y"], found["b"][0], found["a"][0]


HALF = [slice(0, LANES), slice(LANES, 2 * LANES)]
CORNER1 = [(0, 0), (0, 1), (1, 0)]
CORNER2 = [(f, p, q) for f in range(3) for p in range(6) for q in range(6 - p - f // 2)]


def pack_kernel(sz, *refs):
    n = sz.sides
    rhs, diag = refs[:2]
    m_ys, m_b, m_a = sorted_messages(sz, ORDER1, refs[2 : 4 + n])
    m_cas, m_cbs = refs[4 + n : 4 + 2 * n], refs[4 + 2 * n : 4 + 3 * n]
    xr, xd, yr, yd, tr, td, sem = refs[4 + 3 * n :]
    nx, ny = sz.nx, sz.ny
    at = Place(sz)
    copies = []

    def fetch(src, dst):
        copy = pltpu.make_async_copy(src, dst, sem.at[len(copies)])
        copy.start()
        copies.append(copy)

    for s in range(n):
        slab = rows(edge(at.high_out[s], ny, 8), 8)
        fetch(rhs.at[:, :, slab, :], yr.at[s])
        fetch(diag.at[:, slab, :], yd.at[s])
    for e, right in enumerate((at.even, at.odd)):
        fetch(rhs.at[:, pl.ds(edge(right, nx, 3), 3)], xr.at[e])
        fetch(diag.at[pl.ds(edge(right, nx, 2), 2)], xd.at[e])
    split = parity_matrix(False)
    for copy in copies[: 2 * n]:
        copy.wait()
    for s in range(n):
        v = permute_lanes(yr[s].reshape(2 * nx * 8, 2 * LANES), split, 2)
        d = permute_lanes(yd[s].reshape(nx * 8, 2 * LANES), split, 2)
        for h in range(2):
            tr[s, h] = v[:, HALF[h]]
            td[s, h] = d[:, HALF[h]]
        high = at.high_out[s]
        for h in range(2):
            for k in range(3):
                for probe in range(2):
                    i = (probe * 3 + k) * 2 + h
                    row = edge(high, 8, 3) + k + probe * nx * 8
                    m_ys[s][pl.ds(i * nx, nx), :] = tr[s, h, pl.ds(row, nx, stride=8), :]
            for k in range(2):
                row = edge(high, 8, 2) + k
                m_ys[s][pl.ds((12 + 2 * k + h) * nx, nx), :] = td[s, h, pl.ds(row, nx, stride=8), :]
            for msgs, right in ((m_cas, at.even), (m_cbs, at.odd)):
                for m, (p, q) in enumerate(CORNER1):
                    row = pick(high, 7 - q, q) + pick(right, nx - 1 - p, p) * 8
                    for probe in range(2):
                        msgs[s][pl.ds((m * 2 + probe) * 2 + h, 1), :] = tr[s, h, pl.ds(row + probe * nx * 8, 1), :]
                row = pick(high, 7, 0) + pick(right, nx - 1, 0) * 8
                msgs[s][pl.ds(12 + h, 1), :] = td[s, h, pl.ds(row, 1), :]
                msgs[s][pl.ds(14 + h, 1), :] = td[s, h, pl.ds(row, 1), :]
    for copy in copies[2 * n :]:
        copy.wait()
    for e, msg in enumerate((m_a, m_b)):
        v = permute_lanes(xr[e].reshape(6 * ny, 2 * LANES), split, 2)
        d = permute_lanes(xd[e].reshape(2 * ny, 2 * LANES), split, 2)
        for k in range(6):
            for h in range(2):
                msg[pl.ds((2 * k + h) * ny, ny), :] = v[k * ny : (k + 1) * ny, HALF[h]]
        for k in range(2):
            for h in range(2):
                msg[pl.ds((12 + 2 * k + h) * ny, ny), :] = d[k * ny : (k + 1) * ny, HALF[h]]


def open_kernel(sz, rhs, diag, bw, dw, cd, xs):
    nx, ny, wy, cy = sz.nx, sz.ny, sz.wy, sz.cy
    at = Place(sz)
    split = parity_matrix(False)
    zero8 = jnp.zeros((8, LANES), F32)
    zero_at = [pick(at.high_in[s], at.yoff + ny, at.yoff - 8) for s in range(sz.sides)]
    width = 4

    def body(i, _):
        for f in range(3):
            src = diag[pl.ds(width * i, width)] if f == 2 else rhs[f, pl.ds(width * i, width)]
            v = permute_lanes(src.reshape(width * ny, 2 * LANES), split, 2)
            if f == 2:
                v = v + 6.0
            for k in range(width):
                for h in range(2):
                    if f == 2:
                        ref, base = dw.at[h], (width * i + k + 2) * wy
                    else:
                        ref, base = bw.at[f, h], (width * i + k + 3) * wy
                    ref[rows(base + at.yoff, ny), :] = v[k * ny : (k + 1) * ny, HALF[h]]
                    for z in zero_at:
                        ref[rows(base + z, 8), :] = zero8
            if f == 2:
                for k in range(width // 2):
                    low, high = v[2 * k * ny : (2 * k + 1) * ny], v[(2 * k + 1) * ny : (2 * k + 2) * ny]
                    total = low + high
                    xs[k] = total[:, HALF[0]] + total[:, HALF[1]]
                    pair = xs[k, pl.ds(0, cy, stride=2), :] + xs[k, pl.ds(1, cy, stride=2), :]
                    cd[rows((i * (width // 2) + k) * cy, cy), :] = 0.5 * pair - 18.0
        return 0

    lax.fori_loop(0, nx // width, body, 0)


def pre_kernel(sz, *refs):
    n = sz.sides
    cd = refs[2]
    ys, xb, xa = sorted_messages(sz, ORDER1, refs[3 : 5 + n])
    cas, cbs = refs[5 + n : 5 + 2 * n], refs[5 + 2 * n : 5 + 3 * n]
    outs = refs[5 + 3 * n :]
    bw, dw, r_out, sol_out, coarse = outs[:5]
    m_ys, m_b, m_a = sorted_messages(sz, ORDER2, outs[5 : 7 + n])
    m_cas, m_cbs = outs[7 + n : 7 + 2 * n], outs[7 + 2 * n : 7 + 3 * n]
    r1, u2, u3, xs = outs[7 + 3 * n :]
    nx, ny, wy, cx, cy = sz.nx, sz.ny, sz.wy, sz.cx, sz.cy
    at = Place(sz)
    yoff = at.yoff
    masks = lane_masks(wy)

    zero8 = jnp.zeros((8, LANES), F32)
    zero_at = [pick(at.high_in[s], yoff + ny, yoff - 8) for s in range(n)]
    for msg, corners, to_right in ((xa, cas, at.even), (xb, cbs, at.odd)):
        b0 = jnp.where(to_right, nx + 3, 0)
        d0 = jnp.where(to_right, nx + 2, 0)
        for h in range(2):
            for k in range(3):
                for probe in range(2):
                    i = (probe * 3 + k) * 2 + h
                    bw[probe, h, rows((b0 + k) * wy + yoff, ny), :] = msg[pl.ds(i * ny, ny), :]
                    for z in zero_at:
                        bw[probe, h, rows((b0 + k) * wy + z, 8), :] = zero8
            for k in range(2):
                dw[h, rows((d0 + k) * wy + yoff, ny), :] = 6.0 + msg[pl.ds((12 + 2 * k + h) * ny, ny), :]
                for z in zero_at:
                    dw[h, rows((d0 + k) * wy + z, 8), :] = zero8
            for s in range(n):
                for m, (p, q) in enumerate(CORNER1):
                    row = pick(at.high_in[s], yoff + ny + q, yoff - 1 - q)
                    row = row + jnp.where(to_right, nx + 3 + p, 2 - p) * wy
                    for probe in range(2):
                        bw[probe, h, pl.ds(row, 1), :] = corners[s][pl.ds((m * 2 + probe) * 2 + h, 1), :]
                row = pick(at.high_in[s], yoff + ny, yoff - 1) + jnp.where(to_right, nx + 2, 1) * wy
                dw[h, pl.ds(row, 1), :] = 6.0 + corners[s][pl.ds(12 + h, 1), :]
    for s in range(n):
        br = pick(at.high_in[s], ny, -3) + yoff
        dr = pick(at.high_in[s], ny, -2) + yoff
        for h in range(2):
            for k in range(3):
                for probe in range(2):
                    i = (probe * 3 + k) * 2 + h
                    bw[probe, h, pl.ds(3 * wy + br + k, nx, stride=wy), :] = ys[s][pl.ds(i * nx, nx), :]
            for k in range(2):
                i = 12 + 2 * k + h
                dw[h, pl.ds(2 * wy + dr + k, nx, stride=wy), :] = 6.0 + ys[s][pl.ds(i * nx, nx), :]
    zero = jnp.zeros((wy, LANES), F32)
    for probe in range(2):
        for h in range(2):
            for i in (1, nx + 2):
                u2[probe, h, rows(i * wy, wy), :] = zero
                u3[probe, h, rows(i * wy, wy), :] = zero

    inside = row_mask(wy, at.fine)
    c0, (a1, c1), (a2, c2) = FINE[0][1], FINE[1], FINE[2]
    c1 = jnp.where(inside, c1, 0.0)
    c2 = jnp.where(inside, c2, 0.0)

    def step1(first, count):
        def use(probe, p, v, av):
            to = rows((p + 2) * wy, wy)
            for h in range(2):
                res = v[h] - c0 * av[h]
                r1[probe, h, to, :] = res
                u2[probe, h, to, :] = (a1 * c0) * v[h] + c1 * res

        sweep(bw, 3, dw, first, count, wy, masks, use)

    def step2(first, count):
        def use(probe, p, v, av):
            to = rows((p + 2) * wy, wy)
            for h in range(2):
                res = r1[probe, h, to, :] - av[h]
                r1[probe, h, to, :] = res
                u3[probe, h, to, :] = a2 * v[h] + c2 * res

        sweep(u2, 2, dw, first, count, wy, masks, use)

    mine = row_mask(wy, (yoff, yoff + ny))

    def steps3(i, _):
        totals = {}

        def use(probe, p, v, av):
            src = rows((p + 2) * wy, wy)
            to = rows(p * wy, wy)
            total = None
            for h in range(2):
                out = jnp.where(mine, r1[probe, h, src, :] - av[h], 0.0)
                r_out[probe, h, to, :] = out
                sol_out[probe, h, to, :] = (
                    c0 * bw[probe, h, rows((p + 3) * wy, wy), :] + u2[probe, h, src, :] + v[h]
                )
                total = out if total is None else total + out
            k = len(totals.setdefault(probe, []))
            totals[probe].append(total)
            if k % 2:
                xs[k // 2, probe] = totals[probe][k - 1] + total

        sweep(u3, 2, dw, 4 * i, 4, wy, masks, use)
        for k in range(2):
            for probe in range(2):
                pair = (
                    xs[k, probe, pl.ds(yoff, cy, stride=2), :] + xs[k, probe, pl.ds(yoff + 1, cy, stride=2), :]
                )
                coarse[probe, rows((2 * i + k) * cy, cy), :] = 0.5 * pair
        return 0

    @pl.when(at.has_l)
    def _():
        step1(-2, 2)

    @pl.when(at.has_r)
    def _():
        step1(nx, 2)

    looped(step1, nx)

    @pl.when(at.has_l)
    def _():
        step2(-1, 1)

    @pl.when(at.has_r)
    def _():
        step2(nx, 1)

    looped(step2, nx)
    lax.fori_loop(0, nx // 4, steps3, 0)

    field = [coarse.at[0], coarse.at[1], cd]
    depth = [REACH, REACH, REACH - 1]
    for msg, corners, right in ((m_a, m_cas, at.even), (m_b, m_cbs, at.odd)):
        for f in range(3):
            size = (depth[f] - 1) * cy
            first = pick(right, cx - depth[f], 1)
            msg[pl.ds(f * (REACH - 1) * cy, size), :] = field[f][rows(first * cy, size), :]
        for s in range(n):
            for m, (f, p, q) in enumerate(CORNER2):
                row = pick(at.high_out[s], cy - 1 - q, q) + pick(right, cx - 1 - p, p) * cy
                corners[s][pl.ds(m, 1), :] = field[f][pl.ds(row, 1), :]
            row = pick(at.high_out[s], yoff + ny - 1, yoff) + pick(right, nx - 1, 0) * wy
            for probe in range(2):
                for h in range(2):
                    i = len(CORNER2) + probe * 2 + h
                    corners[s][pl.ds(i, 1), :] = r_out[probe, h, pl.ds(row, 1), :]
            corners[s][pl.ds(sz.c2 - 3, 3), :] = jnp.zeros((3, LANES), F32)
        for probe in range(2):
            for h in range(2):
                for k in range(2):
                    i = (probe * 2 + h) * 2 + k
                    row = (edge(right, nx, 2) + k) * wy + yoff
                    msg[pl.ds(sz.x2_base + i * ny, ny), :] = r_out[probe, h, rows(row, ny), :]
    for s in range(n):
        for f in range(3):
            for k in range(depth[f] - 1):
                row = pick(at.high_out[s], cy - depth[f], 1) + k
                m_ys[s][pl.ds((f * (REACH - 1) + k) * cx, cx), :] = field[f][pl.ds(row, cx, stride=cy), :]
        row = edge(at.high_out[s], ny, 2) + yoff
        for probe in range(2):
            for h in range(2):
                for k in range(2):
                    i = (probe * 2 + h) * 2 + k
                    m_ys[s][pl.ds(sz.y2_base + i * nx, nx), :] = r_out[probe, h, pl.ds(row + k, nx, stride=wy), :]


def post_kernel(sz, *refs):
    n = sz.sides
    agg, r_in, sol_in, dw, coarse, cd = refs[:6]
    ys, x_b, x_a = sorted_messages(sz, ORDER2, refs[6 : 8 + n])
    cas, cbs = refs[8 + n : 8 + 2 * n], refs[8 + 2 * n : 8 + 3 * n]
    out = refs[8 + 3 * n]
    cw, cu, cc, pt, st_g, st_u, rh, re, r1, u2, acc, pj, ow, sem = refs[9 + 3 * n :]
    nx, ny, wy, cx, cy, wc = sz.nx, sz.ny, sz.wy, sz.cx, sz.cy, sz.wc
    at = Place(sz)
    yoff = at.yoff
    masks = lane_masks(wy)
    planes = cx + 2 * REACH

    zero8 = jnp.zeros((8, LANES), F32)
    zero_at = [pick(at.high_in[s], yoff + cy, yoff - 8) for s in range(n)]
    field = [coarse.at[0], coarse.at[1], cd]
    depth = [REACH, REACH, REACH - 1]
    for f in range(3):
        for p in range(planes):
            for z in zero_at:
                cw[f, rows(p * wc + z, 8), :] = zero8
        for x in range(cx):
            cw[f, rows((x + REACH) * wc + yoff, cy), :] = field[f][rows(x * cy, cy), :]
        for s in range(n):
            for k in range(depth[f] - 1):
                row = pick(at.high_in[s], yoff + cy + 1, yoff - depth[f]) + k
                cw[f, pl.ds(REACH * wc + row, cx, stride=wc), :] = ys[s][rows((f * (REACH - 1) + k) * cx, cx), :]
            total = None
            for h in range(2):
                for k in range(2):
                    if f == 2:
                        row = pick(at.high_in[s], yoff + ny, yoff - 2) + k
                        part = dw[h, pl.ds(2 * wy + row, nx, stride=wy), :]
                    else:
                        part = ys[s][pl.ds(sz.y2_base + ((f * 2 + h) * 2 + k) * nx, nx), :]
                    total = part if total is None else total + part
            slot = 6 + s * 3 + f
            pt[slot, pl.ds(0, nx), :] = total
            pair = pt[slot, pl.ds(0, cx, stride=2), :] + pt[slot, pl.ds(1, cx, stride=2), :]
            row = pick(at.high_in[s], yoff + cy, yoff - 1)
            cw[f, pl.ds(REACH * wc + row, cx, stride=wc), :] = 0.5 * pair - (18.0 if f == 2 else 0.0)
        for side, (msg, to_right) in enumerate(((x_a, at.even), (x_b, at.odd))):
            first = jnp.where(to_right, REACH + cx + 1, REACH - depth[f])
            for k in range(depth[f] - 1):
                cw[f, rows((first + k) * wc + yoff, cy), :] = msg[rows((f * (REACH - 1) + k) * cy, cy), :]
            total = None
            for h in range(2):
                for k in range(2):
                    if f == 2:
                        plane = jnp.where(to_right, nx + 2, 0) + k
                        part = dw[h, rows(plane * wy + yoff, ny), :]
                    else:
                        part = msg[pl.ds(sz.x2_base + ((f * 2 + h) * 2 + k) * ny, ny), :]
                    total = part if total is None else total + part
            slot = side * 3 + f
            pt[slot, pl.ds(0, ny), :] = total
            pair = pt[slot, pl.ds(0, cy, stride=2), :] + pt[slot, pl.ds(1, cy, stride=2), :]
            plane = jnp.where(to_right, REACH + cx, REACH - 1)
            cw[f, rows(plane * wc + yoff, cy), :] = 0.5 * pair - (18.0 if f == 2 else 0.0)
    for corners, to_right in ((cas, at.even), (cbs, at.odd)):
        for s in range(n):
            for m, (f, p, q) in enumerate(CORNER2):
                row = pick(at.high_in[s], yoff + cy + q, yoff - 1 - q)
                row = row + jnp.where(to_right, REACH + cx + p, REACH - 1 - p) * wc
                cw[f, pl.ds(row, 1), :] = corners[s][pl.ds(m, 1), :]

    cmasks = lane_masks(wc)
    inside = row_mask(wc, at.crs)
    i = at.i
    here = agg[i]
    link_l = (at.has_l & (agg[jnp.maximum(i - 1, 0)] == here)).astype(F32)
    link_r = (at.has_r & (agg[jnp.minimum(i + 1, sz.n_gx - 1)] == here)).astype(F32)
    for p in range(planes):
        to = pl.ds(p * wc, wc)
        for probe in range(2):
            u = jnp.where(inside, COARSE[0][1], 0.0) * cw[probe, to, :]
            cu[0, probe, to, :] = u
            cc[probe, to, :] = u
    for k in range(COARSE_DEG - 1):
        a, c = COARSE[k + 1]
        c = jnp.where(inside, c, 0.0)
        old, new = k % 2, 1 - k % 2
        for p in range(1 + k, planes - 1 - k):
            to = pl.ds(p * wc, wc)
            for probe in range(2):
                u = cu[old, probe, to, :]
                before = cu[old, probe, pl.ds((p - 1) * wc, wc), :]
                after = cu[old, probe, pl.ds((p + 1) * wc, wc), :]
                if p == REACH:
                    before = before * link_l
                if p == REACH - 1:
                    after = after * link_l
                if p == REACH + cx:
                    before = before * link_r
                if p == REACH + cx - 1:
                    after = after * link_r
                row = p * wc
                beside = cu[old, probe, pl.ds(row - 1, wc), :] + cu[old, probe, pl.ds(row + 1, wc), :]
                near = ((before + after) + beside) + (below(u, cmasks) + above(u, cmasks))
                res = cw[probe, to, :] - (cw[2, to, :] * u - near)
                u = a * u + c * res
                if k + 2 < COARSE_DEG:
                    cw[probe, to, :] = res
                    cu[new, probe, to, :] = u
                cc[probe, to, :] = cc[probe, to, :] + u

    for msg, corners, to_right in ((x_a, cas, at.even), (x_b, cbs, at.odd)):
        for probe in range(2):
            for h in range(2):
                for k in range(2):
                    i = (probe * 2 + h) * 2 + k
                    base = (jnp.where(to_right, 2, 0) + k) * wy
                    rh[probe, h, rows(base + yoff, ny), :] = msg[pl.ds(sz.x2_base + i * ny, ny), :]
                    for s in range(n):
                        zero_row = pick(at.high_in[s], yoff + ny, yoff - 8)
                        rh[probe, h, rows(base + zero_row, 8), :] = zero8
                for s in range(n):
                    row = pick(at.high_in[s], yoff + ny, yoff - 1) + jnp.where(to_right, 2, 1) * wy
                    i = len(CORNER2) + probe * 2 + h
                    rh[probe, h, pl.ds(row, 1), :] = corners[s][pl.ds(i, 1), :]

    c0, (a1, c1), (a2, c2) = FINE[0][1], FINE[1], FINE[2]
    valid = row_mask(wy, at.valid)

    def spread(q, r_ref, r_plane, own, slot=0):
        for probe in range(2):
            u = cc[probe, rows((q + REACH) * wc, wc), :]
            sides = [cc[probe, rows((q + REACH - 1 + 2 * k) * wc, wc), :] for k in range(2)]
            u3 = 3.0 * u
            shifted = [pltpu.roll(u, 1, 0), pltpu.roll(u, wc - 1, 0)]
            for row in range(2):
                st_u[slot, probe, pl.ds(row, wc, stride=2), :] = u
            for h in range(2):
                g = u3 + (above(u, cmasks) if h else below(u, cmasks))
                for k in range(2):
                    for row in range(2):
                        st_g[slot, probe, h, k, pl.ds(row, wc, stride=2), :] = (g + sides[k]) + shifted[row]
        for k in range(2):
            to = rows((2 * q + k + 2) * wy, wy)
            for h in range(2):
                d = dw[h, to, :]
                for probe in range(2):
                    u = st_u[slot, probe, rows(yoff, wy), :]
                    old = r_ref[probe, h, rows((r_plane + k) * wy, wy), :]
                    res = (old - d * u) + st_g[slot, probe, h, k, rows(yoff, wy), :]
                    res = jnp.where(valid, res, 0.0)
                    re[probe, h, to, :] = res
                    if own:
                        mine = rows((2 * q + k) * wy, wy)
                        acc[probe, h, mine, :] = (sol_in[probe, h, mine, :] + u) + c0 * res

    def own_planes(i, _):
        for k in range(4):
            spread(4 * i + k, r_in, 2 * (4 * i + k), True, k)
        return 0

    lax.fori_loop(0, cx // 4, own_planes, 0)
    zero = jnp.zeros((wy, LANES), F32)
    for has, q, first in ((at.has_l, -1, 0), (at.has_r, cx, 2)):

        @pl.when(has)
        def _():
            spread(q, rh, first, False)

        @pl.when(jnp.logical_not(has))
        def _():
            for probe in range(2):
                for h in range(2):
                    for k in range(2):
                        re[probe, h, rows((2 * q + 2 + k) * wy, wy), :] = zero
                        u2[probe, h, rows((2 * q + 2 + k) * wy, wy), :] = zero

    for s in range(n):
        row = pick(at.high_in[s], yoff + ny, yoff - 2)
        for probe in range(2):
            for h in range(2):
                for k in range(2):
                    i = (probe * 2 + h) * 2 + k
                    to = pl.ds(2 * wy + row + k, nx, stride=wy)
                    re[probe, h, to, :] = re[probe, h, to, :] + ys[s][pl.ds(sz.y2_base + i * nx, nx), :]

    c1 = jnp.where(row_mask(wy, at.fine), c1, 0.0)

    def step1(first, count):
        def use(probe, p, v, av):
            to = rows((p + 2) * wy, wy)
            for h in range(2):
                res = v[h] - c0 * av[h]
                r1[probe, h, to, :] = res
                u2[probe, h, to, :] = (a1 * c0) * v[h] + c1 * res

        sweep(re, 2, dw, first, count, wy, masks, use)

    join = parity_matrix(True)
    width = 4

    def close(i):
        slot = i % 2
        planes = [(probe, k) for probe in range(2) for k in range(width)]
        own = [
            jnp.concatenate([pj[slot, probe, h, rows(k * wy + yoff, ny), :] for h in range(2)], axis=1)
            for probe, k in planes
        ]
        joined = permute_lanes(jnp.concatenate(own, axis=0), join, 2)
        for m, (probe, k) in enumerate(planes):
            ow[probe, width * i + k] = joined[m * ny : (m + 1) * ny]

    def send(i):
        part = pl.ds(width * i, width)
        return pltpu.make_async_copy(ow.at[:, part], out.at[:, part], sem.at[i])

    def step2(i):
        slot = i % 2

        def use(probe, p, v, av):
            to = rows((p + 2) * wy, wy)
            for h in range(2):
                res = r1[probe, h, to, :] - av[h]
                pj[slot, probe, h, rows((p - width * i) * wy, wy), :] = acc[probe, h, rows(p * wy, wy), :] + (
                    (1.0 + a2) * v[h] + c2 * res
                )

        sweep(u2, 2, dw, width * i, width, wy, masks, use)

    def steps2(i, _):
        close(i - 1)
        step2(i)
        send(i - 1).start()
        return 0

    @pl.when(at.has_l)
    def _():
        step1(-1, 1)

    @pl.when(at.has_r)
    def _():
        step1(nx, 1)

    looped(step1, nx)
    step2(0)
    lax.fori_loop(1, nx // width, steps2, 0)
    close(nx // width - 1)
    send(nx // width - 1).start()
    for i in range(nx // width):
        send(i).wait()


def on_device(n_gx, n_gy, right_side, diagonal, aggregates):
    nx, ny, nz = right_side.shape[1:]
    sz = Sizes(nx, ny, nz, n_gx, n_gy)
    n, wy, wc, cx = sz.sides, sz.wy, sz.wc, sz.cx

    pairs_a = [(k, k ^ 1) for k in range(n_gx)]
    pairs_b = [(k, k + 1) for k in range(1, n_gx - 1, 2)] + [(k + 1, k) for k in range(1, n_gx - 1, 2)]
    along = [[(0, 1), (1, 0)]] if sz.two else [
        [(k, k - 1) for k in range(1, n_gy)],
        [(k, k + 1) for k in range(n_gy - 1)],
    ]

    def both(pairs, perm):
        return [(a * n_gy + c, b * n_gy + d) for a, b in pairs for c, d in perm]

    perms = {"a": [("gx", pairs_a)], "b": [("gx", pairs_b)], "y": [("gy", perm) for perm in along]}
    corner_perms = [(("gx", "gy"), both(pairs, perm)) for pairs in (pairs_a, pairs_b) for perm in along]

    def exchange(order, messages):
        lines = [line for name in order for line in perms[name]] + corner_perms
        return [lax.ppermute(m, *line) for m, line in zip(messages, lines)]

    smem = pl.BlockSpec(memory_space=pltpu.SMEM)
    vmem = pl.BlockSpec(memory_space=pltpu.VMEM)
    hbm = pl.BlockSpec(memory_space=pltpu.HBM)
    params = pltpu.CompilerParams(vmem_limit_bytes=24 << 20)

    def shape(*dims):
        return jax.ShapeDtypeStruct(dims, F32)

    def messages(order, x, y, c):
        sizes = [y if name == "y" else x for name in order for _ in perms[name]]
        return [shape(size, LANES) for size in sizes + [c] * (2 * n)]

    packed = pl.pallas_call(
        functools.partial(pack_kernel, sz),
        in_specs=[hbm] * 2,
        out_specs=[vmem] * (2 + 3 * n),
        out_shape=messages(ORDER1, sz.x1, sz.y1, sz.c1),
        scratch_shapes=[
            pltpu.VMEM((2, 2, 3, ny, nz), F32),
            pltpu.VMEM((2, 2, ny, nz), F32),
            pltpu.VMEM((n, 2, nx, 8, nz), F32),
            pltpu.VMEM((n, nx, 8, nz), F32),
            pltpu.VMEM((n, 2, 2 * nx * 8, LANES), F32),
            pltpu.VMEM((n, 2, nx * 8, LANES), F32),
            pltpu.SemaphoreType.DMA((2 * n + 4,)),
        ],
        compiler_params=pltpu.CompilerParams(vmem_limit_bytes=105 << 19),
        name="pack_kernel",
    )(right_side, diagonal)
    halos = exchange(ORDER1, packed)
    bw, dw, cd = pl.pallas_call(
        functools.partial(open_kernel, sz),
        in_specs=[vmem] * 2,
        out_specs=[vmem] * 3,
        out_shape=[shape(*sz.bw), shape(*sz.dw), shape(sz.coarse, LANES)],
        scratch_shapes=[
            pltpu.VMEM((2, ny, LANES), F32),
        ],
        compiler_params=params,
        name="open_kernel",
    )(right_side, diagonal)
    results = pl.pallas_call(
        functools.partial(pre_kernel, sz),
        in_specs=[vmem] * (5 + 3 * n),
        out_specs=[vmem] * (7 + 3 * n),
        out_shape=[shape(*sz.bw), shape(*sz.dw), shape(*sz.brick), shape(*sz.brick), shape(2, sz.coarse, LANES)]
        + messages(ORDER2, sz.x2, sz.y2, sz.c2),
        scratch_shapes=[pltpu.VMEM((2, 2, (nx + 4) * wy, LANES), F32)] * 3 + [pltpu.VMEM((2, 2, wy, LANES), F32)],
        input_output_aliases={0: 0, 1: 1},
        compiler_params=params,
        name="pre_smooth",
    )(bw, dw, cd, *halos)
    dw, r_own, sol, coarse = results[1:5]
    halos = exchange(ORDER2, results[5:])
    planes = cx + 2 * REACH
    return pl.pallas_call(
        functools.partial(post_kernel, sz),
        in_specs=[smem] + [vmem] * (7 + 3 * n),
        out_specs=hbm,
        out_shape=shape(2, nx, ny, nz),
        scratch_shapes=[
            pltpu.VMEM((3, planes * wc, LANES), F32),
            pltpu.VMEM((2, 2, planes * wc, LANES), F32),
            pltpu.VMEM((2, planes * wc, LANES), F32),
            pltpu.VMEM((6 + 3 * n, max(nx, ny), LANES), F32),
            pltpu.VMEM((4, 2, 2, 2, 2 * wc, LANES), F32),
            pltpu.VMEM((4, 2, 2 * wc, LANES), F32),
            pltpu.VMEM((2, 2, 4 * wy, LANES), F32),
        ]
        + [pltpu.VMEM((2, 2, (nx + 4) * wy, LANES), F32)] * 3
        + [
            pltpu.VMEM(sz.brick, F32),
            pltpu.VMEM((2, 2, 2, 4 * wy, LANES), F32),
            pltpu.VMEM((2, nx, ny, nz), F32),
            pltpu.SemaphoreType.DMA((nx // 4,)),
        ],
        compiler_params=params,
        name="correct_and_smooth",
    )(aggregates, r_own, sol, dw, coarse, cd, *halos)


def solution(mesh):
    return jax.shard_map(
        functools.partial(on_device, mesh.shape["gx"], mesh.shape["gy"]),
        mesh=mesh,
        in_specs=(P(None, "gx", "gy", None), P("gx", "gy", None), P()),
        out_specs=P(None, "gx", "gy", None),
        check_vma=False,
    )
```
